32 devices in a mesh: dp: 8 (over z, y), mp: 4 (over x, core).
Axes of the slice: x: 2, y: 2, z: 4, core: 2. Of those that a mesh axis runs over, the one named last changes fastest.
Arguments:
- latents: float32 [10240, 1024], P(('dp', 'mp')), may hold values from -6 to 6
- cotangent: float32 [10240, 1024], P(('dp', 'mp')), may hold values from -6 to 6
- text_embed: bfloat16 [4, 77, 1024], replicated, may hold values from -6 to 6
- text_mask: int32 [4, 77], replicated, may hold values 0 or 1
- band_ids: int32 [4], replicated, may hold values from 0 to 3, as said below
- rel_index_s: int32 [256, 256], replicated, may hold values from 0 to 1023
- rel_index_t: int32 [320, 320], replicated, may hold values from 0 to 2047
- modulation: float32 [4, 18, 1024], replicated, may hold values from -3 to 3
- qkv_master: float32 [2, 1024, 3072], P(None, 'dp', 'mp'), may hold values from -0.1875 to 0.1875
- out_master: float32 [2, 1024, 1024], P(None, 'mp', 'dp'), may hold values from -0.75 to 0.75
- cq_master: float32 [2, 1024, 1024], P(None, 'dp', 'mp'), may hold values from -0.1875 to 0.1875
- ckv_master: float32 [2, 1024, 2048], P(None, 'dp', 'mp'), may hold values from -0.1875 to 0.1875
- cout_master: float32 [2, 1024, 1024], P(None, 'mp', 'dp'), may hold values from -0.5 to 0.5
- up_master: float32 [2, 1024, 4096], P(None, 'dp', 'mp'), may hold values from -0.1875 to 0.1875
- down_master: float32 [2, 4096, 1024], P(None, 'mp', 'dp'), may hold values from -0.09375 to 0.09375
- rel_s_master: float32 [16, 1024], P('mp', 'dp'), may hold values from -4 to 4
- rel_t_master: float32 [16, 2048], P('mp', 'dp'), may hold values from -4 to 4
- qkv_first: float32 [2, 1024, 3072], P(None, 'dp', 'mp'), may hold values from -32 to 32
- out_first: float32 [2, 1024, 1024], P(None, 'mp', 'dp'), may hold values from -16 to 16
- cq_first: float32 [2, 1024, 1024], P(None, 'dp', 'mp'), may hold values from -96 to 96
- ckv_first: float32 [2, 1024, 2048], P(None, 'dp', 'mp'), may hold values from -80 to 80
- cout_first: float32 [2, 1024, 1024], P(None, 'mp', 'dp'), may hold values from -24 to 24
- up_first: float32 [2, 1024, 4096], P(None, 'dp', 'mp'), may hold values from -20 to 20
- down_first: float32 [2, 4096, 1024], P(None, 'mp', 'dp'), may hold values from -40 to 40
- rel_s_first: float32 [16, 1024], P('mp', 'dp'), may hold values from -12 to 12
- rel_t_first: float32 [16, 2048], P('mp', 'dp'), may hold values from -4 to 4
- qkv_second: float32 [2, 1024, 3072], P(None, 'dp', 'mp'), may hold values from 153.6 to 616
- out_second: float32 [2, 1024, 1024], P(None, 'mp', 'dp'), may hold values from 38.4 to 153.6
- cq_second: float32 [2, 1024, 1024], P(None, 'dp', 'mp'), may hold values from 1140.48 to 4567.2
- ckv_second: float32 [2, 1024, 2048], P(None, 'dp', 'mp'), may hold values from 792 to 3168
- cout_second: float32 [2, 1024, 1024], P(None, 'mp', 'dp'), may hold values from 71.28 to 285.12
- up_second: float32 [2, 1024, 4096], P(None, 'dp', 'mp'), may hold values from 55.296 to 221.184
- down_second: float32 [2, 4096, 1024], P(None, 'mp', 'dp'), may hold values from 221.184 to 884.736
- rel_s_second: float32 [16, 1024], P('mp', 'dp'), may hold values from 17.28 to 69.2
- rel_t_second: float32 [16, 2048], P('mp', 'dp'), may hold values from 8.64 to 34.6
Outputs:
- outputs: float32 [10240, 1024], P(('dp', 'mp'))
- grad_latents: float32 [10240, 1024], P(('dp', 'mp'))
- grad_modulation: float32 [4, 18, 1024], replicated
- qkv_new: float32 [2, 1024, 3072], P(None, 'dp', 'mp')
- qkv_first_new: float32 [2, 1024, 3072], P(None, 'dp', 'mp')
- qkv_second_new: float32 [2, 1024, 3072], P(None, 'dp', 'mp')
- qkv_low: bfloat16 [2, 1024, 3072], P(None, 'dp', 'mp')
- out_new: float32 [2, 1024, 1024], P(None, 'mp', 'dp')
- out_first_new: float32 [2, 1024, 1024], P(None, 'mp', 'dp')
- out_second_new: float32 [2, 1024, 1024], P(None, 'mp', 'dp')
- out_low: bfloat16 [2, 1024, 1024], P(None, 'mp', 'dp')
- cq_new: float32 [2, 1024, 1024], P(None, 'dp', 'mp')
- cq_first_new: float32 [2, 1024, 1024], P(None, 'dp', 'mp')
- cq_second_new: float32 [2, 1024, 1024], P(None, 'dp', 'mp')
- cq_low: bfloat16 [2, 1024, 1024], P(None, 'dp', 'mp')
- ckv_new: float32 [2, 1024, 2048], P(None, 'dp', 'mp')
- ckv_first_new: float32 [2, 1024, 2048], P(None, 'dp', 'mp')
- ckv_second_new: float32 [2, 1024, 2048], P(None, 'dp', 'mp')
- ckv_low: bfloat16 [2, 1024, 2048], P(None, 'dp', 'mp')
- cout_new: float32 [2, 1024, 1024], P(None, 'mp', 'dp')
- cout_first_new: float32 [2, 1024, 1024], P(None, 'mp', 'dp')
- cout_second_new: float32 [2, 1024, 1024], P(None, 'mp', 'dp')
- cout_low: bfloat16 [2, 1024, 1024], P(None, 'mp', 'dp')
- up_new: float32 [2, 1024, 4096], P(None, 'dp', 'mp')
- up_first_new: float32 [2, 1024, 4096], P(None, 'dp', 'mp')
- up_second_new: float32 [2, 1024, 4096], P(None, 'dp', 'mp')
- up_low: bfloat16 [2, 1024, 4096], P(None, 'dp', 'mp')
- down_new: float32 [2, 4096, 1024], P(None, 'mp', 'dp')
- down_first_new: float32 [2, 4096, 1024], P(None, 'mp', 'dp')
- down_second_new: float32 [2, 4096, 1024], P(None, 'mp', 'dp')
- down_low: bfloat16 [2, 4096, 1024], P(None, 'mp', 'dp')
- rel_s_new: float32 [16, 1024], P('mp', 'dp')
- rel_s_first_new: float32 [16, 1024], P('mp', 'dp')
- rel_s_second_new: float32 [16, 1024], P('mp', 'dp')
- rel_s_low: bfloat16 [16, 1024], P('mp', 'dp')
- rel_t_new: float32 [16, 2048], P('mp', 'dp')
- rel_t_first_new: float32 [16, 2048], P('mp', 'dp')
- rel_t_second_new: float32 [16, 2048], P('mp', 'dp')
- rel_t_low: bfloat16 [16, 2048], P('mp', 'dp')
The draws below stay inside these ranges and needn't reach their ends.
Inputs may be any that keep to these rules, and one draw needn't show every extreme that they name: `band_ids`: the first and the last clip share one band; clip 1 lies in another band.
All inputs are finite; a program needn't handle non-finite values.
Results may differ from the reference program's by a relative error of at most 0.028.
Values may be sent and summed in bfloat16 or wider, within the bound.
No kernel may reach another device: no remote copies, remote signals or barrier semaphores. Data moves between devices by JAX's collectives and lax.ppermute only.
A program may use at most 320 MiB of HBM per device.

```python
import math
import jax
import jax.numpy as jnp
from jax import lax

D = 1024
H = 16
HD = 64
FF = 4096
TXT = 77
FRAMES = 5
SIDE = 16
LAYERS = 2
REL_S = 1024
REL_T = 2048
BANDS = 4
STEP = 10
BLOCK = 1280
WIN_S = 256
WIN_T = 320
CLIPS = 4
TOKENS = 10240


def draw_band_ids(key, part):
    shared = jax.random.randint(jax.random.fold_in(key, 11), (), 0, BANDS)
    others = jax.random.randint(jax.random.fold_in(key, 12), (CLIPS,), 0, BANDS)
    offset = jax.random.randint(jax.random.fold_in(key, 13), (), 1, BANDS)
    second = (shared + offset) % BANDS
    position = jnp.arange(CLIPS, dtype=jnp.int32)
    ends = (position == 0) | (position == CLIPS - 1)
    result = jnp.where(ends, shared, others)
    result = jnp.where(position == 1, second, result)
    return result.astype(jnp.int32)


def plant(values, key, smallest, high):
    place = [jax.random.randint(jax.random.fold_in(key, axis), (), 0, length) for axis, length in enumerate(values.shape)]
    main_axis = values.shape.index(max(values.shape))
    beside = place[:main_axis] + [(place[main_axis] + 1) % values.shape[main_axis]] + place[main_axis + 1:]
    return values.at[tuple(place)].set(smallest).at[tuple(beside)].set(high)


def block_scale(stream_key, dims, cuts, low, largest):
    loudness = 1.0
    for dim, shards_of in cuts:
        steps = jax.random.uniform(jax.random.fold_in(jax.random.fold_in(stream_key, 6), dim), (shards_of,), jnp.float32, low / len(cuts), largest / len(cuts))
        loudness = loudness * jnp.repeat(jnp.exp(steps), dims[dim] // shards_of).reshape((-1,) + (1,) * (len(dims) - 1 - dim))
    return loudness


def gaussian(key, shape, deviation, limit, pieces=(), held_as=jnp.bfloat16):
    gain = block_scale(key, shape, pieces, -0.22, 0.18) if pieces else 1.0
    drawn = jax.random.normal(key, shape, jnp.float32) * deviation * gain
    return jnp.minimum(jnp.maximum(drawn, -limit), limit).astype(held_as)


def setup_inputs(seed: int = 0) -> dict:
    key_of = jax.random.split(jax.random.key(seed), 36)
    latents = gaussian(key_of[0], (TOKENS, D), 1.0, 6.0, ((0, 32),), jnp.float32)
    cotangent = gaussian(key_of[1], (TOKENS, D), 1.0, 6.0, ((0, 32),), jnp.float32)
    text_embed = gaussian(key_of[2], (CLIPS, TXT, D), 1.0, 6.0)
    text_mask = plant((jax.random.randint(key_of[3], (CLIPS, TXT), 0, 2) < 1).astype(jnp.int32), jax.random.fold_in(key_of[3], 1), 0, 1)
    band_ids = draw_band_ids(jax.random.fold_in(key_of[35], 71), 0)
    rel_index_s = plant(jax.random.randint(key_of[5], (WIN_S, WIN_S), 0, REL_S), jax.random.fold_in(key_of[5], 1), 0, REL_S - 1).astype(jnp.int32)
    rel_index_t = plant(jax.random.randint(key_of[6], (WIN_T, WIN_T), 0, REL_T), jax.random.fold_in(key_of[6], 1), 0, REL_T - 1).astype(jnp.int32)
    modulation = gaussian(key_of[7], (BANDS, 9 * LAYERS, D), 0.5, 3.0, (), jnp.float32)
    qkv_master = gaussian(key_of[8], (LAYERS, D, 3 * D), D ** -0.5, 0.1875, ((1, 8), (2, 4)), jnp.float32)
    out_master = gaussian(key_of[9], (LAYERS, D, D), (D // 16) ** -0.5, 0.75, ((1, 4), (2, 8)), jnp.float32)
    cq_master = gaussian(key_of[10], (LAYERS, D, D), D ** -0.5, 0.1875, ((1, 8), (2, 4)), jnp.float32)
    ckv_master = gaussian(key_of[11], (LAYERS, D, 2 * D), D ** -0.5, 0.1875, ((1, 8), (2, 4)), jnp.float32)
    cout_master = gaussian(key_of[12], (LAYERS, D, D), (D // 8) ** -0.5, 0.5, ((1, 4), (2, 8)), jnp.float32)
    up_master = gaussian(key_of[13], (LAYERS, D, FF), D ** -0.5, 0.1875, ((1, 8), (2, 4)), jnp.float32)
    down_master = gaussian(key_of[14], (LAYERS, FF, D), FF ** -0.5, 0.09375, ((1, 4), (2, 8)), jnp.float32)
    rel_s_master = gaussian(key_of[15], (H, REL_S), 1.0, 4.0, ((0, 4), (1, 8)), jnp.float32)
    rel_t_master = gaussian(key_of[16], (H, REL_T), 1.0, 4.0, ((0, 4), (1, 8)), jnp.float32)
    qkv_first = gaussian(key_of[17], (LAYERS, D, 3 * D), (0.88 * (TOKENS // WIN_S) ** 0.5), 32.0, ((1, 8), (2, 4)), jnp.float32)
    out_first = gaussian(key_of[18], (LAYERS, D, D), (0.44 * (TOKENS // WIN_S) ** 0.5), 16.0, ((1, 4), (2, 8)), jnp.float32)
    cq_first = gaussian(key_of[19], (LAYERS, D, D), (1.32 * (TOKENS // TXT) ** 0.5), 96.0, ((1, 8), (2, 4)), jnp.float32)
    ckv_first = gaussian(key_of[20], (LAYERS, D, 2 * D), (1.1 * (TOKENS // TXT) ** 0.5), 80.0, ((1, 8), (2, 4)), jnp.float32)
    cout_first = gaussian(key_of[21], (LAYERS, D, D), (0.33 * (TOKENS // TXT) ** 0.5), 24.0, ((1, 4), (2, 8)), jnp.float32)
    up_first = gaussian(key_of[22], (LAYERS, D, FF), (0.066 * (TOKENS * D // FF) ** 0.5), 20.0, ((1, 8), (2, 4)), jnp.float32)
    down_first = gaussian(key_of[23], (LAYERS, FF, D), (0.066 * TOKENS ** 0.5), 40.0, ((1, 4), (2, 8)), jnp.float32)
    rel_s_first = gaussian(key_of[24], (H, REL_S), (1.32 * (HD * TOKENS // (WIN_S * REL_S)) ** 0.5), 12.0, ((0, 4), (1, 8)), jnp.float32)
    rel_t_first = gaussian(key_of[25], (H, REL_T), (1.32 * (HD * TOKENS // (WIN_T * REL_T)) ** 0.5), 4.0, ((0, 4), (1, 8)), jnp.float32)
    qkv_second = jnp.clip(jnp.exp(math.log(616.0) - 1.3888951 * jax.random.uniform(key_of[26], (LAYERS, D, 3 * D), jnp.float32) ** block_scale(key_of[26], (LAYERS, D, 3 * D), ((1, 8), (2, 4)), -0.2, 0.2)), 153.6, 616.0)
    out_second = jnp.clip(jnp.exp(math.log(153.6) - 1.3862944 * jax.random.uniform(key_of[27], (LAYERS, D, D), jnp.float32) ** block_scale(key_of[27], (LAYERS, D, D), ((1, 4), (2, 8)), -0.2, 0.2)), 38.4, 153.6)
    cq_second = jnp.clip(jnp.exp(math.log(4567.2) - 1.3874512 * jax.random.uniform(key_of[28], (LAYERS, D, D), jnp.float32) ** block_scale(key_of[28], (LAYERS, D, D), ((1, 8), (2, 4)), -0.2, 0.2)), 1140.48, 4567.2)
    ckv_second = jnp.clip(jnp.exp(math.log(3168.0) - 1.3862944 * jax.random.uniform(key_of[29], (LAYERS, D, 2 * D), jnp.float32) ** block_scale(key_of[29], (LAYERS, D, 2 * D), ((1, 8), (2, 4)), -0.2, 0.2)), 792.0, 3168.0)
    cout_second = jnp.clip(jnp.exp(math.log(285.12) - 1.3862944 * jax.random.uniform(key_of[30], (LAYERS, D, D), jnp.float32) ** block_scale(key_of[30], (LAYERS, D, D), ((1, 4), (2, 8)), -0.2, 0.2)), 71.28, 285.12)
    up_second = jnp.clip(jnp.exp(math.log(221.184) - 1.3862944 * jax.random.uniform(key_of[31], (LAYERS, D, FF), jnp.float32) ** block_scale(key_of[31], (LAYERS, D, FF), ((1, 8), (2, 4)), -0.2, 0.2)), 55.296, 221.184)
    down_second = jnp.clip(jnp.exp(math.log(884.736) - 1.3862944 * jax.random.uniform(key_of[32], (LAYERS, FF, D), jnp.float32) ** block_scale(key_of[32], (LAYERS, FF, D), ((1, 4), (2, 8)), -0.2, 0.2)), 221.184, 884.736)
    rel_s_second = jnp.clip(jnp.exp(math.log(69.2) - 1.387451 * jax.random.uniform(key_of[33], (H, REL_S), jnp.float32) ** block_scale(key_of[33], (H, REL_S), ((0, 4), (1, 8)), -0.2, 0.2)), 17.28, 69.2)
    rel_t_second = jnp.clip(jnp.exp(math.log(34.6) - 1.387451 * jax.random.uniform(key_of[34], (H, REL_T), jnp.float32) ** block_scale(key_of[34], (H, REL_T), ((0, 4), (1, 8)), -0.2, 0.2)), 8.64, 34.6)
    return {"latents": latents, "cotangent": cotangent, "text_embed": text_embed, "text_mask": text_mask, "band_ids": band_ids, "rel_index_s": rel_index_s, "rel_index_t": rel_index_t, "modulation": modulation, "qkv_master": qkv_master, "out_master": out_master, "cq_master": cq_master, "ckv_master": ckv_master, "cout_master": cout_master, "up_master": up_master, "down_master": down_master, "rel_s_master": rel_s_master, "rel_t_master": rel_t_master, "qkv_first": qkv_first, "out_first": out_first, "cq_first": cq_first, "ckv_first": ckv_first, "cout_first": cout_first, "up_first": up_first, "down_first": down_first, "rel_s_first": rel_s_first, "rel_t_first": rel_t_first, "qkv_second": qkv_second, "out_second": out_second, "cq_second": cq_second, "ckv_second": ckv_second, "cout_second": cout_second, "up_second": up_second, "down_second": down_second, "rel_s_second": rel_s_second, "rel_t_second": rel_t_second}


BETA_ONE = 0.9
BETA_TWO = 0.95
ADAM_EPS = 1e-08
DECAY_RATE = 0.1
HIGH = lax.Precision.HIGHEST

@jax.custom_vjp
def low(v):
    return lax.optimization_barrier(v.astype(jnp.bfloat16)).astype(jnp.float32)

@jax.custom_vjp
def low_back(v):
    return v

def low_keep(v):
    return (low(v), None)

def low_pass(kept, grad):
    return (grad,)

def back_keep(v):
    return (v, None)

def back_low(kept, grad):
    return (low(grad),)
low.defvjp(low_keep, low_pass)
low_back.defvjp(back_keep, back_low)

def learning_rates():
    inverse_root = D ** (-0.5)
    return (1.5 * inverse_root, 6.0 * inverse_root, 1.5 * inverse_root, 1.5 * inverse_root, 4.2 * inverse_root, 1.5 * inverse_root, 1.5 * FF ** (-0.5), 1.5, 1.5)

def round_both(tensor):
    return low(low_back(tensor))

def layer_norm(tensor):
    center = tensor - lax.optimization_barrier(jnp.mean(tensor, axis=-1, keepdims=True))
    return center * lax.rsqrt(lax.optimization_barrier(jnp.mean(center * center, axis=-1, keepdims=True)) + 1e-06)

def to_windows(tensor, window_kind):
    trailing = tensor.shape[1:]
    if window_kind == 0:
        return tensor.reshape((FRAMES, SIDE * SIDE) + trailing)
    halfway = SIDE // 2
    tensor = tensor.reshape((FRAMES, 2, halfway, 2, halfway) + trailing)
    tensor = jnp.transpose(tensor, (1, 3, 0, 2, 4) + tuple(range(5, 5 + len(trailing))))
    return tensor.reshape((4, FRAMES * halfway * halfway) + trailing)

def from_windows(tensor, window_kind):
    trailing = tensor.shape[2:]
    if window_kind == 0:
        return tensor.reshape((FRAMES * SIDE * SIDE,) + trailing)
    halfway = SIDE // 2
    tensor = tensor.reshape((2, 2, FRAMES, halfway, halfway) + trailing)
    tensor = jnp.transpose(tensor, (2, 0, 3, 1, 4) + tuple(range(5, 5 + len(trailing))))
    return tensor.reshape((FRAMES * SIDE * SIDE,) + trailing)

def softmax_rows(scores):
    scores = low_back(scores)
    return low(jnp.exp(scores - jax.nn.logsumexp(scores, axis=-1, keepdims=True)))

def one_block(latent, mod_rows, text_rows, valid, weights, index_tables):
    scaling = HD ** (-0.5)
    for layer_index in range(LAYERS):
        w_qkv, w_out, w_cq, w_ckv, w_cout, w_up, w_down = [low(item[layer_index]) for item in weights[:7]]
        table = low(weights[7 + layer_index])
        base = 9 * layer_index
        normed = low(layer_norm(latent) * (1.0 + mod_rows[base + 1]) + mod_rows[base])
        qkv = round_both(jnp.dot(normed, w_qkv, precision=HIGH)).reshape(BLOCK, H, 3, HD)
        windows = to_windows(qkv, layer_index)
        bias = table[:, index_tables[layer_index]]
        scores = jnp.einsum('wnhe,wmhe->whnm', windows[:, :, :, 0], windows[:, :, :, 1], precision=HIGH) * scaling + bias[None]
        probs = softmax_rows(scores)
        mixed = jnp.einsum('whnm,wmhe->wnhe', probs, windows[:, :, :, 2], precision=HIGH)
        mixed = round_both(from_windows(mixed, layer_index).reshape(BLOCK, D))
        branch = low_back(jnp.dot(mixed, w_out, precision=HIGH))
        latent = latent + mod_rows[base + 2] * branch
        normed = low(layer_norm(latent) * (1.0 + mod_rows[base + 4]) + mod_rows[base + 3])
        queries = round_both(jnp.dot(normed, w_cq, precision=HIGH)).reshape(BLOCK, H, HD)
        keyval = round_both(jnp.dot(text_rows, w_ckv, precision=HIGH)).reshape(TXT, H, 2, HD)
        scores = jnp.einsum('nhe,mhe->hnm', queries, keyval[:, :, 0], precision=HIGH) * scaling + (valid - 1.0) * 1000000000.0
        probs = softmax_rows(scores)
        mixed = jnp.einsum('hnm,mhe->nhe', probs, keyval[:, :, 1], precision=HIGH)
        mixed = round_both(mixed.reshape(BLOCK, D))
        branch = low_back(jnp.dot(mixed, w_cout, precision=HIGH))
        latent = latent + mod_rows[base + 5] * branch
        normed = low(layer_norm(latent) * (1.0 + mod_rows[base + 7]) + mod_rows[base + 6])
        hidden = low_back(jnp.dot(normed, w_up, precision=HIGH))
        active = low(jax.nn.gelu(hidden, approximate=True))
        branch = low_back(jnp.dot(active, w_down, precision=HIGH))
        latent = latent + mod_rows[base + 8] * branch
    return latent

def adam_update(master, first, second, grad, rate):
    first_new = BETA_ONE * first + (1.0 - BETA_ONE) * grad
    second_new = BETA_TWO * second + (1.0 - BETA_TWO) * grad * grad
    step_size = first_new / (1.0 - BETA_ONE ** STEP) / (jnp.sqrt(second_new / (1.0 - BETA_TWO ** STEP)) + ADAM_EPS)
    master_new = master - rate * (step_size + DECAY_RATE * master)
    return (master_new, first_new, second_new, master_new.astype(jnp.bfloat16))

def reference(latents, cotangent, text_embed, text_mask, band_ids, rel_index_s, rel_index_t, modulation, qkv_master, out_master, cq_master, ckv_master, cout_master, up_master, down_master, rel_s_master, rel_t_master, qkv_first, out_first, cq_first, ckv_first, cout_first, up_first, down_first, rel_s_first, rel_t_first, qkv_second, out_second, cq_second, ckv_second, cout_second, up_second, down_second, rel_s_second, rel_t_second):
    masters = (qkv_master, out_master, cq_master, ckv_master, cout_master, up_master, down_master, rel_s_master, rel_t_master)
    firsts = (qkv_first, out_first, cq_first, ckv_first, cout_first, up_first, down_first, rel_s_first, rel_t_first)
    seconds = (qkv_second, out_second, cq_second, ckv_second, cout_second, up_second, down_second, rel_s_second, rel_t_second)
    rates = learning_rates()
    block_count = TOKENS // BLOCK
    clip_of = jnp.arange(block_count, dtype=jnp.int32) // 2
    text_rows = text_embed.astype(jnp.float32)[clip_of]
    first_token = (jnp.arange(TXT, dtype=jnp.int32) == 0).astype(jnp.int32)
    valid_rows = jnp.maximum(text_mask, first_token[None]).astype(jnp.float32)[clip_of]
    band_rows = band_ids[clip_of]
    index_tables = (rel_index_s, rel_index_t)

    def forward(latent_all, modulation_all, weights):
        mod_blocks = modulation_all[band_rows]

        def block_apply(packed):
            return one_block(packed[0], packed[1], packed[2], packed[3], weights, index_tables)
        result = lax.map(jax.checkpoint(block_apply), (latent_all.reshape(block_count, BLOCK, D), mod_blocks, text_rows, valid_rows))
        return result.reshape(TOKENS, D)
    outputs, pullback = jax.vjp(forward, latents, modulation, masters)
    grad_latents, grad_modulation, grads = pullback(cotangent)
    updated = [adam_update(masters[item], firsts[item], seconds[item], grads[item], rates[item]) for item in range(9)]
    return (outputs, grad_latents, grad_modulation, updated[0][0], updated[0][1], updated[0][2], updated[0][3], updated[1][0], updated[1][1], updated[1][2], updated[1][3], updated[2][0], updated[2][1], updated[2][2], updated[2][3], updated[3][0], updated[3][1], updated[3][2], updated[3][3], updated[4][0], updated[4][1], updated[4][2], updated[4][3], updated[5][0], updated[5][1], updated[5][2], updated[5][3], updated[6][0], updated[6][1], updated[6][2], updated[6][3], updated[7][0], updated[7][1], updated[7][2], updated[7][3], updated[8][0], updated[8][1], updated[8][2], updated[8][3])
```

```python
import functools

import jax
import jax.numpy as jnp
from jax import lax
from jax.experimental import pallas as pl
from jax.experimental.pallas import tpu as pltpu
from jax.sharding import PartitionSpec as P

D = 1024
HD = 64
FF = 4096
FRAMES = 5
LAYERS = 2
STEP = 10
LANES = 128

BETA_ONE = 0.9
BETA_TWO = 0.95
ADAM_EPS = 1e-08
DECAY_RATE = 0.1


def learning_rates():
    inverse_root = D ** (-0.5)
    return (
        1.5 * inverse_root,
        6.0 * inverse_root,
        1.5 * inverse_root,
        1.5 * inverse_root,
        4.2 * inverse_root,
        1.5 * inverse_root,
        1.5 * FF ** (-0.5),
        1.5,
        1.5,
    )


def layer_norm(tensor):
    center = tensor - jnp.mean(tensor, axis=-1, keepdims=True)
    inverse = lax.rsqrt(jnp.mean(center * center, axis=-1, keepdims=True) + 1e-06)
    return (center * inverse, inverse)


def norm_back(grad_norm, normed, inverse):
    return inverse * (
        grad_norm
        - jnp.mean(grad_norm, axis=-1, keepdims=True)
        - normed * jnp.mean(grad_norm * normed, axis=-1, keepdims=True)
    )


def modulate_back(grad_latent, grad_input, normed, inverse, scaling):
    grad_norm = grad_input * (1.0 + scaling)
    return (
        grad_latent + norm_back(grad_norm, normed, inverse),
        jnp.sum(grad_input, axis=0),
        jnp.sum(grad_input * normed, axis=0),
    )


VM=pltpu.CompilerParams(vmem_limit_bytes=56*1024*1024)

def bias_kernel(table_ref, index_ref, out_ref):
    heads, groups, _ = table_ref.shape
    rows, cols = index_ref.shape
    def step(i, carry):
        r0 = pl.multiple_of(i * 16, 16)
        for c in range(cols // LANES):
            parts = [[] for _ in range(heads)]
            for half in range(2):
                idx = index_ref[pl.ds(r0 + half * 8, 8), pl.ds(c * LANES, LANES)]
                lo = idx & (LANES - 1)
                hi = idx >> 7
                for h in range(heads):
                    acc = jnp.zeros((8, LANES), jnp.float32)
                    for g in range(groups):
                        row = jnp.broadcast_to(table_ref[h, pl.ds(g, 1), :], (8, LANES))
                        val = jnp.take_along_axis(row, lo, axis=1, mode="promise_in_bounds")
                        acc = jnp.where(hi == g, val, acc)
                    parts[h].append(acc)
            for h in range(heads):
                out_ref[h, pl.ds(r0, 16), pl.ds(c * LANES, LANES)] = jnp.concatenate(parts[h], 0).astype(jnp.bfloat16)
        return carry
    lax.fori_loop(0, rows // 16, step, 0)

def make_bias(table, index):
    heads, reach = table.shape
    n = index.shape[0]
    pad = -n % LANES
    index = jnp.pad(index, ((0, 0), (0, pad)))
    return pl.pallas_call(bias_kernel,
        out_shape=jax.ShapeDtypeStruct((heads, n, n + pad), jnp.bfloat16),
        compiler_params=VM)(table.astype(jnp.float32).reshape(heads, reach // LANES, LANES), index)

LOW=64
def bucket_kernel(sum_ref, index_ref, out_ref):
    heads, rows, cols = sum_ref.shape
    high = out_ref.shape[0] // heads
    out_ref[...] = jnp.zeros_like(out_ref)
    hi_iota = lax.broadcasted_iota(jnp.int32, (high, cols), 0)
    lo_iota = lax.broadcasted_iota(jnp.int32, (LOW, cols), 0)
    def step(i, acc):
        r0 = pl.multiple_of(i * 8, 8)
        idx8 = index_ref[pl.ds(r0, 8), :]
        s8 = [sum_ref[h, pl.ds(r0, 8), :] for h in range(heads)]
        for r in range(8):
            idx = idx8[r:r+1]
            hot_hi = hi_iota == (idx >> 6)
            hot_lo = jnp.where(lo_iota == (idx & (LOW-1)), 1.0, 0.0).astype(jnp.bfloat16)
            left = jnp.concatenate([jnp.where(hot_hi, s8[h][r:r+1], 0.0) for h in range(heads)], 0).astype(jnp.bfloat16)
            acc = acc + lax.dot_general(left, hot_lo, (((1,),(1,)),((),())), preferred_element_type=jnp.float32)
        return acc
    out_ref[...] = lax.fori_loop(0, rows // 8, step, jnp.zeros(out_ref.shape, jnp.float32))

def bucket_sum(summed, index, reach):
    heads = summed.shape[0]
    out = pl.pallas_call(bucket_kernel,
        out_shape=jax.ShapeDtypeStruct((heads * (reach // LOW), LOW), jnp.float32),
        compiler_params=VM)(summed, index)
    return out.reshape(heads, reach)
QUARTER=64
NT=(((1,),(1,)),((),()))
TN=(((0,),(0,)),((),()))
def dot(a,b,dims=(((1,),(0,)),((),()))):
    return lax.dot_general(a,b,dims,preferred_element_type=jnp.float32)

def row_start(position, part):
    share = part // FRAMES
    return pl.multiple_of((position ^ share) * (FRAMES * QUARTER) + (part % FRAMES) * QUARTER, QUARTER)

def load_windows(ref, position, kind, step, cols):
    if kind == 0:
        return [jnp.concatenate([ref[pl.ds(row_start(position, 4 * step + t), QUARTER), cols] for t in range(4)], 0)]
    both = [[], []]
    for f in range(FRAMES):
        for k in range(2):
            block = ref[pl.ds(row_start(position, 4 * f + 2 * step + k), QUARTER), cols].astype(jnp.float32)
            block = block.reshape(4, 2, 8, block.shape[-1])
            for c in range(2):
                both[c].append(block[:, c].reshape(32, block.shape[-1]))
    return [jnp.concatenate(b, 0).astype(jnp.bfloat16) for b in both]

def store_windows(ref, position, kind, step, cols, values):
    if kind == 0:
        for t in range(4):
            ref[pl.ds(row_start(position, 4 * step + t), QUARTER), cols] = values[0][t * QUARTER:(t + 1) * QUARTER].astype(ref.dtype)
        return
    for f in range(FRAMES):
        for k in range(2):
            at = (2 * f + k) * 32
            block = jnp.stack([v[at:at + 32].reshape(4, 8, v.shape[-1]) for v in values], axis=1)
            ref[pl.ds(row_start(position, 4 * f + 2 * step + k), QUARTER), cols] = block.reshape(QUARTER, block.shape[-1]).astype(ref.dtype)

def self_forward_kernel(kind, position_ref, qkv_ref, bias_ref, out_ref, probs_ref):
    step = pl.program_id(0)
    position = position_ref[0]
    width = out_ref.shape[1]
    heads = width // HD
    size = probs_ref.shape[2]
    q, k, v = [load_windows(qkv_ref, position, kind, step, pl.ds(j * width, width)) for j in range(3)]
    lane = lax.broadcasted_iota(jnp.int32, (size, width), 1) // HD
    results = []
    for w in range(len(q)):
        total = jnp.zeros((size, width), jnp.float32)
        scaled = q[w] * jnp.bfloat16(HD ** -0.5)
        for h in range(heads):
            s = dot(jnp.where(lane == h, scaled, jnp.bfloat16(0)), k[w], NT) + bias_ref[h, :, pl.ds(0, size)].astype(jnp.float32)
            s = s - jnp.max(s, axis=-1, keepdims=True)
            e = jnp.exp(s)
            p = (e * (1.0 / jnp.sum(e, axis=-1, keepdims=True))).astype(jnp.bfloat16)
            probs_ref[w, h] = p
            total = total + dot(p, jnp.where(lane == h, v[w], jnp.bfloat16(0)))
        results.append(total)
    store_windows(out_ref, position, kind, step, pl.ds(0, width), results)

def self_forward_call(kind, position, qkv, bias):
    rows, width = qkv.shape
    width //= 3
    heads = width // HD
    size = 256 if kind == 0 else 320
    per = 1 if kind == 0 else 2
    steps = rows // size // per
    return pl.pallas_call(
        functools.partial(self_forward_kernel, kind),
        out_shape=(jax.ShapeDtypeStruct((rows, width), jnp.bfloat16),
                   jax.ShapeDtypeStruct((steps * per, heads, size, size), jnp.bfloat16)),
        grid_spec=pltpu.PrefetchScalarGridSpec(
            num_scalar_prefetch=1, grid=(steps,),
            in_specs=[pl.BlockSpec(qkv.shape, lambda i, p: (0, 0)),
                      pl.BlockSpec(bias.shape, lambda i, p: (0, 0, 0))],
            out_specs=[pl.BlockSpec((rows, width), lambda i, p: (0, 0)),
                       pl.BlockSpec((per, heads, size, size), lambda i, p: (i, 0, 0, 0))]),
        compiler_params=VM,
        name="self_forward",
    )(position, qkv, bias)

def self_backward_kernel(kind, position_ref, qkv_ref, probs_ref, grad_ref, dqkv_ref, sum_ref):
    step = pl.program_id(0)
    position = position_ref[0]
    width = grad_ref.shape[1]
    heads = width // HD
    size = probs_ref.shape[2]
    q, k, v = [load_windows(qkv_ref, position, kind, step, pl.ds(j * width, width)) for j in range(3)]
    g = load_windows(grad_ref, position, kind, step, pl.ds(0, width))
    lane = lax.broadcasted_iota(jnp.int32, (size, width), 1) // HD
    zero = jnp.bfloat16(0)
    @pl.when(step == 0)
    def _():
        sum_ref[...] = jnp.zeros_like(sum_ref)
    outs = [[], [], []]
    for w in range(len(q)):
        dq = jnp.zeros((size, width), jnp.float32)
        dk = jnp.zeros((size, width), jnp.float32)
        dv = jnp.zeros((size, width), jnp.float32)
        scaled = q[w] * jnp.bfloat16(HD ** -0.5)
        kscaled = k[w] * jnp.bfloat16(HD ** -0.5)
        for h in range(heads):
            mine = lane == h
            gh = jnp.where(mine, g[w], zero)
            p16 = probs_ref[w, h]
            p = p16.astype(jnp.float32)
            dp = dot(gh, v[w], NT)
            ds = p * (dp - jnp.sum(p * dp, axis=-1, keepdims=True))
            ds16 = ds.astype(jnp.bfloat16)
            sum_ref[h] += ds16.astype(jnp.float32)
            dq = dq + dot(ds16, jnp.where(mine, kscaled, zero))
            dk = dk + dot(ds16, jnp.where(mine, scaled, zero), TN)
            dv = dv + dot(p16, gh, TN)
        outs[0].append(dq); outs[1].append(dk); outs[2].append(dv)
    for j in range(3):
        store_windows(dqkv_ref, position, kind, step, pl.ds(j * width, width), outs[j])

def self_backward_call(kind, position, qkv, probs, grad):
    rows, width = grad.shape
    heads = width // HD
    size = probs.shape[2]
    per = 1 if kind == 0 else 2
    steps = rows // size // per
    return pl.pallas_call(
        functools.partial(self_backward_kernel, kind),
        out_shape=(jax.ShapeDtypeStruct(qkv.shape, jnp.bfloat16),
                   jax.ShapeDtypeStruct((heads, size, size), jnp.float32)),
        grid_spec=pltpu.PrefetchScalarGridSpec(
            num_scalar_prefetch=1, grid=(steps,),
            in_specs=[pl.BlockSpec(qkv.shape, lambda i, p: (0, 0)),
                      pl.BlockSpec((per, heads, size, size), lambda i, p: (i, 0, 0, 0)),
                      pl.BlockSpec(grad.shape, lambda i, p: (0, 0))],
            out_specs=[pl.BlockSpec(qkv.shape, lambda i, p: (0, 0)),
                       pl.BlockSpec((heads, size, size), lambda i, p: (0, 0, 0))]),
        compiler_params=VM,
        name="self_backward",
    )(position, qkv, probs, grad)
PAD=128

def cross_forward_kernel(q_ref, k_ref, v_ref, bias_ref, out_ref, probs_ref):
    rows = q_ref.shape[0]
    first = lax.broadcasted_iota(jnp.int32, (rows, LANES), 1) < HD
    vfirst = lax.broadcasted_iota(jnp.int32, (PAD, LANES), 1) < HD
    zero = jnp.bfloat16(0)
    q = q_ref[...] * jnp.bfloat16(HD ** -0.5)
    total = jnp.zeros((rows, LANES), jnp.float32)
    for half in range(2):
        s = dot(jnp.where(first == (half == 0), q, zero), k_ref[...], NT) + bias_ref[...]
        s = s - jnp.max(s, axis=-1, keepdims=True)
        e = jnp.exp(s)
        p = (e * (1.0 / jnp.sum(e, axis=-1, keepdims=True))).astype(jnp.bfloat16)
        probs_ref[half] = p
        total = total + dot(p, jnp.where(vfirst == (half == 0), v_ref[...], zero))
    out_ref[...] = total.astype(jnp.bfloat16)

def cross_forward_call(q, k, v, bias):
    rows, width = q.shape
    pairs = width // LANES
    col = lambda i: (0, i)
    return pl.pallas_call(
        cross_forward_kernel, grid=(pairs,),
        in_specs=[pl.BlockSpec((rows, LANES), col), pl.BlockSpec((PAD, LANES), col), pl.BlockSpec((PAD, LANES), col),
                  pl.BlockSpec((1, PAD), lambda i: (0, 0))],
        out_specs=[pl.BlockSpec((rows, LANES), col), pl.BlockSpec((2, rows, PAD), lambda i: (i, 0, 0))],
        out_shape=[jax.ShapeDtypeStruct((rows, width), jnp.bfloat16), jax.ShapeDtypeStruct((2 * pairs, rows, PAD), jnp.bfloat16)],
        compiler_params=VM, name="cross_forward")(q, k, v, bias)

def cross_backward_kernel(q_ref, k_ref, v_ref, probs_ref, grad_ref, dq_ref, dk_ref, dv_ref):
    rows = q_ref.shape[0]
    first = lax.broadcasted_iota(jnp.int32, (rows, LANES), 1) < HD
    kfirst = lax.broadcasted_iota(jnp.int32, (PAD, LANES), 1) < HD
    zero = jnp.bfloat16(0)
    q = q_ref[...] * jnp.bfloat16(HD ** -0.5)
    k = k_ref[...] * jnp.bfloat16(HD ** -0.5)
    dq = jnp.zeros((rows, LANES), jnp.float32)
    dk = jnp.zeros((PAD, LANES), jnp.float32)
    dv = jnp.zeros((PAD, LANES), jnp.float32)
    for half in range(2):
        mine = first == (half == 0)
        g = jnp.where(mine, grad_ref[...], zero)
        p16 = probs_ref[half]
        p = p16.astype(jnp.float32)
        dp = dot(g, v_ref[...], NT)
        ds = (p * (dp - jnp.sum(p * dp, axis=-1, keepdims=True))).astype(jnp.bfloat16)
        dq = dq + dot(ds, jnp.where(kfirst == (half == 0), k, zero))
        dk = dk + dot(ds, jnp.where(mine, q, zero), TN)
        dv = dv + dot(p16, g, TN)
    dq_ref[...] = dq.astype(jnp.bfloat16)
    dk_ref[...] = dk
    dv_ref[...] = dv

def cross_backward_call(q, k, v, probs, grad):
    rows, width = q.shape
    pairs = width // LANES
    col = lambda i: (0, i)
    tok = pl.BlockSpec((rows, LANES), col); txt = pl.BlockSpec((PAD, LANES), col)
    return pl.pallas_call(
        cross_backward_kernel, grid=(pairs,),
        in_specs=[tok, txt, txt, pl.BlockSpec((2, rows, PAD), lambda i: (i, 0, 0)), tok],
        out_specs=[tok, txt, txt],
        out_shape=[jax.ShapeDtypeStruct((rows, width), jnp.bfloat16), jax.ShapeDtypeStruct((PAD, width), jnp.float32), jax.ShapeDtypeStruct((PAD, width), jnp.float32)],
        compiler_params=VM, name="cross_backward")(q, k, v, probs, grad)

def gelu_parts(u):
    inner = 0.7978845608028654 * (u + 0.044715 * u * u * u)
    th = jnp.tanh(inner)
    slope = 0.5 * (1.0 + th) + 0.5 * u * (1.0 - th * th) * (0.7978845608028654 * (1.0 + 3.0 * 0.044715 * u * u))
    return 0.5 * u * (1.0 + th), slope


def feed_forward_kernel(a_ref, b_ref, up_ref, down_ref, hidden_ref, active_ref, pa_ref, pb_ref, acc_ref):
    step = pl.program_id(0)
    rows = a_ref.shape[0]
    for at, ref in ((0, a_ref), (rows, b_ref)):
        u = dot(ref[...], up_ref[...])
        hidden_ref[pl.ds(at, rows), :] = u.astype(jnp.bfloat16)
        active = jax.nn.gelu(u, approximate=True).astype(jnp.bfloat16)
        active_ref[pl.ds(at, rows), :] = active
        part = dot(active, down_ref[...], NT)

        @pl.when(step == 0)
        def _():
            acc_ref[pl.ds(at, rows), :] = part

        @pl.when(step > 0)
        def _():
            acc_ref[pl.ds(at, rows), :] += part

    @pl.when(step == pl.num_programs(0) - 1)
    def _():
        pa_ref[...] = acc_ref[pl.ds(0, rows), :].astype(jnp.bfloat16)
        pb_ref[...] = acc_ref[pl.ds(rows, rows), :].astype(jnp.bfloat16)


FF_TILE = 256


def feed_forward_call(a, b, weights):
    rows, width = a.shape
    hidden = weights.shape[1] // 2
    tiles = hidden // FF_TILE
    whole = pl.BlockSpec((rows, width), lambda i: (0, 0))
    strip = pl.BlockSpec((2 * rows, FF_TILE), lambda i: (0, i))
    return pl.pallas_call(
        feed_forward_kernel,
        grid=(tiles,),
        in_specs=[
            whole,
            whole,
            pl.BlockSpec((width, FF_TILE), lambda i: (0, i)),
            pl.BlockSpec((width, FF_TILE), lambda i: (0, tiles + i)),
        ],
        out_specs=[strip, strip, whole, whole],
        out_shape=[
            jax.ShapeDtypeStruct((2 * rows, hidden), jnp.bfloat16),
            jax.ShapeDtypeStruct((2 * rows, hidden), jnp.bfloat16),
            jax.ShapeDtypeStruct((rows, width), jnp.bfloat16),
            jax.ShapeDtypeStruct((rows, width), jnp.bfloat16),
        ],
        scratch_shapes=[pltpu.VMEM((2 * rows, width), jnp.float32)],
        compiler_params=VM,
        cost_estimate=pl.CostEstimate(
            flops=8 * rows * width * hidden, bytes_accessed=4 * width * hidden + 12 * rows * width, transcendentals=2 * rows * hidden
        ),
        name="feed_forward",
    )(a, b, weights, weights)


def feed_backward_kernel(a_ref, b_ref, hidden_ref, up_ref, down_ref, grad_ref, pa_ref, pb_ref, acc_ref):
    step = pl.program_id(0)
    rows = a_ref.shape[0]
    for at, ref in ((0, a_ref), (rows, b_ref)):
        slope = gelu_parts(hidden_ref[pl.ds(at, rows), :].astype(jnp.float32))[1]
        grad = (dot(ref[...], down_ref[...]) * slope).astype(jnp.bfloat16)
        grad_ref[pl.ds(at, rows), :] = grad
        part = dot(grad, up_ref[...], NT)

        @pl.when(step == 0)
        def _():
            acc_ref[pl.ds(at, rows), :] = part

        @pl.when(step > 0)
        def _():
            acc_ref[pl.ds(at, rows), :] += part

    @pl.when(step == pl.num_programs(0) - 1)
    def _():
        pa_ref[...] = acc_ref[pl.ds(0, rows), :].astype(jnp.bfloat16)
        pb_ref[...] = acc_ref[pl.ds(rows, rows), :].astype(jnp.bfloat16)


def feed_backward_call(a, b, hidden, weights):
    rows, width = a.shape
    units = weights.shape[1] // 2
    tiles = units // FF_TILE
    whole = pl.BlockSpec((rows, width), lambda i: (0, 0))
    strip = pl.BlockSpec((2 * rows, FF_TILE), lambda i: (0, i))
    return pl.pallas_call(
        feed_backward_kernel,
        grid=(tiles,),
        in_specs=[
            whole,
            whole,
            strip,
            pl.BlockSpec((width, FF_TILE), lambda i: (0, i)),
            pl.BlockSpec((width, FF_TILE), lambda i: (0, tiles + i)),
        ],
        out_specs=[strip, whole, whole],
        out_shape=[
            jax.ShapeDtypeStruct((2 * rows, units), jnp.bfloat16),
            jax.ShapeDtypeStruct((rows, width), jnp.bfloat16),
            jax.ShapeDtypeStruct((rows, width), jnp.bfloat16),
        ],
        scratch_shapes=[pltpu.VMEM((2 * rows, width), jnp.float32)],
        compiler_params=VM,
        cost_estimate=pl.CostEstimate(
            flops=8 * rows * width * units, bytes_accessed=4 * width * units + 10 * rows * width, transcendentals=2 * rows * units
        ),
        name="feed_backward",
    )(a, b, hidden, weights, weights)

def adam_update(master, first, second, grad, rate):
    first_new = BETA_ONE * first + (1.0 - BETA_ONE) * grad
    second_new = BETA_TWO * second + (1.0 - BETA_TWO) * grad * grad
    step_size = (
        first_new
        / (1.0 - BETA_ONE**STEP)
        / (jnp.sqrt(second_new / (1.0 - BETA_TWO**STEP)) + ADAM_EPS)
    )
    master_new = master - rate * (step_size + DECAY_RATE * master)
    return (master_new, first_new, second_new, master_new.astype(jnp.bfloat16))


def exchange(value, axis, bit, size):
    return lax.ppermute(value, axis, [(i, i ^ bit) for i in range(size)])


def share_rows(own):
    near = exchange(own, "mp", 1, 4)
    far = exchange(own, "mp", 2, 4)
    return (own, near, far, exchange(far, "mp", 1, 4))


def collect_parts(parts):
    beside = exchange(parts[3], "mp", 1, 4)
    crossing = (parts[2].astype(jnp.float32) + beside.astype(jnp.float32)).astype(jnp.bfloat16)
    far = exchange(crossing, "mp", 2, 4)
    near = exchange(parts[1], "mp", 1, 4)
    return parts[0].astype(jnp.float32) + near.astype(jnp.float32) + far.astype(jnp.float32)


def bits_of(size):
    return [1 << n for n in range(size.bit_length() - 1)]


def halve_rows(total, size):
    me = lax.axis_index("dp")
    width = total.shape[1]
    rows = total.shape[0] // size
    blocks = total.reshape(size, rows, width)
    for n, bit in enumerate(bits_of(size)):
        pairs = blocks.reshape(blocks.shape[0] // 2, 2, rows, width)
        mine = (me >> n) & 1
        keep = lax.dynamic_index_in_dim(pairs, mine, 1, keepdims=False)
        send = lax.dynamic_index_in_dim(pairs, 1 - mine, 1, keepdims=False)
        got = exchange(send, "dp", bit, size)
        total = keep.astype(jnp.float32) + got.astype(jnp.float32)
        blocks = total.astype(jnp.bfloat16)
    return total.reshape(rows, width)


def gather_small(own, size):
    me = lax.axis_index("dp")
    slots = own[None]
    for n, bit in enumerate(bits_of(size)):
        got = exchange(slots, "dp", bit, size)
        slots = jnp.where(((me >> n) & 1) == 0, jnp.concatenate([slots, got]), jnp.concatenate([got, slots]))
    return slots


def modulate(latent, scale, shift):
    normed, inverse = layer_norm(latent)
    return (normed * (1.0 + scale) + shift).astype(jnp.bfloat16)


def split_heads(columns, parts):
    rows = columns.shape[0]
    return columns.reshape(rows, -1, parts, HD).swapaxes(1, 2).reshape(rows, -1)


def join_heads(columns, parts):
    rows = columns.shape[0]
    return columns.reshape(rows, parts, -1, HD).swapaxes(1, 2).reshape(rows, -1)


def narrow(value):
    return value.astype(jnp.bfloat16)


def gather_group(shards):
    return lax.all_gather(jnp.concatenate(shards, axis=1), "dp", axis=0, tiled=True)


def mm(a, b, dims=(((1,), (0,)), ((), ()))):
    return lax.dot_general(a, b, dims, preferred_element_type=jnp.float32)


def body(*args):
    (latents, cotangent, text_embed, text_mask, band_ids, rel_index_s, rel_index_t, modulation) = args[:8]
    masters, firsts, seconds = args[8:17], args[17:26], args[26:35]
    groups = lax.axis_size("dp")
    rates = learning_rates()
    position = lax.axis_index("mp").astype(jnp.int32)[None]
    clip_index = lax.axis_index("dp") // 2
    text_rows = lax.dynamic_index_in_dim(text_embed, clip_index, 0, keepdims=False)
    texts = text_rows.shape[0]
    text_rows = jnp.pad(text_rows, ((0, PAD - texts), (0, 0)))
    mask_row = lax.dynamic_index_in_dim(text_mask, clip_index, 0, keepdims=False)
    column = jnp.arange(PAD, dtype=jnp.int32)
    valid = jnp.maximum(jnp.pad(mask_row, (0, PAD - texts)), (column == 0).astype(jnp.int32)).astype(jnp.float32)
    valid_bias = jnp.where(column < texts, (valid - 1.0) * 1000000000.0, -1e30)[None]
    band_now = lax.dynamic_index_in_dim(band_ids, clip_index, 0, keepdims=False)
    selector = (jnp.arange(modulation.shape[0], dtype=jnp.int32) == band_now).astype(jnp.float32)
    mod_rows = lax.dynamic_index_in_dim(modulation, band_now, 0, keepdims=False)

    tables = gather_small(jnp.concatenate([narrow(masters[7]), narrow(masters[8])], axis=1), groups)
    tables = tables.swapaxes(0, 1)
    cut = masters[7].shape[1]
    table_s = tables[:, :, :cut].reshape(tables.shape[0], -1)
    table_t = tables[:, :, cut:].reshape(tables.shape[0], -1)
    biases = (make_bias(table_s, rel_index_s), make_bias(table_t, rel_index_t))
    index_tables = (rel_index_s, rel_index_t)
    reaches = (table_s.shape[1], table_t.shape[1])

    weights = []
    for layer in range(LAYERS):
        self_group = gather_group([split_heads(narrow(masters[0][layer]), 3), narrow(masters[1][layer]).T])
        cross_group = gather_group(
            [narrow(masters[2][layer]), narrow(masters[4][layer]).T, split_heads(narrow(masters[3][layer]), 2)]
        )
        feed_group = gather_group([narrow(masters[5][layer]), narrow(masters[6][layer]).T])
        weights.append((self_group, cross_group, feed_group))

    latent = latents
    saved = []
    wide = masters[1].shape[1]
    for layer in range(LAYERS):
        self_w, cross_w, feed_w = weights[layer]
        base = 9 * layer
        record = {"in": latent}
        rows = share_rows(modulate(latent, mod_rows[base + 1], mod_rows[base]))
        qkv = jnp.concatenate([narrow(mm(item, self_w[:, : 3 * wide])) for item in rows], axis=0)
        mixed, probs = self_forward_call(layer, position, qkv, biases[layer])
        w_out = self_w[:, 3 * wide :]
        own = latents.shape[0]
        parts = [narrow(mm(mixed[k * own : (k + 1) * own], w_out, NT)) for k in range(4)]
        branch = collect_parts(parts)
        record["self"] = (rows, qkv, probs, mixed, branch)
        latent = latent + mod_rows[base + 2] * branch
        record["mid"] = latent
        normed = modulate(latent, mod_rows[base + 4], mod_rows[base + 3])
        keyval = share_rows(narrow(mm(text_rows, cross_w[:, 2 * wide :])))
        keys = jnp.concatenate([item[:, :wide] for item in keyval], axis=1)
        values = jnp.concatenate([item[:, wide:] for item in keyval], axis=1)
        cross_all = share_rows(cross_w[:, : 2 * wide])
        w_cq = jnp.concatenate([item[:, :wide] for item in cross_all], axis=1)
        w_cout = jnp.concatenate([item[:, wide:] for item in cross_all], axis=1)
        queries = narrow(mm(normed, w_cq))
        mixed, probs = cross_forward_call(queries, keys, values, valid_bias)
        branch = mm(mixed, w_cout, NT)
        record["cross"] = (normed, queries, keys, values, probs, mixed, branch, w_cq, w_cout)
        latent = latent + mod_rows[base + 5] * branch
        record["late"] = latent
        rows = share_rows(modulate(latent, mod_rows[base + 7], mod_rows[base + 6]))
        hidden_near, active_near, p0, p1 = feed_forward_call(rows[0], rows[1], feed_w)
        hidden_far, active_far, p2, p3 = feed_forward_call(rows[2], rows[3], feed_w)
        branch = collect_parts([p0, p1, p2, p3])
        record["feed"] = (rows, (hidden_near, hidden_far), (active_near, active_far), branch)
        latent = latent + mod_rows[base + 8] * branch
        saved.append(record)

    grad_latent = cotangent
    mod_grads = [None, None]
    reduced = [None, None]
    for layer in reversed(range(LAYERS)):
        self_w, cross_w, feed_w = weights[layer]
        base = 9 * layer
        record = saved[layer]
        rows, hiddens, actives, branch = record["feed"]
        gate_m = jnp.sum(grad_latent * branch, axis=0)
        grads = share_rows(narrow(mod_rows[base + 8] * grad_latent))
        dh_near, p0, p1 = feed_backward_call(grads[0], grads[1], hiddens[0], feed_w)
        dh_far, p2, p3 = feed_backward_call(grads[2], grads[3], hiddens[1], feed_w)
        grad_input = collect_parts([p0, p1, p2, p3])
        grad_hidden = jnp.concatenate([dh_near, dh_far], axis=0)
        active = jnp.concatenate(actives, axis=0)
        all_rows = jnp.concatenate(rows, axis=0)
        all_grads = jnp.concatenate(grads, axis=0)
        feed_g = jnp.concatenate([narrow(mm(all_rows, grad_hidden, TN)), narrow(mm(all_grads, active, TN))], axis=1)
        feed_sum = halve_rows(feed_g, groups)
        normed, inverse = layer_norm(record["late"])
        grad_latent, shift_m, scale_m = modulate_back(grad_latent, grad_input, normed, inverse, mod_rows[base + 7])

        hidden, queries, keys, values, probs, mixed, branch, w_cq, w_cout = record["cross"]
        gate_c = jnp.sum(grad_latent * branch, axis=0)
        grad_rows = narrow(mod_rows[base + 5] * grad_latent)
        grad_mixed = narrow(mm(grad_rows, w_cout))
        grad_query, grad_key, grad_value = cross_backward_call(queries, keys, values, probs, grad_mixed)
        grad_input = mm(grad_query, w_cq, NT)
        grad_cq = narrow(mm(hidden, grad_query, TN))
        grad_cout = narrow(mm(grad_rows, mixed, TN))
        cross_parts = [
            jnp.concatenate([grad_cq[:, k * wide : (k + 1) * wide], grad_cout[:, k * wide : (k + 1) * wide]], axis=1) for k in range(4)
        ]
        cross_g = collect_parts(cross_parts)
        kv_parts = [
            narrow(jnp.concatenate([grad_key[:, k * wide : (k + 1) * wide], grad_value[:, k * wide : (k + 1) * wide]], axis=1))
            for k in range(4)
        ]
        grad_kv = narrow(collect_parts(kv_parts))
        cross_g = jnp.concatenate([narrow(cross_g), narrow(mm(text_rows, grad_kv, TN))], axis=1)
        cross_sum = halve_rows(cross_g, groups)
        normed, inverse = layer_norm(record["mid"])
        grad_latent, shift_c, scale_c = modulate_back(grad_latent, grad_input, normed, inverse, mod_rows[base + 4])

        rows, qkv, probs, mixed, branch = record["self"]
        gate_a = jnp.sum(grad_latent * branch, axis=0)
        grads = share_rows(narrow(mod_rows[base + 2] * grad_latent))
        w_out = self_w[:, 3 * wide :]
        grad_mixed = jnp.concatenate([narrow(mm(item, w_out)) for item in grads], axis=0)
        grad_qkv, summed = self_backward_call(layer, position, qkv, probs, grad_mixed)
        parts = [narrow(mm(grad_qkv[k * own : (k + 1) * own], self_w[:, : 3 * wide], NT)) for k in range(4)]
        grad_input = collect_parts(parts)
        all_rows = jnp.concatenate(rows, axis=0)
        all_grads = jnp.concatenate(grads, axis=0)
        self_g = jnp.concatenate([narrow(mm(all_rows, grad_qkv, TN)), narrow(mm(all_grads, mixed, TN))], axis=1)
        self_sum = halve_rows(self_g, groups)
        table_g = bucket_sum(summed, index_tables[layer], reaches[layer])
        table_g = table_g.reshape(table_g.shape[0], groups, -1).swapaxes(0, 1).reshape(-1, reaches[layer] // groups)
        table_sum = halve_rows(narrow(table_g), groups)
        normed, inverse = layer_norm(record["in"])
        grad_latent, shift_a, scale_a = modulate_back(grad_latent, grad_input, normed, inverse, mod_rows[base + 1])
        mod_grads[layer] = [shift_a, scale_a, gate_a, shift_c, scale_c, gate_c, shift_m, scale_m, gate_m]
        reduced[layer] = (
            join_heads(self_sum[:, : 3 * wide], 3),
            self_sum[:, 3 * wide :].T,
            cross_sum[:, :wide],
            join_heads(cross_sum[:, 2 * wide :], 2),
            cross_sum[:, wide : 2 * wide].T,
            feed_sum[:, : masters[5].shape[2]],
            feed_sum[:, masters[5].shape[2] :].T,
            table_sum,
        )
    mod_local = jnp.stack(mod_grads[0] + mod_grads[1], axis=0)
    for bit in (1, 2):
        mod_local = mod_local + exchange(mod_local, "mp", bit, 4)
    grad_modulation = selector[:, None, None] * mod_local[None]
    for bit in bits_of(groups):
        grad_modulation = grad_modulation + exchange(grad_modulation, "dp", bit, groups)
    results = [latent, grad_latent, grad_modulation]
    for item in range(9):
        if item < 7:
            grad = jnp.stack([reduced[0][item], reduced[1][item]], axis=0)
        else:
            grad = reduced[item - 7][7]
        results.extend(adam_update(masters[item], firsts[item], seconds[item], grad, rates[item]))
    return tuple(results)


def solution(mesh):
    in_specs = (
        P(("dp", "mp"), None),
        P(("dp", "mp"), None),
        P(),
        P(),
        P(),
        P(),
        P(),
        P(),
        P(None, "dp", "mp"),
        P(None, "mp", "dp"),
        P(None, "dp", "mp"),
        P(None, "dp", "mp"),
        P(None, "mp", "dp"),
        P(None, "dp", "mp"),
        P(None, "mp", "dp"),
        P("mp", "dp"),
        P("mp", "dp"),
        P(None, "dp", "mp"),
        P(None, "mp", "dp"),
        P(None, "dp", "mp"),
        P(None, "dp", "mp"),
        P(None, "mp", "dp"),
        P(None, "dp", "mp"),
        P(None, "mp", "dp"),
        P("mp", "dp"),
        P("mp", "dp"),
        P(None, "dp", "mp"),
        P(None, "mp", "dp"),
        P(None, "dp", "mp"),
        P(None, "dp", "mp"),
        P(None, "mp", "dp"),
        P(None, "dp", "mp"),
        P(None, "mp", "dp"),
        P("mp", "dp"),
        P("mp", "dp"),
    )
    out_specs = (
        P(("dp", "mp"), None),
        P(("dp", "mp"), None),
        P(),
        P(None, "dp", "mp"),
        P(None, "dp", "mp"),
        P(None, "dp", "mp"),
        P(None, "dp", "mp"),
        P(None, "mp", "dp"),
        P(None, "mp", "dp"),
        P(None, "mp", "dp"),
        P(None, "mp", "dp"),
        P(None, "dp", "mp"),
        P(None, "dp", "mp"),
        P(None, "dp", "mp"),
        P(None, "dp", "mp"),
        P(None, "dp", "mp"),
        P(None, "dp", "mp"),
        P(None, "dp", "mp"),
        P(None, "dp", "mp"),
        P(None, "mp", "dp"),
        P(None, "mp", "dp"),
        P(None, "mp", "dp"),
        P(None, "mp", "dp"),
        P(None, "dp", "mp"),
        P(None, "dp", "mp"),
        P(None, "dp", "mp"),
        P(None, "dp", "mp"),
        P(None, "mp", "dp"),
        P(None, "mp", "dp"),
        P(None, "mp", "dp"),
        P(None, "mp", "dp"),
        P("mp", "dp"),
        P("mp", "dp"),
        P("mp", "dp"),
        P("mp", "dp"),
        P("mp", "dp"),
        P("mp", "dp"),
        P("mp", "dp"),
        P("mp", "dp"),
    )
    return jax.shard_map(body, mesh=mesh, in_specs=in_specs, out_specs=out_specs, check_vma=False)
```

```python
import functools

import jax
import jax.numpy as jnp
from jax import lax
from jax.experimental import pallas as pl
from jax.experimental.pallas import tpu as pltpu
from jax.sharding import PartitionSpec as P

D = 1024
HD = 64
FF = 4096
FRAMES = 5
LAYERS = 2
STEP = 10
LANES = 128

BETA_ONE = 0.9
BETA_TWO = 0.95
ADAM_EPS = 1e-08
DECAY_RATE = 0.1


def learning_rates():
    inverse_root = D ** (-0.5)
    return (
        1.5 * inverse_root,
        6.0 * inverse_root,
        1.5 * inverse_root,
        1.5 * inverse_root,
        4.2 * inverse_root,
        1.5 * inverse_root,
        1.5 * FF ** (-0.5),
        1.5,
        1.5,
    )


def layer_norm(tensor):
    center = tensor - jnp.mean(tensor, axis=-1, keepdims=True)
    inverse = lax.rsqrt(jnp.mean(center * center, axis=-1, keepdims=True) + 1e-06)
    return (center * inverse, inverse)


def norm_back(grad_norm, normed, inverse):
    return inverse * (
        grad_norm
        - jnp.mean(grad_norm, axis=-1, keepdims=True)
        - normed * jnp.mean(grad_norm * normed, axis=-1, keepdims=True)
    )


def modulate_back(grad_latent, grad_input, normed, inverse, scaling):
    grad_norm = grad_input * (1.0 + scaling)
    return (
        grad_latent + norm_back(grad_norm, normed, inverse),
        jnp.sum(grad_input, axis=0),
        jnp.sum(grad_input * normed, axis=0),
    )


VM = pltpu.CompilerParams(vmem_limit_bytes=56 * 1024 * 1024)
LIGHT = pl.CostEstimate(flops=1, bytes_accessed=1, transcendentals=0)

def bias_kernel(table_ref, index_ref, out_ref):
    heads, groups, _ = table_ref.shape
    rows, cols = index_ref.shape
    def step(i, carry):
        r0 = pl.multiple_of(i * 16, 16)
        for c in range(cols // LANES):
            parts = [[] for _ in range(heads)]
            for half in range(2):
                idx = index_ref[pl.ds(r0 + half * 8, 8), pl.ds(c * LANES, LANES)]
                lo = idx & (LANES - 1)
                hi = idx >> 7
                for h in range(heads):
                    acc = jnp.zeros((8, LANES), jnp.float32)
                    for g in range(groups):
                        row = jnp.broadcast_to(table_ref[h, pl.ds(g, 1), :], (8, LANES))
                        val = jnp.take_along_axis(row, lo, axis=1, mode="promise_in_bounds")
                        acc = jnp.where(hi == g, val, acc)
                    parts[h].append(acc)
            for h in range(heads):
                out_ref[h, pl.ds(r0, 16), pl.ds(c * LANES, LANES)] = jnp.concatenate(parts[h], 0).astype(jnp.bfloat16)
        return carry
    lax.fori_loop(0, rows // 16, step, 0)

def make_bias(table, index):
    heads, reach = table.shape
    n = index.shape[0]
    pad = -n % LANES
    index = jnp.pad(index, ((0, 0), (0, pad)))
    return pl.pallas_call(bias_kernel,
        out_shape=jax.ShapeDtypeStruct((heads, n, n + pad), jnp.bfloat16),
        cost_estimate=LIGHT, compiler_params=VM)(table.astype(jnp.float32).reshape(heads, reach // LANES, LANES), index)

LOW=64
def bucket_kernel(sum_ref, index_ref, out_ref):
    heads, rows, cols = sum_ref.shape
    high = out_ref.shape[0] // heads
    out_ref[...] = jnp.zeros_like(out_ref)
    hi_iota = lax.broadcasted_iota(jnp.int32, (high, cols), 0)
    lo_iota = lax.broadcasted_iota(jnp.int32, (LOW, cols), 0)
    def step(i, acc):
        r0 = pl.multiple_of(i * 8, 8)
        idx8 = index_ref[pl.ds(r0, 8), :]
        s8 = [sum_ref[h, pl.ds(r0, 8), :] for h in range(heads)]
        for r in range(8):
            idx = idx8[r:r+1]
            hot_hi = hi_iota == (idx >> 6)
            hot_lo = jnp.where(lo_iota == (idx & (LOW-1)), 1.0, 0.0).astype(jnp.bfloat16)
            left = jnp.concatenate([jnp.where(hot_hi, s8[h][r:r+1], 0.0) for h in range(heads)], 0).astype(jnp.bfloat16)
            acc = acc + lax.dot_general(left, hot_lo, (((1,),(1,)),((),())), preferred_element_type=jnp.float32)
        return acc
    out_ref[...] = lax.fori_loop(0, rows // 8, step, jnp.zeros(out_ref.shape, jnp.float32))

def bucket_sum(summed, index, reach):
    heads = summed.shape[0]
    out = pl.pallas_call(bucket_kernel,
        out_shape=jax.ShapeDtypeStruct((heads * (reach // LOW), LOW), jnp.float32),
        cost_estimate=LIGHT, compiler_params=VM)(summed, index)
    return out.reshape(heads, reach)
QUARTER=64
NT=(((1,),(1,)),((),()))
TN=(((0,),(0,)),((),()))
def dot(a,b,dims=(((1,),(0,)),((),()))):
    return lax.dot_general(a,b,dims,preferred_element_type=jnp.float32)

def row_start(position, part):
    share = part // FRAMES
    return pl.multiple_of((position ^ share) * (FRAMES * QUARTER) + (part % FRAMES) * QUARTER, QUARTER)

def load_windows(ref, position, kind, step, cols):
    if kind == 0:
        return [jnp.concatenate([ref[pl.ds(row_start(position, 4 * step + t), QUARTER), cols] for t in range(4)], 0)]
    both = [[], []]
    for f in range(FRAMES):
        for k in range(2):
            block = ref[pl.ds(row_start(position, 4 * f + 2 * step + k), QUARTER), cols].astype(jnp.float32)
            block = block.reshape(4, 2, 8, block.shape[-1])
            for c in range(2):
                both[c].append(block[:, c].reshape(32, block.shape[-1]))
    return [jnp.concatenate(b, 0).astype(jnp.bfloat16) for b in both]

def store_windows(ref, position, kind, step, cols, values):
    if kind == 0:
        for t in range(4):
            ref[pl.ds(row_start(position, 4 * step + t), QUARTER), cols] = values[0][t * QUARTER:(t + 1) * QUARTER].astype(ref.dtype)
        return
    for f in range(FRAMES):
        for k in range(2):
            at = (2 * f + k) * 32
            block = jnp.stack([v[at:at + 32].reshape(4, 8, v.shape[-1]) for v in values], axis=1)
            ref[pl.ds(row_start(position, 4 * f + 2 * step + k), QUARTER), cols] = block.reshape(QUARTER, block.shape[-1]).astype(ref.dtype)

def self_forward_kernel(kind, position_ref, qkv_ref, bias_ref, out_ref, probs_ref):
    step = pl.program_id(0)
    position = position_ref[0]
    width = out_ref.shape[1]
    heads = width // HD
    size = probs_ref.shape[2]
    q, k, v = [load_windows(qkv_ref, position, kind, step, pl.ds(j * width, width)) for j in range(3)]
    lane = lax.broadcasted_iota(jnp.int32, (size, width), 1) // HD
    results = []
    for w in range(len(q)):
        total = jnp.zeros((size, width), jnp.float32)
        scaled = q[w] * jnp.bfloat16(HD ** -0.5)
        for h in range(heads):
            s = dot(jnp.where(lane == h, scaled, jnp.bfloat16(0)), k[w], NT) + bias_ref[h, :, pl.ds(0, size)].astype(jnp.float32)
            s = s - jnp.max(s, axis=-1, keepdims=True)
            e = jnp.exp(s)
            p = (e * (1.0 / jnp.sum(e, axis=-1, keepdims=True))).astype(jnp.bfloat16)
            probs_ref[w, h] = p
            total = total + dot(p, jnp.where(lane == h, v[w], jnp.bfloat16(0)))
        results.append(total)
    store_windows(out_ref, position, kind, step, pl.ds(0, width), results)

def self_forward_call(kind, position, qkv, bias):
    rows, width = qkv.shape
    width //= 3
    heads = width // HD
    size = 256 if kind == 0 else 320
    per = 1 if kind == 0 else 2
    steps = rows // size // per
    return pl.pallas_call(
        functools.partial(self_forward_kernel, kind),
        out_shape=(jax.ShapeDtypeStruct((rows, width), jnp.bfloat16),
                   jax.ShapeDtypeStruct((steps * per, heads, size, size), jnp.bfloat16)),
        grid_spec=pltpu.PrefetchScalarGridSpec(
            num_scalar_prefetch=1, grid=(steps,),
            in_specs=[pl.BlockSpec(qkv.shape, lambda i, p: (0, 0)),
                      pl.BlockSpec(bias.shape, lambda i, p: (0, 0, 0))],
            out_specs=[pl.BlockSpec((rows, width), lambda i, p: (0, 0)),
                       pl.BlockSpec((per, heads, size, size), lambda i, p: (i, 0, 0, 0))]),
        cost_estimate=LIGHT, compiler_params=VM,
        name="self_forward",
    )(position, qkv, bias)

def self_backward_kernel(kind, position_ref, qkv_ref, probs_ref, grad_ref, dqkv_ref, sum_ref):
    step = pl.program_id(0)
    position = position_ref[0]
    width = grad_ref.shape[1]
    heads = width // HD
    size = probs_ref.shape[2]
    q, k, v = [load_windows(qkv_ref, position, kind, step, pl.ds(j * width, width)) for j in range(3)]
    g = load_windows(grad_ref, position, kind, step, pl.ds(0, width))
    lane = lax.broadcasted_iota(jnp.int32, (size, width), 1) // HD
    zero = jnp.bfloat16(0)
    @pl.when(step == 0)
    def _():
        sum_ref[...] = jnp.zeros_like(sum_ref)
    outs = [[], [], []]
    for w in range(len(q)):
        dq = jnp.zeros((size, width), jnp.float32)
        dk = jnp.zeros((size, width), jnp.float32)
        dv = jnp.zeros((size, width), jnp.float32)
        scaled = q[w] * jnp.bfloat16(HD ** -0.5)
        kscaled = k[w] * jnp.bfloat16(HD ** -0.5)
        for h in range(heads):
            mine = lane == h
            gh = jnp.where(mine, g[w], zero)
            p16 = probs_ref[w, h]
            p = p16.astype(jnp.float32)
            dp = dot(gh, v[w], NT)
            ds = p * (dp - jnp.sum(p * dp, axis=-1, keepdims=True))
            ds16 = ds.astype(jnp.bfloat16)
            sum_ref[h] += ds16.astype(jnp.float32)
            dq = dq + dot(ds16, jnp.where(mine, kscaled, zero))
            dk = dk + dot(ds16, jnp.where(mine, scaled, zero), TN)
            dv = dv + dot(p16, gh, TN)
        outs[0].append(dq); outs[1].append(dk); outs[2].append(dv)
    for j in range(3):
        store_windows(dqkv_ref, position, kind, step, pl.ds(j * width, width), outs[j])

def self_backward_call(kind, position, qkv, probs, grad):
    rows, width = grad.shape
    heads = width // HD
    size = probs.shape[2]
    per = 1 if kind == 0 else 2
    steps = rows // size // per
    return pl.pallas_call(
        functools.partial(self_backward_kernel, kind),
        out_shape=(jax.ShapeDtypeStruct(qkv.shape, jnp.bfloat16),
                   jax.ShapeDtypeStruct((heads, size, size), jnp.float32)),
        grid_spec=pltpu.PrefetchScalarGridSpec(
            num_scalar_prefetch=1, grid=(steps,),
            in_specs=[pl.BlockSpec(qkv.shape, lambda i, p: (0, 0)),
                      pl.BlockSpec((per, heads, size, size), lambda i, p: (i, 0, 0, 0)),
                      pl.BlockSpec(grad.shape, lambda i, p: (0, 0))],
            out_specs=[pl.BlockSpec(qkv.shape, lambda i, p: (0, 0)),
                       pl.BlockSpec((heads, size, size), lambda i, p: (0, 0, 0))]),
        cost_estimate=LIGHT, compiler_params=VM,
        name="self_backward",
    )(position, qkv, probs, grad)
PAD=128

def cross_forward_kernel(q_ref, k_ref, v_ref, bias_ref, out_ref, probs_ref):
    rows = q_ref.shape[0]
    first = lax.broadcasted_iota(jnp.int32, (rows, LANES), 1) < HD
    vfirst = lax.broadcasted_iota(jnp.int32, (PAD, LANES), 1) < HD
    zero = jnp.bfloat16(0)
    q = q_ref[...] * jnp.bfloat16(HD ** -0.5)
    total = jnp.zeros((rows, LANES), jnp.float32)
    for half in range(2):
        s = dot(jnp.where(first == (half == 0), q, zero), k_ref[...], NT) + bias_ref[...]
        s = s - jnp.max(s, axis=-1, keepdims=True)
        e = jnp.exp(s)
        p = (e * (1.0 / jnp.sum(e, axis=-1, keepdims=True))).astype(jnp.bfloat16)
        probs_ref[half] = p
        total = total + dot(p, jnp.where(vfirst == (half == 0), v_ref[...], zero))
    out_ref[...] = total.astype(jnp.bfloat16)

def cross_forward_call(q, k, v, bias):
    rows, width = q.shape
    pairs = width // LANES
    col = lambda i: (0, i)
    return pl.pallas_call(
        cross_forward_kernel, grid=(pairs,),
        in_specs=[pl.BlockSpec((rows, LANES), col), pl.BlockSpec((PAD, LANES), col), pl.BlockSpec((PAD, LANES), col),
                  pl.BlockSpec((1, PAD), lambda i: (0, 0))],
        out_specs=[pl.BlockSpec((rows, LANES), col), pl.BlockSpec((2, rows, PAD), lambda i: (i, 0, 0))],
        out_shape=[jax.ShapeDtypeStruct((rows, width), jnp.bfloat16), jax.ShapeDtypeStruct((2 * pairs, rows, PAD), jnp.bfloat16)],
        cost_estimate=LIGHT, compiler_params=VM, name="cross_forward")(q, k, v, bias)

def cross_backward_kernel(q_ref, k_ref, v_ref, probs_ref, grad_ref, dq_ref, dk_ref, dv_ref):
    rows = q_ref.shape[0]
    first = lax.broadcasted_iota(jnp.int32, (rows, LANES), 1) < HD
    kfirst = lax.broadcasted_iota(jnp.int32, (PAD, LANES), 1) < HD
    zero = jnp.bfloat16(0)
    q = q_ref[...] * jnp.bfloat16(HD ** -0.5)
    k = k_ref[...] * jnp.bfloat16(HD ** -0.5)
    dq = jnp.zeros((rows, LANES), jnp.float32)
    dk = jnp.zeros((PAD, LANES), jnp.float32)
    dv = jnp.zeros((PAD, LANES), jnp.float32)
    for half in range(2):
        mine = first == (half == 0)
        g = jnp.where(mine, grad_ref[...], zero)
        p16 = probs_ref[half]
        p = p16.astype(jnp.float32)
        dp = dot(g, v_ref[...], NT)
        ds = (p * (dp - jnp.sum(p * dp, axis=-1, keepdims=True))).astype(jnp.bfloat16)
        dq = dq + dot(ds, jnp.where(kfirst == (half == 0), k, zero))
        dk = dk + dot(ds, jnp.where(mine, q, zero), TN)
        dv = dv + dot(p16, g, TN)
    dq_ref[...] = dq.astype(jnp.bfloat16)
    dk_ref[...] = dk
    dv_ref[...] = dv

def cross_backward_call(q, k, v, probs, grad):
    rows, width = q.shape
    pairs = width // LANES
    col = lambda i: (0, i)
    tok = pl.BlockSpec((rows, LANES), col); txt = pl.BlockSpec((PAD, LANES), col)
    return pl.pallas_call(
        cross_backward_kernel, grid=(pairs,),
        in_specs=[tok, txt, txt, pl.BlockSpec((2, rows, PAD), lambda i: (i, 0, 0)), tok],
        out_specs=[tok, txt, txt],
        out_shape=[jax.ShapeDtypeStruct((rows, width), jnp.bfloat16), jax.ShapeDtypeStruct((PAD, width), jnp.float32), jax.ShapeDtypeStruct((PAD, width), jnp.float32)],
        cost_estimate=LIGHT, compiler_params=VM, name="cross_backward")(q, k, v, probs, grad)


def gelu_slope(u):
    inner = 0.7978845608028654 * (u + 0.044715 * u * u * u)
    th = jnp.tanh(inner)
    return 0.5 * (1.0 + th) + 0.5 * u * (1.0 - th * th) * (0.7978845608028654 * (1.0 + 3.0 * 0.044715 * u * u))


FF_TILE = 256


def feed_forward_kernel(a_ref, b_ref, up_ref, down_ref, hidden_ref, active_ref, pa_ref, pb_ref):
    rows = a_ref.shape[0]
    units = up_ref.shape[1]
    for at, ref in ((0, a_ref), (rows, b_ref)):
        for t in range(0, units, FF_TILE):
            u = dot(ref[...], up_ref[:, t : t + FF_TILE])
            hidden_ref[pl.ds(at, rows), t : t + FF_TILE] = u.astype(jnp.bfloat16)
            active_ref[pl.ds(at, rows), t : t + FF_TILE] = jax.nn.gelu(u, approximate=True).astype(jnp.bfloat16)
    pa_ref[...] = dot(active_ref[pl.ds(0, rows), :], down_ref[...], NT).astype(jnp.bfloat16)
    pb_ref[...] = dot(active_ref[pl.ds(rows, rows), :], down_ref[...], NT).astype(jnp.bfloat16)


def half_columns(weights):
    units = weights.shape[1] // 2
    return [pl.BlockSpec((weights.shape[0], units), lambda i: (0, 0)), pl.BlockSpec((weights.shape[0], units), lambda i: (0, 1))]


def feed_forward_call(a, b, weights):
    rows, width = a.shape
    units = weights.shape[1] // 2
    whole = pl.BlockSpec((rows, width), lambda i: (0, 0))
    wide = pl.BlockSpec((2 * rows, units), lambda i: (0, 0))
    return pl.pallas_call(
        feed_forward_kernel,
        grid=(1,),
        in_specs=[whole, whole] + half_columns(weights),
        out_specs=[wide, wide, whole, whole],
        out_shape=[
            jax.ShapeDtypeStruct((2 * rows, units), jnp.bfloat16),
            jax.ShapeDtypeStruct((2 * rows, units), jnp.bfloat16),
            jax.ShapeDtypeStruct((rows, width), jnp.bfloat16),
            jax.ShapeDtypeStruct((rows, width), jnp.bfloat16),
        ],
        cost_estimate=LIGHT, compiler_params=VM,
        name="feed_forward",
    )(a, b, weights, weights)


def feed_backward_kernel(a_ref, b_ref, hidden_ref, up_ref, down_ref, grad_ref, pa_ref, pb_ref):
    rows = a_ref.shape[0]
    units = up_ref.shape[1]
    for at, ref in ((0, a_ref), (rows, b_ref)):
        for t in range(0, units, FF_TILE):
            slope = gelu_slope(hidden_ref[pl.ds(at, rows), t : t + FF_TILE].astype(jnp.float32))
            grad_ref[pl.ds(at, rows), t : t + FF_TILE] = (dot(ref[...], down_ref[:, t : t + FF_TILE]) * slope).astype(jnp.bfloat16)
    pa_ref[...] = dot(grad_ref[pl.ds(0, rows), :], up_ref[...], NT).astype(jnp.bfloat16)
    pb_ref[...] = dot(grad_ref[pl.ds(rows, rows), :], up_ref[...], NT).astype(jnp.bfloat16)


def feed_backward_call(a, b, hidden, weights):
    rows, width = a.shape
    units = weights.shape[1] // 2
    whole = pl.BlockSpec((rows, width), lambda i: (0, 0))
    wide = pl.BlockSpec((2 * rows, units), lambda i: (0, 0))
    return pl.pallas_call(
        feed_backward_kernel,
        grid=(1,),
        in_specs=[whole, whole, wide] + half_columns(weights),
        out_specs=[wide, whole, whole],
        out_shape=[
            jax.ShapeDtypeStruct((2 * rows, units), jnp.bfloat16),
            jax.ShapeDtypeStruct((rows, width), jnp.bfloat16),
            jax.ShapeDtypeStruct((rows, width), jnp.bfloat16),
        ],
        cost_estimate=LIGHT, compiler_params=VM,
        name="feed_backward",
    )(a, b, hidden, weights, weights)


def weight_grad_kernel(counts, splits, order_ref, *refs):
    step = pl.program_id(0)
    (ln_a, rn_a), (ln_b, rn_b) = splits
    left = (refs[:ln_a], refs[ln_a : ln_a + ln_b])
    refs = refs[ln_a + ln_b :]
    right = (refs[:rn_a], refs[rn_a : rn_a + rn_b])
    out_ref, turned_ref = refs[rn_a + rn_b :]
    blocks = order_ref.shape[0]
    width = turned_ref.shape[0] // blocks

    def turn(pieces):
        at = 0
        for ref in pieces:
            rows = ref.shape[0]
            for p in range(blocks):
                column = pl.multiple_of(order_ref[p] * width, width)
                turned_ref[pl.ds(p * width, width), pl.ds(at, rows)] = ref[:, pl.ds(column, width)].T
            at += rows

    def product(pieces):
        at = 0
        total = None
        for ref in pieces:
            rows = ref.shape[0]
            part = dot(turned_ref[:, pl.ds(at, rows)], ref[...])
            total = part if total is None else total + part
            at += rows
        out_ref[...] = total.astype(jnp.bfloat16).reshape(out_ref.shape)

    for n, begin in ((0, 0), (1, counts[0])):

        @pl.when(step == begin)
        def _():
            turn(left[n])

        @pl.when(jnp.logical_and(step >= begin, step < begin + counts[n]))
        def _():
            product(right[n])


GRAD_TILE = 256


def weight_grad_call(order, lefts, rights, out_shape, out_map):
    counts = [sum_cols // GRAD_TILE for sum_cols in (rights[0][0][0].shape[1], rights[1][0][0].shape[1])]
    splits = [(len(lefts[n]), len(rights[n])) for n in range(2)]
    in_specs, operands = [], []
    for n in range(2):
        for item in lefts[n]:
            in_specs.append(pl.BlockSpec(item.shape, lambda i, o: (0, 0)))
            operands.append(item)
    for n in range(2):
        begin, count = (0, counts[0])[n], counts[n]
        for item, rows, block in rights[n]:
            in_specs.append(
                pl.BlockSpec(
                    (rows, GRAD_TILE),
                    lambda i, o, begin=begin, count=count, block=block: (block, jnp.clip(i - begin, 0, count - 1)),
                )
            )
            operands.append(item)
    tokens = sum(item.shape[0] for item in lefts[0])
    width = lefts[0][0].shape[1]
    tiles = counts[0] + counts[1]
    block_shape = out_shape[:-1] + (GRAD_TILE,) if len(out_shape) == 2 else (1, out_shape[1], GRAD_TILE)
    return pl.pallas_call(
        functools.partial(weight_grad_kernel, counts, splits),
        grid_spec=pltpu.PrefetchScalarGridSpec(
            num_scalar_prefetch=1,
            grid=(tiles,),
            in_specs=in_specs,
            out_specs=pl.BlockSpec(block_shape, out_map),
            scratch_shapes=[pltpu.VMEM((width, tokens), jnp.bfloat16)],
        ),
        out_shape=jax.ShapeDtypeStruct(out_shape, jnp.bfloat16),
        cost_estimate=LIGHT, compiler_params=VM,
        name="weight_grad",
    )(order, *operands)


def regroup(columns, outer, inner):
    pieces = []
    for i in range(inner):
        for o in range(outer):
            at = (o * inner + i) * HD
            pieces.append(columns[:, at : at + HD])
    return jnp.concatenate(pieces, axis=1)


def prepare_kernel(qkv_ref, out_ref, cq_ref, ckv_ref, cout_ref, up_ref, down_ref, self_ref, pair_ref, text_ref, feed_ref):
    wide = cq_ref.shape[2]
    heads = wide // HD
    units = up_ref.shape[2]
    self_ref[0, :, : 3 * wide] = regroup(qkv_ref[0], heads, 3).astype(jnp.bfloat16)
    self_ref[0, :, 3 * wide :] = out_ref[0].T.astype(jnp.bfloat16)
    pair_ref[0, :, :wide] = cq_ref[0].astype(jnp.bfloat16)
    pair_ref[0, :, wide:] = cout_ref[0].T.astype(jnp.bfloat16)
    text_ref[0] = regroup(ckv_ref[0], heads, 2).astype(jnp.bfloat16)
    feed_ref[0, :, :units] = up_ref[0].astype(jnp.bfloat16)
    feed_ref[0, :, units:] = down_ref[0].T.astype(jnp.bfloat16)


def layer_block(shape):
    return pl.BlockSpec((1,) + tuple(shape[1:]), lambda i: (i, 0, 0))


def prepare_call(masters):
    layers, block, wide = masters[2].shape
    units = masters[5].shape[2]
    shapes = [(layers, block, 4 * wide), (layers, block, 2 * wide), (layers, block, 2 * wide), (layers, block, 2 * units)]
    return pl.pallas_call(
        prepare_kernel,
        grid=(layers,),
        in_specs=[layer_block(item.shape) for item in masters],
        out_specs=[layer_block(shape) for shape in shapes],
        out_shape=[jax.ShapeDtypeStruct(shape, jnp.bfloat16) for shape in shapes],
        cost_estimate=LIGHT, compiler_params=VM,
        name="prepare",
    )(*masters)


def adam_math(master, first, second, grad, rate):
    first_new = BETA_ONE * first + (1.0 - BETA_ONE) * grad
    second_new = BETA_TWO * second + (1.0 - BETA_TWO) * grad * grad
    step_size = (
        first_new / (1.0 - BETA_ONE**STEP) / (jnp.sqrt(second_new / (1.0 - BETA_TWO**STEP)) + ADAM_EPS)
    )
    master_new = master - rate * (step_size + DECAY_RATE * master)
    return (master_new, first_new, second_new, master_new.astype(jnp.bfloat16))


def adam_kernel(plans, n_grads, *refs):
    layer = pl.program_id(0)
    count = len(plans)
    sources = [jnp.where(layer == 0, refs[2 * n][...], refs[2 * n + 1][...]).astype(jnp.float32) for n in range(n_grads)]
    refs = refs[2 * n_grads :]
    for n, (source, begin, width, kind, rate) in enumerate(plans):
        master, first, second = [refs[3 * n + m][0] for m in range(3)]
        outs = refs[3 * count + 4 * n : 3 * count + 4 * n + 4]
        grad = sources[source][:, begin : begin + width]
        if kind == "turn":
            grad = grad.T
        elif kind:
            grad = regroup(grad, kind, width // (kind * HD))
        for ref, value in zip(outs, adam_math(master, first, second, grad, rate)):
            ref[0] = value


def adam_call(plans, grads, states):
    in_specs, operands, out_specs, out_shape = [], [], [], []
    for pair in grads:
        for item in pair:
            in_specs.append(pl.BlockSpec(item.shape, lambda i: (0, 0)))
            operands.append(item)
    for group in states:
        for item in group:
            in_specs.append(layer_block(item.shape))
            operands.append(item)
        shape = group[0].shape
        for dtype in (jnp.float32, jnp.float32, jnp.float32, jnp.bfloat16):
            out_specs.append(layer_block(shape))
            out_shape.append(jax.ShapeDtypeStruct(shape, dtype))
    result = pl.pallas_call(
        functools.partial(adam_kernel, plans, len(grads)),
        grid=(states[0][0].shape[0],),
        in_specs=in_specs,
        out_specs=out_specs,
        out_shape=out_shape,
        cost_estimate=LIGHT, compiler_params=VM,
        name="adam",
    )(*operands)
    return [result[4 * n : 4 * n + 4] for n in range(len(states))]


def exchange(value, axis, bit, size):
    return lax.ppermute(value, axis, [(i, i ^ bit) for i in range(size)])


def after(value, *anchors):
    return lax.optimization_barrier((value, anchors))[0]


def share_rows(own, meanwhile):
    far = exchange(own, "mp", 2, 4)
    near = exchange(own, "mp", 1, 4)
    done = meanwhile(own, near)
    far = after(far, done)
    return (own, near, far, exchange(far, "mp", 1, 4)), done


def share_small(own):
    far = exchange(own, "mp", 2, 4)
    near = exchange(own, "mp", 1, 4)
    return (own, near, far, exchange(far, "mp", 1, 4))


def collect_parts(parts, meanwhile=None):
    beside = exchange(parts[3], "mp", 1, 4)
    crossing = narrow(parts[2].astype(jnp.float32) + beside.astype(jnp.float32))
    far = exchange(crossing, "mp", 2, 4)
    near_part, done = parts[1], None
    if meanwhile is not None:
        done = meanwhile(crossing)
        far = after(far, done)
    near = exchange(after(parts[1], crossing), "mp", 1, 4)
    total = parts[0].astype(jnp.float32) + near.astype(jnp.float32) + far.astype(jnp.float32)
    return total if meanwhile is None else (total, done)


def bits_of(size):
    return [1 << n for n in range(size.bit_length() - 1)]


class Flow:
    def __init__(self, stages):
        self.stages = stages
        self.result = None
        self.pending = next(stages)

    def take(self, value):
        try:
            self.pending = self.stages.send(value)
        except StopIteration as stop:
            self.pending = None
            self.result = stop.value

    def finish(self):
        while self.pending is not None:
            self.take(self.pending)
        return self.result


def tick(anchor, *flows):
    flows = [flow for flow in flows if flow is not None and flow.pending is not None]
    if not flows:
        return anchor
    anchor, values = lax.optimization_barrier((anchor, [flow.pending for flow in flows]))
    for flow, value in zip(flows, values):
        flow.take(value)
    return anchor


def block_order(size):
    me = lax.axis_index("dp").astype(jnp.int32)
    if (D // size) % LANES:
        return jnp.arange(D // LANES, dtype=jnp.int32), False
    order = [0]
    for bit in reversed(bits_of(size)):
        order = order + [item | bit for item in order]
    return jnp.array(order, jnp.int32) ^ me, True


def halving(total, size, ordered):
    me = lax.axis_index("dp")
    rows, width = total.shape
    if ordered:
        for bit in bits_of(size):
            half = total.shape[0] // 2
            got = yield exchange(narrow(total[half:]), "dp", bit, size)
            total = total[:half].astype(jnp.float32) + got.astype(jnp.float32)
            if bit * 2 < size:
                total = narrow(total)
        return total
    blocks = total.reshape(size, rows // size, width)
    for n, bit in enumerate(bits_of(size)):
        pairs = blocks.reshape(blocks.shape[0] // 2, 2, rows // size, width)
        mine = (me >> n) & 1
        keep = lax.dynamic_index_in_dim(pairs, mine, 1, keepdims=False)
        send = lax.dynamic_index_in_dim(pairs, 1 - mine, 1, keepdims=False)
        got = yield exchange(send, "dp", bit, size)
        total = keep.astype(jnp.float32) + got.astype(jnp.float32)
        blocks = narrow(total)
    return total.reshape(rows // size, width)


def doubling(own, size):
    me = lax.axis_index("dp")
    rows, width = own.shape
    own = own[None, None]
    for n, bit in reversed(list(enumerate(bits_of(size)))):
        got = yield exchange(own, "dp", bit, size)
        own = jnp.where(((me >> n) & 1) == 0, jnp.concatenate([own, got], axis=1), jnp.concatenate([got, own], axis=1))
        own = own.reshape(own.shape[0] * 2, 1, rows, width)
    return own.reshape(size * rows, width)


def collecting(parts):
    beside, near = yield (exchange(parts[3], "mp", 1, 4), exchange(parts[1], "mp", 1, 4))
    crossing = narrow(parts[2].astype(jnp.float32) + beside.astype(jnp.float32))
    far = yield exchange(crossing, "mp", 2, 4)
    return parts[0].astype(jnp.float32) + near.astype(jnp.float32) + far.astype(jnp.float32)


def collect_then_gather(parts, size):
    total = yield from collecting(parts)
    total = narrow(total)
    got = yield exchange(total, "dp", 1, size)
    slots = narrow(total.astype(jnp.float32) + got.astype(jnp.float32))[None, None]
    me = lax.axis_index("dp")
    for n, bit in reversed(list(enumerate(bits_of(size)))[1:]):
        got = yield exchange(slots, "dp", bit, size)
        slots = jnp.where(((me >> n) & 1) == 0, jnp.concatenate([slots, got], axis=1), jnp.concatenate([got, slots], axis=1))
        slots = slots.reshape((slots.shape[0] * 2, 1) + slots.shape[2:])
    return slots[:, 0]


def pair_up(slots):
    got = yield (exchange(slots[1], "mp", 1, 4), exchange(slots[3], "mp", 1, 4))
    return jnp.concatenate([narrow(slots[2 * k].astype(jnp.float32) + got[k].astype(jnp.float32)) for k in range(2)], axis=1)


def halve_then_cross(total, size, ordered, width):
    total = yield from halving(total, size, ordered)
    got = yield exchange(narrow(total[:, width : 2 * width]), "mp", 2, 4)
    return total[:, :width] + got.astype(jnp.float32), total[:, 2 * width :]


def gathering(own, size):
    me = lax.axis_index("dp")
    slots = own[None]
    for n, bit in enumerate(bits_of(size)):
        got = yield exchange(slots, "dp", bit, size)
        slots = jnp.where(((me >> n) & 1) == 0, jnp.concatenate([slots, got]), jnp.concatenate([got, slots]))
    return slots


def gather_small(own, size):
    return Flow(gathering(own, size)).finish()


def modulate(latent, scale, shift):
    normed, inverse = layer_norm(latent)
    return (normed * (1.0 + scale) + shift).astype(jnp.bfloat16)


def narrow(value):
    return value.astype(jnp.bfloat16)


def mm(a, b, dims=(((1,), (0,)), ((), ()))):
    return lax.dot_general(a, b, dims, preferred_element_type=jnp.float32)


def body(*args):
    (latents, cotangent, text_embed, text_mask, band_ids, rel_index_s, rel_index_t, modulation) = args[:8]
    masters, firsts, seconds = args[8:17], args[17:26], args[26:35]
    groups = lax.axis_size("dp")
    rates = learning_rates()
    own = latents.shape[0]
    half = 2 * own
    wide = masters[1].shape[1]
    index_tables = (rel_index_s, rel_index_t)
    reaches = (masters[7].shape[1] * groups, masters[8].shape[1] * groups)

    order, ordered = block_order(groups)

    block = D // groups
    self_shards, pair_shards, text_shards, feed_shards = prepare_call(masters[:7])
    pair_shards = pair_shards.reshape(LAYERS * block, 2 * wide)
    other = exchange(pair_shards, "mp", 2, 4)

    def cross_shard(layer):
        rows = slice(layer * block, (layer + 1) * block)
        return [pair_shards[rows], other[rows], text_shards[layer]]

    self_flow_0 = Flow(doubling(self_shards[0], groups))

    position = lax.axis_index("mp").astype(jnp.int32)[None]
    clip_index = lax.axis_index("dp") // 2
    text_rows = lax.dynamic_index_in_dim(text_embed, clip_index, 0, keepdims=False)
    texts = text_rows.shape[0]
    texts_pad = -(-texts // 16) * 16
    text_rows = jnp.pad(text_rows, ((0, PAD - texts), (0, 0)))
    mask_row = lax.dynamic_index_in_dim(text_mask, clip_index, 0, keepdims=False)
    column = jnp.arange(PAD, dtype=jnp.int32)
    valid = jnp.maximum(jnp.pad(mask_row, (0, PAD - texts)), (column == 0).astype(jnp.int32)).astype(jnp.float32)
    valid_bias = jnp.where(column < texts, (valid - 1.0) * 1000000000.0, -1e30)[None]
    band_now = lax.dynamic_index_in_dim(band_ids, clip_index, 0, keepdims=False)
    selector = (jnp.arange(modulation.shape[0], dtype=jnp.int32) == band_now).astype(jnp.float32)
    mod_rows = lax.dynamic_index_in_dim(modulation, band_now, 0, keepdims=False)
    text_columns = lax.dynamic_slice_in_dim(text_embed, lax.axis_index("dp") * (D // groups), D // groups, axis=2)

    tables = gather_small(jnp.concatenate([narrow(masters[7]), narrow(masters[8])], axis=1), groups)
    tables = tables.swapaxes(0, 1)
    cut = masters[7].shape[1]
    table_s = tables[:, :, :cut].reshape(tables.shape[0], -1)
    table_t = tables[:, :, cut:].reshape(tables.shape[0], -1)
    biases = (make_bias(table_s, rel_index_s), make_bias(table_t, rel_index_t))

    latent = latents
    saved = []
    weights = []
    for layer in range(LAYERS):
        base = 9 * layer
        record = {"in": latent}
        sending = modulate(latent, mod_rows[base + 1], mod_rows[base])
        if layer == 0:
            cross_start = tick(jnp.concatenate(cross_shard(0), axis=1), self_flow_0)
            cross_flow_0 = Flow(doubling(cross_start, groups))
            biases = tick(biases, self_flow_0, cross_flow_0)
            feed_start = tick(feed_shards[0], self_flow_0, cross_flow_0)
            feed_flow_0 = Flow(doubling(feed_start, groups))
            self_w = after(self_flow_0.finish(), feed_start, biases)
        else:
            self_w = self_flow_1.finish()
        w_in = self_w[:, : 3 * wide]
        rows, near_qkv = share_rows(sending, lambda one, two: (narrow(mm(one, w_in)), narrow(mm(two, w_in))))
        qkv = jnp.concatenate(near_qkv + tuple(narrow(mm(item, w_in)) for item in rows[2:]), axis=0)
        mixed, probs = self_forward_call(layer, position, qkv, biases[layer])
        w_out = self_w[:, 3 * wide :]
        project = lambda k: narrow(mm(mixed[k * own : (k + 1) * own], w_out, NT))
        p2, p3 = project(2), project(3)
        p3 = tick(p3, feed_flow_0 if layer == 0 else feed_flow_1)
        branch = collect_parts([project(0), project(1), p2, p3])
        if layer == 0:
            branch = tick(branch, feed_flow_0, cross_flow_0)
            self_flow_1 = Flow(doubling(after(self_shards[1], branch), groups))
        else:
            branch = tick(branch, feed_flow_1, cross_flow_1)
        record["self"] = (rows, qkv, probs, mixed, branch)
        latent = latent + mod_rows[base + 2] * branch
        record["mid"] = latent
        normed = modulate(latent, mod_rows[base + 4], mod_rows[base + 3])
        if layer == 0:
            cross_w = cross_flow_0.finish()
        else:
            cross_w = cross_flow_1.finish()
        keyval = share_small(narrow(mm(text_rows, cross_w[:, 4 * wide :])))
        keys = jnp.concatenate([item[:, :wide] for item in keyval], axis=1)
        values = jnp.concatenate([item[:, wide:] for item in keyval], axis=1)
        across = exchange(cross_w[:, : 4 * wide], "mp", 1, 4)
        cross_all = (cross_w[:, : 2 * wide], across[:, : 2 * wide], cross_w[:, 2 * wide : 4 * wide], across[:, 2 * wide :])
        w_cq = jnp.concatenate([item[:, :wide] for item in cross_all], axis=1)
        w_cout = jnp.concatenate([item[:, wide:] for item in cross_all], axis=1)
        queries = narrow(mm(normed, w_cq))
        mixed, probs = cross_forward_call(queries, keys, values, valid_bias)
        branch = mm(mixed, w_cout, NT)
        record["cross"] = (normed, queries, keys, values, probs, mixed, branch, w_cq, w_cout)
        latent = latent + mod_rows[base + 5] * branch
        if layer == 0:
            latent = tick(latent, self_flow_1)
        record["late"] = latent
        if layer == 0:
            feed_w = tick(feed_flow_0.finish(), self_flow_1)
            cross_flow_1 = Flow(doubling(after(jnp.concatenate(cross_shard(1), axis=1), feed_w), groups))
        else:
            feed_w = feed_flow_1.finish()
        weights.append((self_w, feed_w))
        rows, (hidden_near, active_near, p0, p1) = share_rows(
            modulate(latent, mod_rows[base + 7], mod_rows[base + 6]), lambda one, two: feed_forward_call(one, two, feed_w)
        )
        hidden_far, active_far, p2, p3 = feed_forward_call(rows[2], rows[3], feed_w)
        if layer == 0:
            p3 = tick(p3, cross_flow_1)
        branch = collect_parts([p0, p1, p2, p3])
        if layer == 0:
            branch = tick(branch, cross_flow_1, self_flow_1)
            feed_flow_1 = Flow(doubling(after(feed_shards[1], branch), groups))
        record["feed"] = (rows, (hidden_near, hidden_far), (active_near, active_far), branch)
        latent = latent + mod_rows[base + 8] * branch
        saved.append(record)

    grad_latent = cotangent
    mod_grads = [None, None]
    feed_flows, self_flows, cross_flows, tables_sent, kv_grads = [None] * 2, [None] * 2, [None] * 2, [None] * 2, [None] * 2
    kv_flow = None
    for layer in reversed(range(LAYERS)):
        self_w, feed_w = weights[layer]
        last = layer == 0
        late = None if not last else self_flows[1]
        base = 9 * layer
        record = saved[layer]
        rows, hiddens, actives, branch = record["feed"]
        gate_m = jnp.sum(grad_latent * branch, axis=0)
        grads, (dh_near, p0, p1) = share_rows(
            narrow(mod_rows[base + 8] * grad_latent), lambda one, two: feed_backward_call(one, two, hiddens[0], feed_w)
        )
        dh_far, p2, p3 = feed_backward_call(grads[2], grads[3], hiddens[1], feed_w)
        units = dh_near.shape[1]
        grad_input, feed_g = collect_parts(
            [p0, p1, p2, p3],
            lambda sent: weight_grad_call(
                order,
                (rows, grads),
                (((after(dh_near, sent), half, 0), (dh_far, half, 0)), ((actives[0], half, 0), (actives[1], half, 0))),
                (D, 2 * units),
                lambda i, o: (0, i),
            ),
        )
        feed_flows[layer] = Flow(halving(feed_g, groups, ordered))
        grad_input = tick(grad_input, late)
        normed, inverse = layer_norm(record["late"])
        grad_latent, shift_m, scale_m = modulate_back(grad_latent, grad_input, normed, inverse, mod_rows[base + 7])

        hidden, queries, keys, values, probs, mixed, branch, w_cq, w_cout = record["cross"]
        gate_c = jnp.sum(grad_latent * branch, axis=0)
        grad_rows = narrow(mod_rows[base + 5] * grad_latent)
        grad_mixed = narrow(mm(grad_rows, w_cout))
        grad_query, grad_key, grad_value = cross_backward_call(queries, keys, values, probs, grad_mixed)
        kv_grads[layer] = [
            narrow(
                jnp.concatenate(
                    [grad_key[:texts_pad, k * wide : (k + 1) * wide], grad_value[:texts_pad, k * wide : (k + 1) * wide]], axis=1
                )
            )
            for k in range(4)
        ]
        grad_input = mm(grad_query, w_cq, NT)
        normed, inverse = layer_norm(record["mid"])
        grad_latent, shift_c, scale_c = modulate_back(grad_latent, grad_input, normed, inverse, mod_rows[base + 4])
        tiles = queries.shape[1] // GRAD_TILE
        if last:
            kv_flow = Flow(
                collect_then_gather([jnp.concatenate([kv_grads[0][k], kv_grads[1][k]], axis=0) for k in range(4)], groups)
            )
        if last:
            grad_latent = tick(grad_latent, late, feed_flows[0])
        sending = narrow(mod_rows[base + 2] * grad_latent)
        w_out = self_w[:, 3 * wide :]
        grads, (cross_g, near_mixed) = share_rows(
            sending,
            lambda one, two: (
                weight_grad_call(
                    order,
                    ((after(hidden, sending),), (grad_rows,)),
                    (((grad_query, own, 0),), ((mixed, own, 0),)),
                    (tiles, D, 2 * GRAD_TILE),
                    lambda i, o: (i % tiles, 0, i // tiles),
                ),
                (narrow(mm(one, w_out)), narrow(mm(two, w_out))),
            ),
        )
        rows, qkv, probs, mixed, branch = record["self"]
        gate_a = jnp.sum(grad_latent * branch, axis=0)
        grad_mixed = jnp.concatenate(near_mixed + tuple(narrow(mm(item, w_out)) for item in grads[2:]), axis=0)
        pairing = Flow(pair_up(cross_g))
        grad_mixed = tick(grad_mixed, kv_flow, None if last else feed_flows[1])
        grad_qkv, summed = self_backward_call(layer, position, qkv, probs, grad_mixed)
        grad_qkv = tick(grad_qkv, pairing, kv_flow, late, feed_flows[layer])
        if last:
            cross_flows[0] = Flow(halve_then_cross(pairing.finish(), groups, ordered, 2 * wide))
        back = lambda k: narrow(mm(grad_qkv[k * own : (k + 1) * own], self_w[:, : 3 * wide], NT))
        p2, p3 = back(2), back(3)
        grad_input, self_g = collect_parts(
            [back(0), back(1), p2, p3],
            lambda sent: weight_grad_call(
                order,
                (rows, grads),
                (((after(grad_qkv, sent), half, 0), (grad_qkv, half, 1)), ((mixed, half, 0), (mixed, half, 1))),
                (D, 4 * wide),
                lambda i, o: (0, i),
            ),
        )
        if last:
            self_flows[0] = Flow(halving(self_g, groups, ordered))
        else:
            both = jnp.concatenate([pairing.finish(), self_g], axis=1)
            self_flows[1] = Flow(halve_then_cross(both, groups, ordered, 2 * wide))
        tables_sent[layer] = summed
        if last:
            grad_input = tick(grad_input, kv_flow, cross_flows[0], late, feed_flows[0])
        normed, inverse = layer_norm(record["in"])
        grad_latent, shift_a, scale_a = modulate_back(grad_latent, grad_input, normed, inverse, mod_rows[base + 1])
        mod_grads[layer] = [shift_a, scale_a, gate_a, shift_c, scale_c, gate_c, shift_m, scale_m, gate_m]
        if last:
            grad_latent = tick(grad_latent, kv_flow, cross_flows[0])
        else:
            grad_latent = tick(grad_latent, feed_flows[1])

    mod_local = jnp.stack(mod_grads[0] + mod_grads[1], axis=0)
    for bit in (1, 2):
        mod_local = mod_local + exchange(mod_local, "mp", bit, 4)
    grad_modulation = selector[:, None, None] * mod_local[None]
    for bit in bits_of(groups):
        grad_modulation = grad_modulation + exchange(grad_modulation, "dp", bit, groups)

    tables_sent = after(tables_sent, grad_latent)
    table_grads = [bucket_sum(tables_sent[layer], index_tables[layer], reaches[layer]) for layer in range(LAYERS)]
    table_rows = [item.reshape(item.shape[0], groups, -1).swapaxes(0, 1) for item in table_grads]
    table_rows = jnp.concatenate(table_rows, axis=2)
    me = lax.axis_index("dp")
    blocks = table_rows
    for n, bit in enumerate(bits_of(groups)):
        pairs = blocks.reshape((blocks.shape[0] // 2, 2) + blocks.shape[1:])
        mine = (me >> n) & 1
        keep = lax.dynamic_index_in_dim(pairs, mine, 1, keepdims=False)
        blocks = keep + exchange(lax.dynamic_index_in_dim(pairs, 1 - mine, 1, keepdims=False), "dp", bit, groups)
    table_sum = blocks[0]

    units = masters[5].shape[2]
    state = lambda item: (masters[item], firsts[item], seconds[item])
    updates = [None] * 9
    updates[5], updates[6] = adam_call(
        ((0, 0, units, None, rates[5]), (0, units, units, "turn", rates[6])), [[flow.finish() for flow in feed_flows]], [state(5), state(6)]
    )
    kv_all = kv_flow.finish()
    kv_sums = []
    for layer in range(LAYERS):
        grad_kv = kv_all[:, layer * texts_pad : layer * texts_pad + texts]
        kv_sums.append(
            lax.dot_general(text_columns, grad_kv, (((0, 1), (0, 1)), ((), ())), preferred_element_type=jnp.float32)
        )
    cross_1, self_1 = self_flows[1].finish()
    cross_sums = [cross_flows[0].finish()[0], cross_1]
    updates[2], updates[3], updates[4] = adam_call(
        ((0, 0, wide, None, rates[2]), (1, 0, 2 * wide, 2, rates[3]), (0, wide, wide, "turn", rates[4])),
        [cross_sums, kv_sums],
        [state(2), state(3), state(4)],
    )
    self_sums = [self_flows[0].finish(), self_1]
    updates[0], updates[1] = adam_call(
        ((0, 0, 3 * wide, 3, rates[0]), (0, 3 * wide, wide, "turn", rates[1])), [self_sums], [state(0), state(1)]
    )
    updates[7] = adam_math(masters[7], firsts[7], seconds[7], table_sum[:, :cut], rates[7])
    updates[8] = adam_math(masters[8], firsts[8], seconds[8], table_sum[:, cut:], rates[8])
    results = [latent, grad_latent, grad_modulation]
    for item in updates:
        results.extend(item)
    return tuple(results)


def solution(mesh):
    in_specs = (
        P(("dp", "mp"), None),
        P(("dp", "mp"), None),
        P(),
        P(),
        P(),
        P(),
        P(),
        P(),
        P(None, "dp", "mp"),
        P(None, "mp", "dp"),
        P(None, "dp", "mp"),
        P(None, "dp", "mp"),
        P(None, "mp", "dp"),
        P(None, "dp", "mp"),
        P(None, "mp", "dp"),
        P("mp", "dp"),
        P("mp", "dp"),
        P(None, "dp", "mp"),
        P(None, "mp", "dp"),
        P(None, "dp", "mp"),
        P(None, "dp", "mp"),
        P(None, "mp", "dp"),
        P(None, "dp", "mp"),
        P(None, "mp", "dp"),
        P("mp", "dp"),
        P("mp", "dp"),
        P(None, "dp", "mp"),
        P(None, "mp", "dp"),
        P(None, "dp", "mp"),
        P(None, "dp", "mp"),
        P(None, "mp", "dp"),
        P(None, "dp", "mp"),
        P(None, "mp", "dp"),
        P("mp", "dp"),
        P("mp", "dp"),
    )
    out_specs = (
        P(("dp", "mp"), None),
        P(("dp", "mp"), None),
        P(),
        P(None, "dp", "mp"),
        P(None, "dp", "mp"),
        P(None, "dp", "mp"),
        P(None, "dp", "mp"),
        P(None, "mp", "dp"),
        P(None, "mp", "dp"),
        P(None, "mp", "dp"),
        P(None, "mp", "dp"),
        P(None, "dp", "mp"),
        P(None, "dp", "mp"),
        P(None, "dp", "mp"),
        P(None, "dp", "mp"),
        P(None, "dp", "mp"),
        P(None, "dp", "mp"),
        P(None, "dp", "mp"),
        P(None, "dp", "mp"),
        P(None, "mp", "dp"),
        P(None, "mp", "dp"),
        P(None, "mp", "dp"),
        P(None, "mp", "dp"),
        P(None, "dp", "mp"),
        P(None, "dp", "mp"),
        P(None, "dp", "mp"),
        P(None, "dp", "mp"),
        P(None, "mp", "dp"),
        P(None, "mp", "dp"),
        P(None, "mp", "dp"),
        P(None, "mp", "dp"),
        P("mp", "dp"),
        P("mp", "dp"),
        P("mp", "dp"),
        P("mp", "dp"),
        P("mp", "dp"),
        P("mp", "dp"),
        P("mp", "dp"),
        P("mp", "dp"),
    )
    return jax.shard_map(body, mesh=mesh, in_specs=in_specs, out_specs=out_specs, check_vma=False)
```

```python
import functools

import jax
import jax.numpy as jnp
from jax import lax
from jax.experimental import pallas as pl
from jax.experimental.pallas import tpu as pltpu
from jax.sharding import PartitionSpec as P

D = 1024
HD = 64
FF = 4096
FRAMES = 5
LAYERS = 2
STEP = 10
LANES = 128

BETA_ONE = 0.9
BETA_TWO = 0.95
ADAM_EPS = 1e-08
DECAY_RATE = 0.1


def learning_rates():
    inverse_root = D ** (-0.5)
    return (
        1.5 * inverse_root,
        6.0 * inverse_root,
        1.5 * inverse_root,
        1.5 * inverse_root,
        4.2 * inverse_root,
        1.5 * inverse_root,
        1.5 * FF ** (-0.5),
        1.5,
        1.5,
    )


def layer_norm(tensor):
    center = tensor - jnp.mean(tensor, axis=-1, keepdims=True)
    inverse = lax.rsqrt(jnp.mean(center * center, axis=-1, keepdims=True) + 1e-06)
    return (center * inverse, inverse)


def norm_back(grad_norm, normed, inverse):
    return inverse * (
        grad_norm
        - jnp.mean(grad_norm, axis=-1, keepdims=True)
        - normed * jnp.mean(grad_norm * normed, axis=-1, keepdims=True)
    )


def modulate_back(grad_latent, grad_input, normed, inverse, scaling):
    grad_norm = grad_input * (1.0 + scaling)
    return (
        grad_latent + norm_back(grad_norm, normed, inverse),
        jnp.sum(grad_input, axis=0),
        jnp.sum(grad_input * normed, axis=0),
    )


VM = pltpu.CompilerParams(vmem_limit_bytes=56 * 1024 * 1024)


def cost(microseconds):
    return pl.CostEstimate(flops=int(microseconds * 5e8), bytes_accessed=int(microseconds * 1.5e6), transcendentals=0)


def bias_kernel(table_ref, index_ref, out_ref):
    heads, groups, _ = table_ref.shape
    rows, cols = index_ref.shape
    def step(i, carry):
        r0 = pl.multiple_of(i * 16, 16)
        for c in range(cols // LANES):
            parts = [[] for _ in range(heads)]
            for half in range(2):
                idx = index_ref[pl.ds(r0 + half * 8, 8), pl.ds(c * LANES, LANES)]
                lo = idx & (LANES - 1)
                hi = idx >> 7
                for h in range(heads):
                    acc = jnp.zeros((8, LANES), jnp.float32)
                    for g in range(groups):
                        row = jnp.broadcast_to(table_ref[h, pl.ds(g, 1), :], (8, LANES))
                        val = jnp.take_along_axis(row, lo, axis=1, mode="promise_in_bounds")
                        acc = jnp.where(hi == g, val, acc)
                    parts[h].append(acc)
            for h in range(heads):
                out_ref[h, pl.ds(r0, 16), pl.ds(c * LANES, LANES)] = jnp.concatenate(parts[h], 0).astype(jnp.bfloat16)
        return carry
    lax.fori_loop(0, rows // 16, step, 0)

def make_bias(table, index):
    heads, reach = table.shape
    n = index.shape[0]
    pad = -n % LANES
    index = jnp.pad(index, ((0, 0), (0, pad)))
    return pl.pallas_call(bias_kernel,
        out_shape=jax.ShapeDtypeStruct((heads, n, n + pad), jnp.bfloat16),
        cost_estimate=cost(6), compiler_params=VM)(table.astype(jnp.float32).reshape(heads, reach // LANES, LANES), index)

LOW=64
def bucket_kernel(sum_ref, index_ref, out_ref):
    heads, rows, cols = sum_ref.shape
    high = out_ref.shape[0] // heads
    out_ref[...] = jnp.zeros_like(out_ref)
    hi_iota = lax.broadcasted_iota(jnp.int32, (high, cols), 0)
    lo_iota = lax.broadcasted_iota(jnp.int32, (LOW, cols), 0)
    def step(i, acc):
        r0 = pl.multiple_of(i * 8, 8)
        idx8 = index_ref[pl.ds(r0, 8), :]
        s8 = [sum_ref[h, pl.ds(r0, 8), :] for h in range(heads)]
        for r in range(8):
            idx = idx8[r:r+1]
            hot_hi = hi_iota == (idx >> 6)
            hot_lo = jnp.where(lo_iota == (idx & (LOW-1)), 1.0, 0.0).astype(jnp.bfloat16)
            left = jnp.concatenate([jnp.where(hot_hi, s8[h][r:r+1], 0.0) for h in range(heads)], 0).astype(jnp.bfloat16)
            acc = acc + lax.dot_general(left, hot_lo, (((1,),(1,)),((),())), preferred_element_type=jnp.float32)
        return acc
    out_ref[...] = lax.fori_loop(0, rows // 8, step, jnp.zeros(out_ref.shape, jnp.float32))

def bucket_sum(summed, index, reach):
    heads = summed.shape[0]
    out = pl.pallas_call(bucket_kernel,
        out_shape=jax.ShapeDtypeStruct((heads * (reach // LOW), LOW), jnp.float32),
        cost_estimate=cost(13), compiler_params=VM)(summed, index)
    return out.reshape(heads, reach)
QUARTER=64
NT=(((1,),(1,)),((),()))
TN=(((0,),(0,)),((),()))
def dot(a,b,dims=(((1,),(0,)),((),()))):
    return lax.dot_general(a,b,dims,preferred_element_type=jnp.float32)

def row_start(position, part):
    share = part // FRAMES
    return pl.multiple_of((position ^ share) * (FRAMES * QUARTER) + (part % FRAMES) * QUARTER, QUARTER)

def load_windows(ref, position, kind, step, cols):
    if kind == 0:
        return [jnp.concatenate([ref[pl.ds(row_start(position, 4 * step + t), QUARTER), cols] for t in range(4)], 0)]
    both = [[], []]
    for f in range(FRAMES):
        for k in range(2):
            block = ref[pl.ds(row_start(position, 4 * f + 2 * step + k), QUARTER), cols].astype(jnp.float32)
            block = block.reshape(4, 2, 8, block.shape[-1])
            for c in range(2):
                both[c].append(block[:, c].reshape(32, block.shape[-1]))
    return [jnp.concatenate(b, 0).astype(jnp.bfloat16) for b in both]

def store_windows(ref, position, kind, step, cols, values):
    if kind == 0:
        for t in range(4):
            ref[pl.ds(row_start(position, 4 * step + t), QUARTER), cols] = values[0][t * QUARTER:(t + 1) * QUARTER].astype(ref.dtype)
        return
    for f in range(FRAMES):
        for k in range(2):
            at = (2 * f + k) * 32
            block = jnp.stack([v[at:at + 32].reshape(4, 8, v.shape[-1]) for v in values], axis=1)
            ref[pl.ds(row_start(position, 4 * f + 2 * step + k), QUARTER), cols] = block.reshape(QUARTER, block.shape[-1]).astype(ref.dtype)

def self_forward_kernel(kind, position_ref, qkv_ref, bias_ref, out_ref, probs_ref):
    step = pl.program_id(0)
    position = position_ref[0]
    width = out_ref.shape[1]
    heads = width // HD
    size = probs_ref.shape[2]
    q, k, v = [load_windows(qkv_ref, position, kind, step, pl.ds(j * width, width)) for j in range(3)]
    lane = lax.broadcasted_iota(jnp.int32, (size, width), 1) // HD
    results = []
    for w in range(len(q)):
        total = jnp.zeros((size, width), jnp.float32)
        scaled = q[w] * jnp.bfloat16(HD ** -0.5)
        for h in range(heads):
            s = dot(jnp.where(lane == h, scaled, jnp.bfloat16(0)), k[w], NT) + bias_ref[h, :, pl.ds(0, size)].astype(jnp.float32)
            s = s - jnp.max(s, axis=-1, keepdims=True)
            e = jnp.exp(s)
            p = (e * (1.0 / jnp.sum(e, axis=-1, keepdims=True))).astype(jnp.bfloat16)
            probs_ref[w, h] = p
            total = total + dot(p, jnp.where(lane == h, v[w], jnp.bfloat16(0)))
        results.append(total)
    store_windows(out_ref, position, kind, step, pl.ds(0, width), results)

def self_forward_call(kind, position, qkv, bias):
    rows, width = qkv.shape
    width //= 3
    heads = width // HD
    size = 256 if kind == 0 else 320
    per = 1 if kind == 0 else 2
    steps = rows // size // per
    return pl.pallas_call(
        functools.partial(self_forward_kernel, kind),
        out_shape=(jax.ShapeDtypeStruct((rows, width), jnp.bfloat16),
                   jax.ShapeDtypeStruct((steps * per, heads, size, size), jnp.bfloat16)),
        grid_spec=pltpu.PrefetchScalarGridSpec(
            num_scalar_prefetch=1, grid=(steps,),
            in_specs=[pl.BlockSpec(qkv.shape, lambda i, p: (0, 0)),
                      pl.BlockSpec(bias.shape, lambda i, p: (0, 0, 0))],
            out_specs=[pl.BlockSpec((rows, width), lambda i, p: (0, 0)),
                       pl.BlockSpec((per, heads, size, size), lambda i, p: (i, 0, 0, 0))]),
        cost_estimate=cost(8), compiler_params=VM,
        name="self_forward",
    )(position, qkv, bias)

def self_backward_kernel(kind, position_ref, qkv_ref, probs_ref, grad_ref, dqkv_ref, sum_ref):
    step = pl.program_id(0)
    position = position_ref[0]
    width = grad_ref.shape[1]
    heads = width // HD
    size = probs_ref.shape[2]
    q, k, v = [load_windows(qkv_ref, position, kind, step, pl.ds(j * width, width)) for j in range(3)]
    g = load_windows(grad_ref, position, kind, step, pl.ds(0, width))
    lane = lax.broadcasted_iota(jnp.int32, (size, width), 1) // HD
    zero = jnp.bfloat16(0)
    @pl.when(step == 0)
    def _():
        sum_ref[...] = jnp.zeros_like(sum_ref)
    outs = [[], [], []]
    for w in range(len(q)):
        dq = jnp.zeros((size, width), jnp.float32)
        dk = jnp.zeros((size, width), jnp.float32)
        dv = jnp.zeros((size, width), jnp.float32)
        scaled = q[w] * jnp.bfloat16(HD ** -0.5)
        kscaled = k[w] * jnp.bfloat16(HD ** -0.5)
        for h in range(heads):
            mine = lane == h
            gh = jnp.where(mine, g[w], zero)
            p16 = probs_ref[w, h]
            p = p16.astype(jnp.float32)
            dp = dot(gh, v[w], NT)
            ds = p * (dp - jnp.sum(p * dp, axis=-1, keepdims=True))
            ds16 = ds.astype(jnp.bfloat16)
            sum_ref[h] += ds16.astype(jnp.float32)
            dq = dq + dot(ds16, jnp.where(mine, kscaled, zero))
            dk = dk + dot(ds16, jnp.where(mine, scaled, zero), TN)
            dv = dv + dot(p16, gh, TN)
        outs[0].append(dq); outs[1].append(dk); outs[2].append(dv)
    for j in range(3):
        store_windows(dqkv_ref, position, kind, step, pl.ds(j * width, width), outs[j])

def self_backward_call(kind, position, qkv, probs, grad):
    rows, width = grad.shape
    heads = width // HD
    size = probs.shape[2]
    per = 1 if kind == 0 else 2
    steps = rows // size // per
    return pl.pallas_call(
        functools.partial(self_backward_kernel, kind),
        out_shape=(jax.ShapeDtypeStruct(qkv.shape, jnp.bfloat16),
                   jax.ShapeDtypeStruct((heads, size, size), jnp.float32)),
        grid_spec=pltpu.PrefetchScalarGridSpec(
            num_scalar_prefetch=1, grid=(steps,),
            in_specs=[pl.BlockSpec(qkv.shape, lambda i, p: (0, 0)),
                      pl.BlockSpec((per, heads, size, size), lambda i, p: (i, 0, 0, 0)),
                      pl.BlockSpec(grad.shape, lambda i, p: (0, 0))],
            out_specs=[pl.BlockSpec(qkv.shape, lambda i, p: (0, 0)),
                       pl.BlockSpec((heads, size, size), lambda i, p: (0, 0, 0))]),
        cost_estimate=cost(13), compiler_params=VM,
        name="self_backward",
    )(position, qkv, probs, grad)
PAD=128

CROSS = 2 * LANES


def cross_forward_kernel(q_ref, k_ref, v_ref, bias_ref, out_ref, probs_ref):
    rows = q_ref.shape[0]
    first = lax.broadcasted_iota(jnp.int32, (rows, LANES), 1) < HD
    vfirst = lax.broadcasted_iota(jnp.int32, (PAD, LANES), 1) < HD
    zero = jnp.bfloat16(0)
    for at in range(0, CROSS, LANES):
        q = q_ref[:, at : at + LANES] * jnp.bfloat16(HD ** -0.5)
        v = v_ref[:, at : at + LANES]
        total = jnp.zeros((rows, LANES), jnp.float32)
        for half in range(2):
            s = dot(jnp.where(first == (half == 0), q, zero), k_ref[:, at : at + LANES], NT) + bias_ref[...]
            s = s - jnp.max(s, axis=-1, keepdims=True)
            e = jnp.exp(s)
            p = (e * (1.0 / jnp.sum(e, axis=-1, keepdims=True))).astype(jnp.bfloat16)
            probs_ref[at // HD + half] = p
            total = total + dot(p, jnp.where(vfirst == (half == 0), v, zero))
        out_ref[:, at : at + LANES] = total.astype(jnp.bfloat16)


def cross_forward_call(q, k, v, bias):
    rows, width = q.shape
    pairs = width // CROSS
    col = lambda i: (0, i)
    return pl.pallas_call(
        cross_forward_kernel, grid=(pairs,),
        in_specs=[pl.BlockSpec((rows, CROSS), col), pl.BlockSpec((PAD, CROSS), col), pl.BlockSpec((PAD, CROSS), col),
                  pl.BlockSpec((1, PAD), lambda i: (0, 0))],
        out_specs=[pl.BlockSpec((rows, CROSS), col), pl.BlockSpec((4, rows, PAD), lambda i: (i, 0, 0))],
        out_shape=[jax.ShapeDtypeStruct((rows, width), jnp.bfloat16), jax.ShapeDtypeStruct((4 * pairs, rows, PAD), jnp.bfloat16)],
        cost_estimate=cost(8), compiler_params=VM, name="cross_forward")(q, k, v, bias)

def cross_backward_kernel(q_ref, k_ref, v_ref, probs_ref, grad_ref, dq_ref, dk_ref, dv_ref):
    rows = q_ref.shape[0]
    first = lax.broadcasted_iota(jnp.int32, (rows, LANES), 1) < HD
    kfirst = lax.broadcasted_iota(jnp.int32, (PAD, LANES), 1) < HD
    zero = jnp.bfloat16(0)
    for at in range(0, CROSS, LANES):
        q = q_ref[:, at : at + LANES] * jnp.bfloat16(HD ** -0.5)
        k = k_ref[:, at : at + LANES] * jnp.bfloat16(HD ** -0.5)
        grad = grad_ref[:, at : at + LANES]
        dq = jnp.zeros((rows, LANES), jnp.float32)
        dk = jnp.zeros((PAD, LANES), jnp.float32)
        dv = jnp.zeros((PAD, LANES), jnp.float32)
        for half in range(2):
            mine = first == (half == 0)
            g = jnp.where(mine, grad, zero)
            p16 = probs_ref[at // HD + half]
            p = p16.astype(jnp.float32)
            dp = dot(g, v_ref[:, at : at + LANES], NT)
            ds = (p * (dp - jnp.sum(p * dp, axis=-1, keepdims=True))).astype(jnp.bfloat16)
            dq = dq + dot(ds, jnp.where(kfirst == (half == 0), k, zero))
            dk = dk + dot(ds, jnp.where(mine, q, zero), TN)
            dv = dv + dot(p16, g, TN)
        dq_ref[:, at : at + LANES] = dq.astype(jnp.bfloat16)
        dk_ref[:, at : at + LANES] = dk
        dv_ref[:, at : at + LANES] = dv


def cross_backward_call(q, k, v, probs, grad):
    rows, width = q.shape
    pairs = width // CROSS
    col = lambda i: (0, i)
    tok = pl.BlockSpec((rows, CROSS), col); txt = pl.BlockSpec((PAD, CROSS), col)
    return pl.pallas_call(
        cross_backward_kernel, grid=(pairs,),
        in_specs=[tok, txt, txt, pl.BlockSpec((4, rows, PAD), lambda i: (i, 0, 0)), tok],
        out_specs=[tok, txt, txt],
        out_shape=[jax.ShapeDtypeStruct((rows, width), jnp.bfloat16), jax.ShapeDtypeStruct((PAD, width), jnp.float32), jax.ShapeDtypeStruct((PAD, width), jnp.float32)],
        cost_estimate=cost(9), compiler_params=VM, name="cross_backward")(q, k, v, probs, grad)


def gelu_slope(u):
    inner = 0.7978845608028654 * (u + 0.044715 * u * u * u)
    th = jnp.tanh(inner)
    return 0.5 * (1.0 + th) + 0.5 * u * (1.0 - th * th) * (0.7978845608028654 * (1.0 + 3.0 * 0.044715 * u * u))


FF_TILE = 256


def feed_forward_kernel(a_ref, b_ref, up_ref, down_ref, hidden_ref, active_ref, pa_ref, pb_ref):
    rows = a_ref.shape[0]
    units = up_ref.shape[1]
    for at, ref in ((0, a_ref), (rows, b_ref)):
        for t in range(0, units, FF_TILE):
            u = dot(ref[...], up_ref[:, t : t + FF_TILE])
            hidden_ref[pl.ds(at, rows), t : t + FF_TILE] = u.astype(jnp.bfloat16)
            active_ref[pl.ds(at, rows), t : t + FF_TILE] = jax.nn.gelu(u, approximate=True).astype(jnp.bfloat16)
    pa_ref[...] = dot(active_ref[pl.ds(0, rows), :], down_ref[...], NT).astype(jnp.bfloat16)
    pb_ref[...] = dot(active_ref[pl.ds(rows, rows), :], down_ref[...], NT).astype(jnp.bfloat16)


def half_columns(weights):
    units = weights.shape[1] // 2
    return [pl.BlockSpec((weights.shape[0], units), lambda i: (0, 0)), pl.BlockSpec((weights.shape[0], units), lambda i: (0, 1))]


def feed_forward_call(a, b, weights):
    rows, width = a.shape
    units = weights.shape[1] // 2
    whole = pl.BlockSpec((rows, width), lambda i: (0, 0))
    wide = pl.BlockSpec((2 * rows, units), lambda i: (0, 0))
    return pl.pallas_call(
        feed_forward_kernel,
        grid=(1,),
        in_specs=[whole, whole] + half_columns(weights),
        out_specs=[wide, wide, whole, whole],
        out_shape=[
            jax.ShapeDtypeStruct((2 * rows, units), jnp.bfloat16),
            jax.ShapeDtypeStruct((2 * rows, units), jnp.bfloat16),
            jax.ShapeDtypeStruct((rows, width), jnp.bfloat16),
            jax.ShapeDtypeStruct((rows, width), jnp.bfloat16),
        ],
        cost_estimate=cost(7), compiler_params=VM,
        name="feed_forward",
    )(a, b, weights, weights)


def feed_backward_kernel(a_ref, b_ref, hidden_ref, up_ref, down_ref, grad_ref, pa_ref, pb_ref):
    rows = a_ref.shape[0]
    units = up_ref.shape[1]
    for at, ref in ((0, a_ref), (rows, b_ref)):
        for t in range(0, units, FF_TILE):
            slope = gelu_slope(hidden_ref[pl.ds(at, rows), t : t + FF_TILE].astype(jnp.float32))
            grad_ref[pl.ds(at, rows), t : t + FF_TILE] = (dot(ref[...], down_ref[:, t : t + FF_TILE]) * slope).astype(jnp.bfloat16)
    pa_ref[...] = dot(grad_ref[pl.ds(0, rows), :], up_ref[...], NT).astype(jnp.bfloat16)
    pb_ref[...] = dot(grad_ref[pl.ds(rows, rows), :], up_ref[...], NT).astype(jnp.bfloat16)


def feed_backward_call(a, b, hidden, weights):
    rows, width = a.shape
    units = weights.shape[1] // 2
    whole = pl.BlockSpec((rows, width), lambda i: (0, 0))
    wide = pl.BlockSpec((2 * rows, units), lambda i: (0, 0))
    return pl.pallas_call(
        feed_backward_kernel,
        grid=(1,),
        in_specs=[whole, whole, wide] + half_columns(weights),
        out_specs=[wide, whole, whole],
        out_shape=[
            jax.ShapeDtypeStruct((2 * rows, units), jnp.bfloat16),
            jax.ShapeDtypeStruct((rows, width), jnp.bfloat16),
            jax.ShapeDtypeStruct((rows, width), jnp.bfloat16),
        ],
        cost_estimate=cost(8), compiler_params=VM,
        name="feed_backward",
    )(a, b, hidden, weights, weights)


def weight_grad_kernel(counts, splits, order_ref, *refs):
    step = pl.program_id(0)
    (ln_a, rn_a), (ln_b, rn_b) = splits
    left = (refs[:ln_a], refs[ln_a : ln_a + ln_b])
    refs = refs[ln_a + ln_b :]
    right = (refs[:rn_a], refs[rn_a : rn_a + rn_b])
    out_ref, turned_ref = refs[rn_a + rn_b :]
    blocks = order_ref.shape[0]
    width = turned_ref.shape[0] // blocks

    def turn(pieces):
        at = 0
        for ref in pieces:
            rows = ref.shape[0]
            for p in range(blocks):
                column = pl.multiple_of(order_ref[p] * width, width)
                turned_ref[pl.ds(p * width, width), pl.ds(at, rows)] = ref[:, pl.ds(column, width)].T
            at += rows

    def product(pieces):
        at = 0
        total = None
        for ref in pieces:
            rows = ref.shape[0]
            part = dot(turned_ref[:, pl.ds(at, rows)], ref[...])
            total = part if total is None else total + part
            at += rows
        out_ref[...] = total.astype(jnp.bfloat16).reshape(out_ref.shape)

    for n, begin in ((0, 0), (1, counts[0])):

        @pl.when(step == begin)
        def _():
            turn(left[n])

        @pl.when(jnp.logical_and(step >= begin, step < begin + counts[n]))
        def _():
            product(right[n])


GRAD_TILE = 256


def weight_grad_call(order, lefts, rights, out_shape, out_map):
    counts = [sum_cols // GRAD_TILE for sum_cols in (rights[0][0][0].shape[1], rights[1][0][0].shape[1])]
    splits = [(len(lefts[n]), len(rights[n])) for n in range(2)]
    in_specs, operands = [], []
    for n in range(2):
        for item in lefts[n]:
            in_specs.append(pl.BlockSpec(item.shape, lambda i, o: (0, 0)))
            operands.append(item)
    for n in range(2):
        begin, count = (0, counts[0])[n], counts[n]
        for item, rows, block in rights[n]:
            in_specs.append(
                pl.BlockSpec(
                    (rows, GRAD_TILE),
                    lambda i, o, begin=begin, count=count, block=block: (block, jnp.clip(i - begin, 0, count - 1)),
                )
            )
            operands.append(item)
    tokens = sum(item.shape[0] for item in lefts[0])
    width = lefts[0][0].shape[1]
    tiles = counts[0] + counts[1]
    block_shape = out_shape[:-1] + (GRAD_TILE,) if len(out_shape) == 2 else (1, out_shape[1], GRAD_TILE)
    return pl.pallas_call(
        functools.partial(weight_grad_kernel, counts, splits),
        grid_spec=pltpu.PrefetchScalarGridSpec(
            num_scalar_prefetch=1,
            grid=(tiles,),
            in_specs=in_specs,
            out_specs=pl.BlockSpec(block_shape, out_map),
            scratch_shapes=[pltpu.VMEM((width, tokens), jnp.bfloat16)],
        ),
        out_shape=jax.ShapeDtypeStruct(out_shape, jnp.bfloat16),
        cost_estimate=cost(12), compiler_params=VM,
        name="weight_grad",
    )(order, *operands)


def regroup(columns, outer, inner):
    pieces = []
    for i in range(inner):
        for o in range(outer):
            at = (o * inner + i) * HD
            pieces.append(columns[:, at : at + HD])
    return jnp.concatenate(pieces, axis=1)


def prepare_kernel(qkv_ref, out_ref, cq_ref, ckv_ref, cout_ref, up_ref, down_ref, self_ref, pair_ref, text_ref, feed_ref):
    wide = cq_ref.shape[2]
    heads = wide // HD
    units = up_ref.shape[2]
    self_ref[0, :, : 3 * wide] = regroup(qkv_ref[0], heads, 3).astype(jnp.bfloat16)
    self_ref[0, :, 3 * wide :] = out_ref[0].T.astype(jnp.bfloat16)
    pair_ref[0, :, :wide] = cq_ref[0].astype(jnp.bfloat16)
    pair_ref[0, :, wide:] = cout_ref[0].T.astype(jnp.bfloat16)
    text_ref[0] = regroup(ckv_ref[0], heads, 2).astype(jnp.bfloat16)
    feed_ref[0, :, :units] = up_ref[0].astype(jnp.bfloat16)
    feed_ref[0, :, units:] = down_ref[0].T.astype(jnp.bfloat16)


def layer_block(shape):
    return pl.BlockSpec((1,) + tuple(shape[1:]), lambda i: (i, 0, 0))


def prepare_call(masters):
    layers, block, wide = masters[2].shape
    units = masters[5].shape[2]
    shapes = [(layers, block, 4 * wide), (layers, block, 2 * wide), (layers, block, 2 * wide), (layers, block, 2 * units)]
    return pl.pallas_call(
        prepare_kernel,
        grid=(layers,),
        in_specs=[layer_block(item.shape) for item in masters],
        out_specs=[layer_block(shape) for shape in shapes],
        out_shape=[jax.ShapeDtypeStruct(shape, jnp.bfloat16) for shape in shapes],
        cost_estimate=cost(3), compiler_params=VM,
        name="prepare",
    )(*masters)


def adam_math(master, first, second, grad, rate):
    first_new = BETA_ONE * first + (1.0 - BETA_ONE) * grad
    second_new = BETA_TWO * second + (1.0 - BETA_TWO) * grad * grad
    step_size = (
        first_new / (1.0 - BETA_ONE**STEP) / (jnp.sqrt(second_new / (1.0 - BETA_TWO**STEP)) + ADAM_EPS)
    )
    master_new = master - rate * (step_size + DECAY_RATE * master)
    return (master_new, first_new, second_new, master_new.astype(jnp.bfloat16))


def adam_kernel(plans, n_grads, *refs):
    layer = pl.program_id(0)
    count = len(plans)
    sources = [jnp.where(layer == 0, refs[2 * n][...], refs[2 * n + 1][...]).astype(jnp.float32) for n in range(n_grads)]
    refs = refs[2 * n_grads :]
    for n, (source, begin, width, kind, rate) in enumerate(plans):
        master, first, second = [refs[3 * n + m][0] for m in range(3)]
        outs = refs[3 * count + 4 * n : 3 * count + 4 * n + 4]
        grad = sources[source][:, begin : begin + width]
        if kind == "turn":
            grad = grad.T
        elif kind:
            grad = regroup(grad, kind, width // (kind * HD))
        for ref, value in zip(outs, adam_math(master, first, second, grad, rate)):
            ref[0] = value


def adam_call(plans, grads, states):
    in_specs, operands, out_specs, out_shape = [], [], [], []
    for pair in grads:
        for item in pair:
            in_specs.append(pl.BlockSpec(item.shape, lambda i: (0, 0)))
            operands.append(item)
    for group in states:
        for item in group:
            in_specs.append(layer_block(item.shape))
            operands.append(item)
        shape = group[0].shape
        for dtype in (jnp.float32, jnp.float32, jnp.float32, jnp.bfloat16):
            out_specs.append(layer_block(shape))
            out_shape.append(jax.ShapeDtypeStruct(shape, dtype))
    result = pl.pallas_call(
        functools.partial(adam_kernel, plans, len(grads)),
        grid=(states[0][0].shape[0],),
        in_specs=in_specs,
        out_specs=out_specs,
        out_shape=out_shape,
        cost_estimate=cost(5), compiler_params=VM,
        name="adam",
    )(*operands)
    return [result[4 * n : 4 * n + 4] for n in range(len(states))]


def exchange(value, axis, bit, size):
    return lax.ppermute(value, axis, [(i, i ^ bit) for i in range(size)])


def after(value, *anchors):
    return lax.optimization_barrier((value, anchors))[0]


def share_rows(own, meanwhile):
    far = exchange(own, "mp", 2, 4)
    near = exchange(own, "mp", 1, 4)
    done = meanwhile(own, near)
    far = after(far, done)
    return (own, near, far, exchange(far, "mp", 1, 4)), done


def share_small(own):
    far = exchange(own, "mp", 2, 4)
    near = exchange(own, "mp", 1, 4)
    return (own, near, far, exchange(far, "mp", 1, 4))


def collect_parts(parts, meanwhile=None):
    beside = exchange(parts[3], "mp", 1, 4)
    crossing = narrow(parts[2].astype(jnp.float32) + beside.astype(jnp.float32))
    far = exchange(crossing, "mp", 2, 4)
    near_part, done = parts[1], None
    if meanwhile is not None:
        done = meanwhile((crossing, parts[0], parts[1]))
        far = after(far, done)
    near = exchange(after(parts[1], crossing), "mp", 1, 4)
    total = parts[0].astype(jnp.float32) + near.astype(jnp.float32) + far.astype(jnp.float32)
    return total if meanwhile is None else (total, done)


def bits_of(size):
    return [1 << n for n in range(size.bit_length() - 1)]


class Flow:
    def __init__(self, stages):
        self.stages = stages
        self.result = None
        self.pending = next(stages)

    def take(self, value):
        try:
            self.pending = self.stages.send(value)
        except StopIteration as stop:
            self.pending = None
            self.result = stop.value

    def finish(self):
        while self.pending is not None:
            self.take(self.pending)
        return self.result


def tick(anchor, *flows):
    flows = [flow for flow in flows if flow is not None and flow.pending is not None]
    if not flows:
        return anchor
    anchor, values = lax.optimization_barrier((anchor, [flow.pending for flow in flows]))
    for flow, value in zip(flows, values):
        flow.take(value)
    return anchor


def block_order(size):
    me = lax.axis_index("dp").astype(jnp.int32)
    if (D // size) % LANES:
        return jnp.arange(D // LANES, dtype=jnp.int32), False
    order = [0]
    for bit in reversed(bits_of(size)):
        order = order + [item | bit for item in order]
    return jnp.array(order, jnp.int32) ^ me, True


def halving(total, size, ordered):
    me = lax.axis_index("dp")
    rows, width = total.shape
    if ordered:
        for bit in bits_of(size):
            half = total.shape[0] // 2
            got = yield exchange(narrow(total[half:]), "dp", bit, size)
            total = total[:half].astype(jnp.float32) + got.astype(jnp.float32)
            if bit * 2 < size:
                total = narrow(total)
        return total
    blocks = total.reshape(size, rows // size, width)
    for n, bit in enumerate(bits_of(size)):
        pairs = blocks.reshape(blocks.shape[0] // 2, 2, rows // size, width)
        mine = (me >> n) & 1
        keep = lax.dynamic_index_in_dim(pairs, mine, 1, keepdims=False)
        send = lax.dynamic_index_in_dim(pairs, 1 - mine, 1, keepdims=False)
        got = yield exchange(send, "dp", bit, size)
        total = keep.astype(jnp.float32) + got.astype(jnp.float32)
        blocks = narrow(total)
    return total.reshape(rows // size, width)


def doubling(own, size):
    me = lax.axis_index("dp")
    rows, width = own.shape
    own = own[None, None]
    for n, bit in reversed(list(enumerate(bits_of(size)))):
        got = yield exchange(own, "dp", bit, size)
        own = jnp.where(((me >> n) & 1) == 0, jnp.concatenate([own, got], axis=1), jnp.concatenate([got, own], axis=1))
        own = own.reshape(own.shape[0] * 2, 1, rows, width)
    return own.reshape(size * rows, width)


def collecting(parts):
    beside, near = yield (exchange(parts[3], "mp", 1, 4), exchange(parts[1], "mp", 1, 4))
    crossing = narrow(parts[2].astype(jnp.float32) + beside.astype(jnp.float32))
    far = yield exchange(crossing, "mp", 2, 4)
    return parts[0].astype(jnp.float32) + near.astype(jnp.float32) + far.astype(jnp.float32)


def collect_then_gather(parts, size):
    total = yield from collecting(parts)
    total = narrow(total)
    got = yield exchange(total, "dp", 1, size)
    slots = narrow(total.astype(jnp.float32) + got.astype(jnp.float32))[None, None]
    me = lax.axis_index("dp")
    for n, bit in reversed(list(enumerate(bits_of(size)))[1:]):
        got = yield exchange(slots, "dp", bit, size)
        slots = jnp.where(((me >> n) & 1) == 0, jnp.concatenate([slots, got], axis=1), jnp.concatenate([got, slots], axis=1))
        slots = slots.reshape((slots.shape[0] * 2, 1) + slots.shape[2:])
    return slots[:, 0]


def pair_up(slots):
    got = yield (exchange(slots[1], "mp", 1, 4), exchange(slots[3], "mp", 1, 4))
    return jnp.concatenate([narrow(slots[2 * k].astype(jnp.float32) + got[k].astype(jnp.float32)) for k in range(2)], axis=1)


def halve_then_cross(total, size, ordered, width):
    total = yield from halving(total, size, ordered)
    got = yield exchange(narrow(total[:, width : 2 * width]), "mp", 2, 4)
    return total[:, :width] + got.astype(jnp.float32), total[:, 2 * width :]


def summing_rows(rows, size):
    for bit in (1, 2):
        got = yield exchange(narrow(rows), "mp", bit, 4)
        rows = rows + got.astype(jnp.float32)
    slots = narrow(rows)[None, None]
    me = lax.axis_index("dp")
    for n, bit in reversed(list(enumerate(bits_of(size)))[1:]):
        got = yield exchange(slots, "dp", bit, size)
        slots = jnp.where(((me >> n) & 1) == 0, jnp.concatenate([slots, got], axis=1), jnp.concatenate([got, slots], axis=1))
        slots = slots.reshape((slots.shape[0] * 2, 1) + slots.shape[2:])
    got = yield exchange(slots, "dp", 1, size)
    return slots.astype(jnp.float32) + got.astype(jnp.float32)


def halving_blocks(blocks, size):
    me = lax.axis_index("dp")
    for n, bit in enumerate(bits_of(size)):
        pairs = blocks.reshape((blocks.shape[0] // 2, 2) + blocks.shape[1:])
        mine = (me >> n) & 1
        got = yield exchange(lax.dynamic_index_in_dim(pairs, 1 - mine, 1, keepdims=False), "dp", bit, size)
        blocks = lax.dynamic_index_in_dim(pairs, mine, 1, keepdims=False) + got
    return blocks[0]


def gathering(own, size):
    me = lax.axis_index("dp")
    slots = own[None]
    for n, bit in enumerate(bits_of(size)):
        got = yield exchange(slots, "dp", bit, size)
        slots = jnp.where(((me >> n) & 1) == 0, jnp.concatenate([slots, got]), jnp.concatenate([got, slots]))
    return slots


def gather_small(own, size):
    return Flow(gathering(own, size)).finish()


def modulate(latent, scale, shift):
    normed, inverse = layer_norm(latent)
    return (normed * (1.0 + scale) + shift).astype(jnp.bfloat16)


def narrow(value):
    return value.astype(jnp.bfloat16)


def mm(a, b, dims=(((1,), (0,)), ((), ()))):
    return lax.dot_general(a, b, dims, preferred_element_type=jnp.float32)


def body(*args):
    (latents, cotangent, text_embed, text_mask, band_ids, rel_index_s, rel_index_t, modulation) = args[:8]
    masters, firsts, seconds = args[8:17], args[17:26], args[26:35]
    groups = lax.axis_size("dp")
    rates = learning_rates()
    own = latents.shape[0]
    half = 2 * own
    wide = masters[1].shape[1]
    index_tables = (rel_index_s, rel_index_t)
    reaches = (masters[7].shape[1] * groups, masters[8].shape[1] * groups)

    order, ordered = block_order(groups)
    plain = jnp.arange(D // LANES, dtype=jnp.int32)

    block = D // groups
    self_shards, pair_shards, text_shards, feed_shards = prepare_call(masters[:7])
    pair_shards = pair_shards.reshape(LAYERS * block, 2 * wide)
    other = exchange(pair_shards, "mp", 2, 4)

    def cross_shard(layer):
        rows = slice(layer * block, (layer + 1) * block)
        return [pair_shards[rows], other[rows], text_shards[layer]]

    def gather(pieces):
        return lax.all_gather(jnp.concatenate(pieces, axis=1), "dp", axis=0, tiled=True)

    split = 4 * wide
    self_flow_0 = Flow(doubling(self_shards[0], groups))
    first_all = gather(cross_shard(0) + [feed_shards[0]])
    next_all = gather([self_shards[1]] + cross_shard(1))
    feed_1 = lax.all_gather(feed_shards[1], "dp", axis=0, tiled=True)
    cross_ws = (first_all[:, : 6 * wide], next_all[:, split:])
    feed_ws = (first_all[:, 6 * wide :], feed_1)

    position = lax.axis_index("mp").astype(jnp.int32)[None]
    clip_index = lax.axis_index("dp") // 2
    text_rows = lax.dynamic_index_in_dim(text_embed, clip_index, 0, keepdims=False)
    texts = text_rows.shape[0]
    texts_pad = -(-texts // 16) * 16
    text_rows = jnp.pad(text_rows, ((0, PAD - texts), (0, 0)))
    mask_row = lax.dynamic_index_in_dim(text_mask, clip_index, 0, keepdims=False)
    column = jnp.arange(PAD, dtype=jnp.int32)
    valid = jnp.maximum(jnp.pad(mask_row, (0, PAD - texts)), (column == 0).astype(jnp.int32)).astype(jnp.float32)
    valid_bias = jnp.where(column < texts, (valid - 1.0) * 1000000000.0, -1e30)[None]
    band_now = lax.dynamic_index_in_dim(band_ids, clip_index, 0, keepdims=False)
    mod_rows = lax.dynamic_index_in_dim(modulation, band_now, 0, keepdims=False)
    text_columns = lax.dynamic_slice_in_dim(text_embed, lax.axis_index("dp") * (D // groups), D // groups, axis=2)

    tables = gather_small(jnp.concatenate([narrow(masters[7]), narrow(masters[8])], axis=1), groups)
    tables = tables.swapaxes(0, 1)
    cut = masters[7].shape[1]
    table_s = tables[:, :, :cut].reshape(tables.shape[0], -1)
    table_t = tables[:, :, cut:].reshape(tables.shape[0], -1)
    biases = (make_bias(table_s, rel_index_s), make_bias(table_t, rel_index_t))

    latent = latents
    saved = []
    weights = []
    for layer in range(LAYERS):
        base = 9 * layer
        record = {"in": latent}
        sending = modulate(latent, mod_rows[base + 1], mod_rows[base])
        if layer == 0:
            self_w = after(self_flow_0.finish(), biases)
        else:
            self_w = next_all[:, :split]
        w_in = self_w[:, : 3 * wide]
        rows, near_qkv = share_rows(sending, lambda one, two: (narrow(mm(one, w_in)), narrow(mm(two, w_in))))
        qkv = jnp.concatenate(near_qkv + tuple(narrow(mm(item, w_in)) for item in rows[2:]), axis=0)
        mixed, probs = self_forward_call(layer, position, qkv, biases[layer])
        w_out = self_w[:, 3 * wide :]
        project = lambda k: narrow(mm(mixed[k * own : (k + 1) * own], w_out, NT))
        p2, p3 = project(2), project(3)
        branch = collect_parts([project(0), project(1), p2, p3])
        record["self"] = (rows, qkv, probs, mixed, branch)
        latent = latent + mod_rows[base + 2] * branch
        record["mid"] = latent
        normed = modulate(latent, mod_rows[base + 4], mod_rows[base + 3])
        cross_w = cross_ws[layer]
        keyval = share_small(narrow(mm(text_rows, cross_w[:, 4 * wide :])))
        keys = jnp.concatenate([item[:, :wide] for item in keyval], axis=1)
        values = jnp.concatenate([item[:, wide:] for item in keyval], axis=1)
        across = exchange(cross_w[:, : 4 * wide], "mp", 1, 4)
        cross_all = (cross_w[:, : 2 * wide], across[:, : 2 * wide], cross_w[:, 2 * wide : 4 * wide], across[:, 2 * wide :])
        w_cq = jnp.concatenate([item[:, :wide] for item in cross_all], axis=1)
        w_cout = jnp.concatenate([item[:, wide:] for item in cross_all], axis=1)
        queries = narrow(mm(normed, w_cq))
        mixed, probs = cross_forward_call(queries, keys, values, valid_bias)
        branch = mm(mixed, w_cout, NT)
        record["cross"] = (normed, queries, keys, values, probs, mixed, branch, w_cq, w_cout)
        latent = latent + mod_rows[base + 5] * branch
        record["late"] = latent
        feed_w = feed_ws[layer]
        weights.append((self_w, feed_w))
        rows, (hidden_near, active_near, p0, p1) = share_rows(
            modulate(latent, mod_rows[base + 7], mod_rows[base + 6]), lambda one, two: feed_forward_call(one, two, feed_w)
        )
        hidden_far, active_far, p2, p3 = feed_forward_call(rows[2], rows[3], feed_w)
        branch = collect_parts([p0, p1, p2, p3])
        record["feed"] = (rows, (hidden_near, hidden_far), (active_near, active_far), branch)
        latent = latent + mod_rows[base + 8] * branch
        saved.append(record)

    grad_latent = cotangent
    mod_grads = [None, None]
    feed_flows, self_flows, cross_flows, tables_sent, kv_grads = [None] * 2, [None] * 2, [None] * 2, [None] * 2, [None] * 2
    kv_flow = None
    for layer in reversed(range(LAYERS)):
        self_w, feed_w = weights[layer]
        last = layer == 0
        base = 9 * layer
        record = saved[layer]
        rows, hiddens, actives, branch = record["feed"]
        gate_m = jnp.sum(grad_latent * branch, axis=0)
        grads, (dh_near, p0, p1) = share_rows(
            narrow(mod_rows[base + 8] * grad_latent), lambda one, two: feed_backward_call(one, two, hiddens[0], feed_w)
        )
        dh_far, p2, p3 = feed_backward_call(grads[2], grads[3], hiddens[1], feed_w)
        units = dh_near.shape[1]
        grad_input, feed_g = collect_parts(
            [p0, p1, p2, p3],
            lambda sent: weight_grad_call(
                plain,
                (rows, grads),
                (((after(dh_near, sent), half, 0), (dh_far, half, 0)), ((actives[0], half, 0), (actives[1], half, 0))),
                (D, 2 * units),
                lambda i, o: (0, i),
            ),
        )
        feed_flows[layer] = lax.psum_scatter(feed_g, "dp", scatter_dimension=0, tiled=True)
        if last:
            grad_input = after(grad_input, feed_flows[1])
        normed, inverse = layer_norm(record["late"])
        grad_latent, shift_m, scale_m = modulate_back(grad_latent, grad_input, normed, inverse, mod_rows[base + 7])

        hidden, queries, keys, values, probs, mixed, branch, w_cq, w_cout = record["cross"]
        gate_c = jnp.sum(grad_latent * branch, axis=0)
        grad_rows = narrow(mod_rows[base + 5] * grad_latent)
        grad_mixed = narrow(mm(grad_rows, w_cout))
        grad_query, grad_key, grad_value = cross_backward_call(queries, keys, values, probs, grad_mixed)
        kv_grads[layer] = [
            narrow(
                jnp.concatenate(
                    [grad_key[:texts_pad, k * wide : (k + 1) * wide], grad_value[:texts_pad, k * wide : (k + 1) * wide]], axis=1
                )
            )
            for k in range(4)
        ]
        if last:
            kv_flow = Flow(
                collect_then_gather([jnp.concatenate([kv_grads[0][k], kv_grads[1][k]], axis=0) for k in range(4)], groups)
            )
        grad_input = mm(grad_query, w_cq, NT)
        normed, inverse = layer_norm(record["mid"])
        grad_latent, shift_c, scale_c = modulate_back(grad_latent, grad_input, normed, inverse, mod_rows[base + 4])
        tiles = queries.shape[1] // GRAD_TILE
        if last:
            grad_latent = tick(grad_latent, kv_flow)
        sending = narrow(mod_rows[base + 2] * grad_latent)
        w_out = self_w[:, 3 * wide :]
        grads, (cross_g, near_mixed) = share_rows(
            sending,
            lambda one, two: (
                weight_grad_call(
                    order if last else plain,
                    ((after(hidden, sending),), (grad_rows,)),
                    (((grad_query, own, 0),), ((mixed, own, 0),)),
                    (tiles, D, 2 * GRAD_TILE),
                    lambda i, o: (i % tiles, 0, i // tiles),
                ),
                (narrow(mm(one, w_out)), narrow(mm(two, w_out))),
            ),
        )
        rows, qkv, probs, mixed, branch = record["self"]
        gate_a = jnp.sum(grad_latent * branch, axis=0)
        grad_mixed = jnp.concatenate(near_mixed + tuple(narrow(mm(item, w_out)) for item in grads[2:]), axis=0)
        pairing = Flow(pair_up(cross_g))
        grad_mixed = tick(grad_mixed, kv_flow)
        grad_qkv, summed = self_backward_call(layer, position, qkv, probs, grad_mixed)
        grad_qkv = tick(grad_qkv, pairing, kv_flow)
        if last:
            cross_flows[0] = Flow(halve_then_cross(pairing.finish(), groups, ordered, 2 * wide))
        back = lambda k: narrow(mm(grad_qkv[k * own : (k + 1) * own], self_w[:, : 3 * wide], NT))
        p2, p3 = back(2), back(3)
        grad_input, self_g = collect_parts(
            [back(0), back(1), p2, p3],
            lambda sent: weight_grad_call(
                order if last else plain,
                (rows, grads),
                (((after(grad_qkv, sent), half, 0), (grad_qkv, half, 1)), ((mixed, half, 0), (mixed, half, 1))),
                (D, 4 * wide),
                lambda i, o: (0, i),
            ),
        )
        if last:
            self_flows[0] = Flow(halving(self_g, groups, ordered))
        else:
            both = jnp.concatenate([pairing.finish(), after(self_g, grad_input)], axis=1)
            upper = lax.psum_scatter(both, "dp", scatter_dimension=0, tiled=True)
            from_pair = exchange(upper[:, 2 * wide : 4 * wide], "mp", 2, 4)
            cross_1 = upper[:, : 2 * wide].astype(jnp.float32) + from_pair.astype(jnp.float32)
            self_1 = upper[:, 4 * wide :]
        tables_sent[layer] = summed
        if last:
            grad_input = tick(grad_input, kv_flow, cross_flows[0])
        normed, inverse = layer_norm(record["in"])
        grad_latent, shift_a, scale_a = modulate_back(grad_latent, grad_input, normed, inverse, mod_rows[base + 1])
        mod_grads[layer] = [shift_a, scale_a, gate_a, shift_c, scale_c, gate_c, shift_m, scale_m, gate_m]
        if last:
            grad_latent = after(grad_latent, upper)

    mod_local = jnp.stack(mod_grads[0] + mod_grads[1], axis=0)
    mod_local = tick(mod_local, cross_flows[0])
    mod_flow = Flow(summing_rows(mod_local, groups))
    table_1 = bucket_sum(after(tables_sent[1], mod_local), index_tables[1], reaches[1])
    table_1 = tick(table_1, mod_flow, cross_flows[0], self_flows[0], kv_flow)
    table_0 = bucket_sum(after(tables_sent[0], table_1), index_tables[0], reaches[0])
    table_0 = tick(table_0, mod_flow, self_flows[0], cross_flows[0])
    table_grads = [table_0, table_1]
    table_rows = [item.reshape(item.shape[0], groups, -1).swapaxes(0, 1) for item in table_grads]
    table_flow = Flow(halving_blocks(jnp.concatenate(table_rows, axis=2), groups))
    units = masters[5].shape[2]
    state = lambda item: (masters[item], firsts[item], seconds[item])
    updates = [None] * 9
    updates[5], updates[6] = adam_call(
        ((0, 0, units, None, rates[5]), (0, units, units, "turn", rates[6])), [feed_flows], [state(5), state(6)]
    )
    updates[5] = tick(updates[5], mod_flow, self_flows[0], cross_flows[0], table_flow)
    mod_clips = mod_flow.finish()
    bands = (band_ids[None, :] == jnp.arange(modulation.shape[0], dtype=jnp.int32)[:, None]).astype(jnp.float32)
    grad_modulation = jnp.sum(bands[:, :, None, None] * mod_clips[None, :, 0], axis=1)

    table_sum = table_flow.finish()
    kv_all = kv_flow.finish()
    kv_sums = []
    for layer in range(LAYERS):
        grad_kv = kv_all[:, layer * texts_pad : layer * texts_pad + texts]
        kv_sums.append(
            lax.dot_general(text_columns, grad_kv, (((0, 1), (0, 1)), ((), ())), preferred_element_type=jnp.float32)
        )
    cross_sums = [cross_flows[0].finish()[0], cross_1]
    updates[2], updates[3], updates[4] = adam_call(
        ((0, 0, wide, None, rates[2]), (1, 0, 2 * wide, 2, rates[3]), (0, wide, wide, "turn", rates[4])),
        [cross_sums, kv_sums],
        [state(2), state(3), state(4)],
    )
    self_sums = [self_flows[0].finish(), self_1]
    updates[0], updates[1] = adam_call(
        ((0, 0, 3 * wide, 3, rates[0]), (0, 3 * wide, wide, "turn", rates[1])), [self_sums], [state(0), state(1)]
    )
    updates[7] = adam_math(masters[7], firsts[7], seconds[7], table_sum[:, :cut], rates[7])
    updates[8] = adam_math(masters[8], firsts[8], seconds[8], table_sum[:, cut:], rates[8])
    results = [latent, grad_latent, grad_modulation]
    for item in updates:
        results.extend(item)
    return tuple(results)


def solution(mesh):
    in_specs = (
        P(("dp", "mp"), None),
        P(("dp", "mp"), None),
        P(),
        P(),
        P(),
        P(),
        P(),
        P(),
        P(None, "dp", "mp"),
        P(None, "mp", "dp"),
        P(None, "dp", "mp"),
        P(None, "dp", "mp"),
        P(None, "mp", "dp"),
        P(None, "dp", "mp"),
        P(None, "mp", "dp"),
        P("mp", "dp"),
        P("mp", "dp"),
        P(None, "dp", "mp"),
        P(None, "mp", "dp"),
        P(None, "dp", "mp"),
        P(None, "dp", "mp"),
        P(None, "mp", "dp"),
        P(None, "dp", "mp"),
        P(None, "mp", "dp"),
        P("mp", "dp"),
        P("mp", "dp"),
        P(None, "dp", "mp"),
        P(None, "mp", "dp"),
        P(None, "dp", "mp"),
        P(None, "dp", "mp"),
        P(None, "mp", "dp"),
        P(None, "dp", "mp"),
        P(None, "mp", "dp"),
        P("mp", "dp"),
        P("mp", "dp"),
    )
    out_specs = (
        P(("dp", "mp"), None),
        P(("dp", "mp"), None),
        P(),
        P(None, "dp", "mp"),
        P(None, "dp", "mp"),
        P(None, "dp", "mp"),
        P(None, "dp", "mp"),
        P(None, "mp", "dp"),
        P(None, "mp", "dp"),
        P(None, "mp", "dp"),
        P(None, "mp", "dp"),
        P(None, "dp", "mp"),
        P(None, "dp", "mp"),
        P(None, "dp", "mp"),
        P(None, "dp", "mp"),
        P(None, "dp", "mp"),
        P(None, "dp", "mp"),
        P(None, "dp", "mp"),
        P(None, "dp", "mp"),
        P(None, "mp", "dp"),
        P(None, "mp", "dp"),
        P(None, "mp", "dp"),
        P(None, "mp", "dp"),
        P(None, "dp", "mp"),
        P(None, "dp", "mp"),
        P(None, "dp", "mp"),
        P(None, "dp", "mp"),
        P(None, "mp", "dp"),
        P(None, "mp", "dp"),
        P(None, "mp", "dp"),
        P(None, "mp", "dp"),
        P("mp", "dp"),
        P("mp", "dp"),
        P("mp", "dp"),
        P("mp", "dp"),
        P("mp", "dp"),
        P("mp", "dp"),
        P("mp", "dp"),
        P("mp", "dp"),
    )
    return jax.shard_map(body, mesh=mesh, in_specs=in_specs, out_specs=out_specs, check_vma=False)
```

```python
import functools

import jax
import jax.numpy as jnp
from jax import lax
from jax.experimental import pallas as pl
from jax.experimental.pallas import tpu as pltpu
from jax.sharding import PartitionSpec as P

D = 1024
HD = 64
FF = 4096
FRAMES = 5
LAYERS = 2
STEP = 10
LANES = 128

BETA_ONE = 0.9
BETA_TWO = 0.95
ADAM_EPS = 1e-08
DECAY_RATE = 0.1


def learning_rates():
    inverse_root = D ** (-0.5)
    return (
        1.5 * inverse_root,
        6.0 * inverse_root,
        1.5 * inverse_root,
        1.5 * inverse_root,
        4.2 * inverse_root,
        1.5 * inverse_root,
        1.5 * FF ** (-0.5),
        1.5,
        1.5,
    )


def layer_norm(tensor):
    center = tensor - jnp.mean(tensor, axis=-1, keepdims=True)
    inverse = lax.rsqrt(jnp.mean(center * center, axis=-1, keepdims=True) + 1e-06)
    return (center * inverse, inverse)


def norm_back(grad_norm, normed, inverse):
    return inverse * (
        grad_norm
        - jnp.mean(grad_norm, axis=-1, keepdims=True)
        - normed * jnp.mean(grad_norm * normed, axis=-1, keepdims=True)
    )


def modulate_back(grad_latent, grad_input, normed, inverse, scaling):
    grad_norm = grad_input * (1.0 + scaling)
    return (
        grad_latent + norm_back(grad_norm, normed, inverse),
        jnp.sum(grad_input, axis=0),
        jnp.sum(grad_input * normed, axis=0),
    )


VM = pltpu.CompilerParams(vmem_limit_bytes=56 * 1024 * 1024)


def cost(microseconds):
    return pl.CostEstimate(flops=int(microseconds * 5e8), bytes_accessed=int(microseconds * 1.5e6), transcendentals=0)


def bias_kernel(table_ref, index_ref, out_ref):
    heads, groups, _ = table_ref.shape
    rows, cols = index_ref.shape
    def step(i, carry):
        r0 = pl.multiple_of(i * 16, 16)
        for c in range(cols // LANES):
            parts = [[] for _ in range(heads)]
            for half in range(2):
                idx = index_ref[pl.ds(r0 + half * 8, 8), pl.ds(c * LANES, LANES)]
                lo = idx & (LANES - 1)
                hi = idx >> 7
                for h in range(heads):
                    acc = jnp.zeros((8, LANES), jnp.float32)
                    for g in range(groups):
                        row = jnp.broadcast_to(table_ref[h, pl.ds(g, 1), :], (8, LANES))
                        val = jnp.take_along_axis(row, lo, axis=1, mode="promise_in_bounds")
                        acc = jnp.where(hi == g, val, acc)
                    parts[h].append(acc)
            for h in range(heads):
                out_ref[h, pl.ds(r0, 16), pl.ds(c * LANES, LANES)] = jnp.concatenate(parts[h], 0).astype(jnp.bfloat16)
        return carry
    lax.fori_loop(0, rows // 16, step, 0)

def make_bias(table, index):
    heads, reach = table.shape
    n = index.shape[0]
    pad = -n % LANES
    index = jnp.pad(index, ((0, 0), (0, pad)))
    return pl.pallas_call(bias_kernel,
        out_shape=jax.ShapeDtypeStruct((heads, n, n + pad), jnp.bfloat16),
        cost_estimate=cost(6), compiler_params=VM)(table.astype(jnp.float32).reshape(heads, reach // LANES, LANES), index)

LOW=64
def bucket_kernel(sum_ref, index_ref, out_ref):
    heads, rows, cols = sum_ref.shape
    high = out_ref.shape[0] // heads
    out_ref[...] = jnp.zeros_like(out_ref)
    hi_iota = lax.broadcasted_iota(jnp.int32, (high, cols), 0)
    lo_iota = lax.broadcasted_iota(jnp.int32, (LOW, cols), 0)
    def step(i, acc):
        r0 = pl.multiple_of(i * 8, 8)
        idx8 = index_ref[pl.ds(r0, 8), :]
        s8 = [sum_ref[h, pl.ds(r0, 8), :] for h in range(heads)]
        for r in range(8):
            idx = idx8[r:r+1]
            hot_hi = hi_iota == (idx >> 6)
            hot_lo = jnp.where(lo_iota == (idx & (LOW-1)), 1.0, 0.0).astype(jnp.bfloat16)
            left = jnp.concatenate([jnp.where(hot_hi, s8[h][r:r+1], 0.0) for h in range(heads)], 0).astype(jnp.bfloat16)
            acc = acc + lax.dot_general(left, hot_lo, (((1,),(1,)),((),())), preferred_element_type=jnp.float32)
        return acc
    out_ref[...] = lax.fori_loop(0, rows // 8, step, jnp.zeros(out_ref.shape, jnp.float32))

def bucket_sum(summed, index, reach):
    heads = summed.shape[0]
    out = pl.pallas_call(bucket_kernel,
        out_shape=jax.ShapeDtypeStruct((heads * (reach // LOW), LOW), jnp.float32),
        cost_estimate=cost(13), compiler_params=VM)(summed, index)
    return out.reshape(heads, reach)
QUARTER=64
NT=(((1,),(1,)),((),()))
TN=(((0,),(0,)),((),()))
def dot(a,b,dims=(((1,),(0,)),((),()))):
    return lax.dot_general(a,b,dims,preferred_element_type=jnp.float32)

def row_start(position, part):
    share = part // FRAMES
    return pl.multiple_of((position ^ share) * (FRAMES * QUARTER) + (part % FRAMES) * QUARTER, QUARTER)

def load_windows(ref, position, kind, step, cols):
    if kind == 0:
        return [jnp.concatenate([ref[pl.ds(row_start(position, 4 * step + t), QUARTER), cols] for t in range(4)], 0)]
    both = [[], []]
    for f in range(FRAMES):
        for k in range(2):
            block = ref[pl.ds(row_start(position, 4 * f + 2 * step + k), QUARTER), cols].astype(jnp.float32)
            block = block.reshape(4, 2, 8, block.shape[-1])
            for c in range(2):
                both[c].append(block[:, c].reshape(32, block.shape[-1]))
    return [jnp.concatenate(b, 0).astype(jnp.bfloat16) for b in both]

def store_windows(ref, position, kind, step, cols, values):
    if kind == 0:
        for t in range(4):
            ref[pl.ds(row_start(position, 4 * step + t), QUARTER), cols] = values[0][t * QUARTER:(t + 1) * QUARTER].astype(ref.dtype)
        return
    for f in range(FRAMES):
        for k in range(2):
            at = (2 * f + k) * 32
            block = jnp.stack([v[at:at + 32].reshape(4, 8, v.shape[-1]) for v in values], axis=1)
            ref[pl.ds(row_start(position, 4 * f + 2 * step + k), QUARTER), cols] = block.reshape(QUARTER, block.shape[-1]).astype(ref.dtype)

def self_forward_kernel(kind, position_ref, qkv_ref, bias_ref, out_ref, probs_ref):
    step = pl.program_id(0)
    position = position_ref[0]
    width = out_ref.shape[1]
    heads = width // HD
    size = probs_ref.shape[2]
    q, k, v = [load_windows(qkv_ref, position, kind, step, pl.ds(j * width, width)) for j in range(3)]
    lane = lax.broadcasted_iota(jnp.int32, (size, width), 1) // HD
    results = []
    for w in range(len(q)):
        total = jnp.zeros((size, width), jnp.float32)
        scaled = q[w] * jnp.bfloat16(HD ** -0.5)
        for h in range(heads):
            s = dot(jnp.where(lane == h, scaled, jnp.bfloat16(0)), k[w], NT) + bias_ref[h, :, pl.ds(0, size)].astype(jnp.float32)
            s = s - jnp.max(s, axis=-1, keepdims=True)
            e = jnp.exp(s)
            p = (e * (1.0 / jnp.sum(e, axis=-1, keepdims=True))).astype(jnp.bfloat16)
            probs_ref[w, h] = p
            total = total + dot(p, jnp.where(lane == h, v[w], jnp.bfloat16(0)))
        results.append(total)
    store_windows(out_ref, position, kind, step, pl.ds(0, width), results)

def self_forward_call(kind, position, qkv, bias):
    rows, width = qkv.shape
    width //= 3
    heads = width // HD
    size = 256 if kind == 0 else 320
    per = 1 if kind == 0 else 2
    steps = rows // size // per
    return pl.pallas_call(
        functools.partial(self_forward_kernel, kind),
        out_shape=(jax.ShapeDtypeStruct((rows, width), jnp.bfloat16),
                   jax.ShapeDtypeStruct((steps * per, heads, size, size), jnp.bfloat16)),
        grid_spec=pltpu.PrefetchScalarGridSpec(
            num_scalar_prefetch=1, grid=(steps,),
            in_specs=[pl.BlockSpec(qkv.shape, lambda i, p: (0, 0)),
                      pl.BlockSpec(bias.shape, lambda i, p: (0, 0, 0))],
            out_specs=[pl.BlockSpec((rows, width), lambda i, p: (0, 0)),
                       pl.BlockSpec((per, heads, size, size), lambda i, p: (i, 0, 0, 0))]),
        cost_estimate=cost(8), compiler_params=VM,
        name="self_forward",
    )(position, qkv, bias)

def self_backward_kernel(kind, position_ref, qkv_ref, probs_ref, grad_ref, dqkv_ref, sum_ref):
    step = pl.program_id(0)
    position = position_ref[0]
    width = grad_ref.shape[1]
    heads = width // HD
    size = probs_ref.shape[2]
    q, k, v = [load_windows(qkv_ref, position, kind, step, pl.ds(j * width, width)) for j in range(3)]
    g = load_windows(grad_ref, position, kind, step, pl.ds(0, width))
    lane = lax.broadcasted_iota(jnp.int32, (size, width), 1) // HD
    zero = jnp.bfloat16(0)
    @pl.when(step == 0)
    def _():
        sum_ref[...] = jnp.zeros_like(sum_ref)
    outs = [[], [], []]
    for w in range(len(q)):
        dq = jnp.zeros((size, width), jnp.float32)
        dk = jnp.zeros((size, width), jnp.float32)
        dv = jnp.zeros((size, width), jnp.float32)
        scaled = q[w] * jnp.bfloat16(HD ** -0.5)
        kscaled = k[w] * jnp.bfloat16(HD ** -0.5)
        for h in range(heads):
            mine = lane == h
            gh = jnp.where(mine, g[w], zero)
            p16 = probs_ref[w, h]
            p = p16.astype(jnp.float32)
            dp = dot(gh, v[w], NT)
            ds = p * (dp - jnp.sum(p * dp, axis=-1, keepdims=True))
            ds16 = ds.astype(jnp.bfloat16)
            sum_ref[h] += ds16.astype(jnp.float32)
            dq = dq + dot(ds16, jnp.where(mine, kscaled, zero))
            dk = dk + dot(ds16, jnp.where(mine, scaled, zero), TN)
            dv = dv + dot(p16, gh, TN)
        outs[0].append(dq); outs[1].append(dk); outs[2].append(dv)
    for j in range(3):
        store_windows(dqkv_ref, position, kind, step, pl.ds(j * width, width), outs[j])

def self_backward_call(kind, position, qkv, probs, grad):
    rows, width = grad.shape
    heads = width // HD
    size = probs.shape[2]
    per = 1 if kind == 0 else 2
    steps = rows // size // per
    return pl.pallas_call(
        functools.partial(self_backward_kernel, kind),
        out_shape=(jax.ShapeDtypeStruct(qkv.shape, jnp.bfloat16),
                   jax.ShapeDtypeStruct((heads, size, size), jnp.float32)),
        grid_spec=pltpu.PrefetchScalarGridSpec(
            num_scalar_prefetch=1, grid=(steps,),
            in_specs=[pl.BlockSpec(qkv.shape, lambda i, p: (0, 0)),
                      pl.BlockSpec((per, heads, size, size), lambda i, p: (i, 0, 0, 0)),
                      pl.BlockSpec(grad.shape, lambda i, p: (0, 0))],
            out_specs=[pl.BlockSpec(qkv.shape, lambda i, p: (0, 0)),
                       pl.BlockSpec((heads, size, size), lambda i, p: (0, 0, 0))]),
        cost_estimate=cost(13), compiler_params=VM,
        name="self_backward",
    )(position, qkv, probs, grad)
PAD=128

CROSS = 2 * LANES


def cross_forward_kernel(q_ref, k_ref, v_ref, bias_ref, out_ref, probs_ref):
    rows = q_ref.shape[0]
    first = lax.broadcasted_iota(jnp.int32, (rows, LANES), 1) < HD
    vfirst = lax.broadcasted_iota(jnp.int32, (PAD, LANES), 1) < HD
    zero = jnp.bfloat16(0)
    for at in range(0, CROSS, LANES):
        q = q_ref[:, at : at + LANES] * jnp.bfloat16(HD ** -0.5)
        v = v_ref[:, at : at + LANES]
        total = jnp.zeros((rows, LANES), jnp.float32)
        for half in range(2):
            s = dot(jnp.where(first == (half == 0), q, zero), k_ref[:, at : at + LANES], NT) + bias_ref[...]
            s = s - jnp.max(s, axis=-1, keepdims=True)
            e = jnp.exp(s)
            p = (e * (1.0 / jnp.sum(e, axis=-1, keepdims=True))).astype(jnp.bfloat16)
            probs_ref[at // HD + half] = p
            total = total + dot(p, jnp.where(vfirst == (half == 0), v, zero))
        out_ref[:, at : at + LANES] = total.astype(jnp.bfloat16)


def cross_forward_call(q, k, v, bias):
    rows, width = q.shape
    pairs = width // CROSS
    col = lambda i: (0, i)
    return pl.pallas_call(
        cross_forward_kernel, grid=(pairs,),
        in_specs=[pl.BlockSpec((rows, CROSS), col), pl.BlockSpec((PAD, CROSS), col), pl.BlockSpec((PAD, CROSS), col),
                  pl.BlockSpec((1, PAD), lambda i: (0, 0))],
        out_specs=[pl.BlockSpec((rows, CROSS), col), pl.BlockSpec((4, rows, PAD), lambda i: (i, 0, 0))],
        out_shape=[jax.ShapeDtypeStruct((rows, width), jnp.bfloat16), jax.ShapeDtypeStruct((4 * pairs, rows, PAD), jnp.bfloat16)],
        cost_estimate=cost(8), compiler_params=VM, name="cross_forward")(q, k, v, bias)

def cross_backward_kernel(q_ref, k_ref, v_ref, probs_ref, grad_ref, dq_ref, dk_ref, dv_ref):
    rows = q_ref.shape[0]
    first = lax.broadcasted_iota(jnp.int32, (rows, LANES), 1) < HD
    kfirst = lax.broadcasted_iota(jnp.int32, (PAD, LANES), 1) < HD
    zero = jnp.bfloat16(0)
    for at in range(0, CROSS, LANES):
        q = q_ref[:, at : at + LANES] * jnp.bfloat16(HD ** -0.5)
        k = k_ref[:, at : at + LANES] * jnp.bfloat16(HD ** -0.5)
        grad = grad_ref[:, at : at + LANES]
        dq = jnp.zeros((rows, LANES), jnp.float32)
        dk = jnp.zeros((PAD, LANES), jnp.float32)
        dv = jnp.zeros((PAD, LANES), jnp.float32)
        for half in range(2):
            mine = first == (half == 0)
            g = jnp.where(mine, grad, zero)
            p16 = probs_ref[at // HD + half]
            p = p16.astype(jnp.float32)
            dp = dot(g, v_ref[:, at : at + LANES], NT)
            ds = (p * (dp - jnp.sum(p * dp, axis=-1, keepdims=True))).astype(jnp.bfloat16)
            dq = dq + dot(ds, jnp.where(kfirst == (half == 0), k, zero))
            dk = dk + dot(ds, jnp.where(mine, q, zero), TN)
            dv = dv + dot(p16, g, TN)
        dq_ref[:, at : at + LANES] = dq.astype(jnp.bfloat16)
        dk_ref[:, at : at + LANES] = dk
        dv_ref[:, at : at + LANES] = dv


def cross_backward_call(q, k, v, probs, grad):
    rows, width = q.shape
    pairs = width // CROSS
    col = lambda i: (0, i)
    tok = pl.BlockSpec((rows, CROSS), col); txt = pl.BlockSpec((PAD, CROSS), col)
    return pl.pallas_call(
        cross_backward_kernel, grid=(pairs,),
        in_specs=[tok, txt, txt, pl.BlockSpec((4, rows, PAD), lambda i: (i, 0, 0)), tok],
        out_specs=[tok, txt, txt],
        out_shape=[jax.ShapeDtypeStruct((rows, width), jnp.bfloat16), jax.ShapeDtypeStruct((PAD, width), jnp.float32), jax.ShapeDtypeStruct((PAD, width), jnp.float32)],
        cost_estimate=cost(9), compiler_params=VM, name="cross_backward")(q, k, v, probs, grad)


def gelu_slope(u):
    inner = 0.7978845608028654 * (u + 0.044715 * u * u * u)
    th = jnp.tanh(inner)
    return 0.5 * (1.0 + th) + 0.5 * u * (1.0 - th * th) * (0.7978845608028654 * (1.0 + 3.0 * 0.044715 * u * u))


FF_TILE = 256


def feed_forward_kernel(a_ref, b_ref, up_ref, down_ref, hidden_ref, active_ref, pa_ref, pb_ref):
    rows = a_ref.shape[0]
    units = up_ref.shape[1]
    for at, ref in ((0, a_ref), (rows, b_ref)):
        for t in range(0, units, FF_TILE):
            u = dot(ref[...], up_ref[:, t : t + FF_TILE])
            hidden_ref[pl.ds(at, rows), t : t + FF_TILE] = u.astype(jnp.bfloat16)
            active_ref[pl.ds(at, rows), t : t + FF_TILE] = jax.nn.gelu(u, approximate=True).astype(jnp.bfloat16)
    pa_ref[...] = dot(active_ref[pl.ds(0, rows), :], down_ref[...], NT).astype(jnp.bfloat16)
    pb_ref[...] = dot(active_ref[pl.ds(rows, rows), :], down_ref[...], NT).astype(jnp.bfloat16)


def half_columns(weights):
    units = weights.shape[1] // 2
    return [pl.BlockSpec((weights.shape[0], units), lambda i: (0, 0)), pl.BlockSpec((weights.shape[0], units), lambda i: (0, 1))]


def feed_forward_call(a, b, weights):
    rows, width = a.shape
    units = weights.shape[1] // 2
    whole = pl.BlockSpec((rows, width), lambda i: (0, 0))
    wide = pl.BlockSpec((2 * rows, units), lambda i: (0, 0))
    return pl.pallas_call(
        feed_forward_kernel,
        grid=(1,),
        in_specs=[whole, whole] + half_columns(weights),
        out_specs=[wide, wide, whole, whole],
        out_shape=[
            jax.ShapeDtypeStruct((2 * rows, units), jnp.bfloat16),
            jax.ShapeDtypeStruct((2 * rows, units), jnp.bfloat16),
            jax.ShapeDtypeStruct((rows, width), jnp.bfloat16),
            jax.ShapeDtypeStruct((rows, width), jnp.bfloat16),
        ],
        cost_estimate=cost(7), compiler_params=VM,
        name="feed_forward",
    )(a, b, weights, weights)


def feed_backward_kernel(a_ref, b_ref, hidden_ref, up_ref, down_ref, grad_ref, pa_ref, pb_ref):
    rows = a_ref.shape[0]
    units = up_ref.shape[1]
    for at, ref in ((0, a_ref), (rows, b_ref)):
        for t in range(0, units, FF_TILE):
            slope = gelu_slope(hidden_ref[pl.ds(at, rows), t : t + FF_TILE].astype(jnp.float32))
            grad_ref[pl.ds(at, rows), t : t + FF_TILE] = (dot(ref[...], down_ref[:, t : t + FF_TILE]) * slope).astype(jnp.bfloat16)
    pa_ref[...] = dot(grad_ref[pl.ds(0, rows), :], up_ref[...], NT).astype(jnp.bfloat16)
    pb_ref[...] = dot(grad_ref[pl.ds(rows, rows), :], up_ref[...], NT).astype(jnp.bfloat16)


def feed_backward_call(a, b, hidden, weights):
    rows, width = a.shape
    units = weights.shape[1] // 2
    whole = pl.BlockSpec((rows, width), lambda i: (0, 0))
    wide = pl.BlockSpec((2 * rows, units), lambda i: (0, 0))
    return pl.pallas_call(
        feed_backward_kernel,
        grid=(1,),
        in_specs=[whole, whole, wide] + half_columns(weights),
        out_specs=[wide, whole, whole],
        out_shape=[
            jax.ShapeDtypeStruct((2 * rows, units), jnp.bfloat16),
            jax.ShapeDtypeStruct((rows, width), jnp.bfloat16),
            jax.ShapeDtypeStruct((rows, width), jnp.bfloat16),
        ],
        cost_estimate=cost(8), compiler_params=VM,
        name="feed_backward",
    )(a, b, hidden, weights, weights)


def weight_grad_kernel(counts, splits, order_ref, *refs):
    step = pl.program_id(0)
    (ln_a, rn_a), (ln_b, rn_b) = splits
    left = (refs[:ln_a], refs[ln_a : ln_a + ln_b])
    refs = refs[ln_a + ln_b :]
    right = (refs[:rn_a], refs[rn_a : rn_a + rn_b])
    out_ref, turned_ref = refs[rn_a + rn_b :]
    blocks = order_ref.shape[0]
    width = turned_ref.shape[0] // blocks

    def turn(pieces):
        at = 0
        for ref in pieces:
            rows = ref.shape[0]
            for p in range(blocks):
                column = pl.multiple_of(order_ref[p] * width, width)
                turned_ref[pl.ds(p * width, width), pl.ds(at, rows)] = ref[:, pl.ds(column, width)].T
            at += rows

    def product(pieces):
        at = 0
        total = None
        for ref in pieces:
            rows = ref.shape[0]
            part = dot(turned_ref[:, pl.ds(at, rows)], ref[...])
            total = part if total is None else total + part
            at += rows
        out_ref[...] = total.astype(jnp.bfloat16).reshape(out_ref.shape)

    for n, begin in ((0, 0), (1, counts[0])):

        @pl.when(step == begin)
        def _():
            turn(left[n])

        @pl.when(jnp.logical_and(step >= begin, step < begin + counts[n]))
        def _():
            product(right[n])


GRAD_TILE = 256


def weight_grad_call(order, lefts, rights, out_shape, out_map):
    counts = [sum_cols // GRAD_TILE for sum_cols in (rights[0][0][0].shape[1], rights[1][0][0].shape[1])]
    splits = [(len(lefts[n]), len(rights[n])) for n in range(2)]
    in_specs, operands = [], []
    for n in range(2):
        for item in lefts[n]:
            in_specs.append(pl.BlockSpec(item.shape, lambda i, o: (0, 0)))
            operands.append(item)
    for n in range(2):
        begin, count = (0, counts[0])[n], counts[n]
        for item, rows, block in rights[n]:
            in_specs.append(
                pl.BlockSpec(
                    (rows, GRAD_TILE),
                    lambda i, o, begin=begin, count=count, block=block: (block, jnp.clip(i - begin, 0, count - 1)),
                )
            )
            operands.append(item)
    tokens = sum(item.shape[0] for item in lefts[0])
    width = lefts[0][0].shape[1]
    tiles = counts[0] + counts[1]
    block_shape = out_shape[:-1] + (GRAD_TILE,) if len(out_shape) == 2 else (1, out_shape[1], GRAD_TILE)
    return pl.pallas_call(
        functools.partial(weight_grad_kernel, counts, splits),
        grid_spec=pltpu.PrefetchScalarGridSpec(
            num_scalar_prefetch=1,
            grid=(tiles,),
            in_specs=in_specs,
            out_specs=pl.BlockSpec(block_shape, out_map),
            scratch_shapes=[pltpu.VMEM((width, tokens), jnp.bfloat16)],
        ),
        out_shape=jax.ShapeDtypeStruct(out_shape, jnp.bfloat16),
        cost_estimate=cost(12), compiler_params=VM,
        name="weight_grad",
    )(order, *operands)


def regroup(columns, outer, inner):
    pieces = []
    for i in range(inner):
        for o in range(outer):
            at = (o * inner + i) * HD
            pieces.append(columns[:, at : at + HD])
    return jnp.concatenate(pieces, axis=1)


def prepare_kernel(qkv_ref, out_ref, cq_ref, ckv_ref, cout_ref, up_ref, down_ref, self_ref, pair_ref, text_ref, feed_ref):
    wide = cq_ref.shape[2]
    heads = wide // HD
    units = up_ref.shape[2]
    self_ref[0, :, : 3 * wide] = regroup(qkv_ref[0], heads, 3).astype(jnp.bfloat16)
    self_ref[0, :, 3 * wide :] = out_ref[0].T.astype(jnp.bfloat16)
    pair_ref[0, :, :wide] = cq_ref[0].astype(jnp.bfloat16)
    pair_ref[0, :, wide:] = cout_ref[0].T.astype(jnp.bfloat16)
    text_ref[0] = regroup(ckv_ref[0], heads, 2).astype(jnp.bfloat16)
    feed_ref[0, :, :units] = up_ref[0].astype(jnp.bfloat16)
    feed_ref[0, :, units:] = down_ref[0].T.astype(jnp.bfloat16)


def layer_block(shape):
    return pl.BlockSpec((1,) + tuple(shape[1:]), lambda i: (i, 0, 0))


def prepare_call(masters):
    layers, block, wide = masters[2].shape
    units = masters[5].shape[2]
    shapes = [(layers, block, 4 * wide), (layers, block, 2 * wide), (layers, block, 2 * wide), (layers, block, 2 * units)]
    return pl.pallas_call(
        prepare_kernel,
        grid=(layers,),
        in_specs=[layer_block(item.shape) for item in masters],
        out_specs=[layer_block(shape) for shape in shapes],
        out_shape=[jax.ShapeDtypeStruct(shape, jnp.bfloat16) for shape in shapes],
        cost_estimate=cost(3), compiler_params=VM,
        name="prepare",
    )(*masters)


def adam_math(master, first, second, grad, rate):
    first_new = BETA_ONE * first + (1.0 - BETA_ONE) * grad
    second_new = BETA_TWO * second + (1.0 - BETA_TWO) * grad * grad
    step_size = (
        first_new / (1.0 - BETA_ONE**STEP) / (jnp.sqrt(second_new / (1.0 - BETA_TWO**STEP)) + ADAM_EPS)
    )
    master_new = master - rate * (step_size + DECAY_RATE * master)
    return (master_new, first_new, second_new, master_new.astype(jnp.bfloat16))


def adam_kernel(plans, n_grads, *refs):
    layer = pl.program_id(0)
    count = len(plans)
    sources = [jnp.where(layer == 0, refs[2 * n][...], refs[2 * n + 1][...]).astype(jnp.float32) for n in range(n_grads)]
    refs = refs[2 * n_grads :]
    for n, (source, begin, width, kind, rate) in enumerate(plans):
        master, first, second = [refs[3 * n + m][0] for m in range(3)]
        outs = refs[3 * count + 4 * n : 3 * count + 4 * n + 4]
        grad = sources[source][:, begin : begin + width]
        if kind == "turn":
            grad = grad.T
        elif kind:
            grad = regroup(grad, kind, width // (kind * HD))
        for ref, value in zip(outs, adam_math(master, first, second, grad, rate)):
            ref[0] = value


def adam_call(plans, grads, states):
    in_specs, operands, out_specs, out_shape = [], [], [], []
    for pair in grads:
        for item in pair:
            in_specs.append(pl.BlockSpec(item.shape, lambda i: (0, 0)))
            operands.append(item)
    for group in states:
        for item in group:
            in_specs.append(layer_block(item.shape))
            operands.append(item)
        shape = group[0].shape
        for dtype in (jnp.float32, jnp.float32, jnp.float32, jnp.bfloat16):
            out_specs.append(layer_block(shape))
            out_shape.append(jax.ShapeDtypeStruct(shape, dtype))
    result = pl.pallas_call(
        functools.partial(adam_kernel, plans, len(grads)),
        grid=(states[0][0].shape[0],),
        in_specs=in_specs,
        out_specs=out_specs,
        out_shape=out_shape,
        cost_estimate=cost(5), compiler_params=VM,
        name="adam",
    )(*operands)
    return [result[4 * n : 4 * n + 4] for n in range(len(states))]


def exchange(value, axis, bit, size):
    return lax.ppermute(value, axis, [(i, i ^ bit) for i in range(size)])


def after(value, *anchors):
    return lax.optimization_barrier((value, anchors))[0]


def share_rows(own, meanwhile):
    far = exchange(own, "mp", 2, 4)
    near = exchange(own, "mp", 1, 4)
    done = meanwhile(own, near)
    far = after(far, done)
    return (own, near, far, exchange(far, "mp", 1, 4)), done


def share_small(own):
    far = exchange(own, "mp", 2, 4)
    near = exchange(own, "mp", 1, 4)
    return (own, near, far, exchange(far, "mp", 1, 4))


def collect_parts(parts, meanwhile=None):
    beside = exchange(parts[3], "mp", 1, 4)
    crossing = narrow(parts[2].astype(jnp.float32) + beside.astype(jnp.float32))
    far = exchange(crossing, "mp", 2, 4)
    near_part, done = parts[1], None
    if meanwhile is not None:
        done = meanwhile((crossing, parts[0], parts[1]))
        far = after(far, done)
    near = exchange(after(parts[1], crossing), "mp", 1, 4)
    total = parts[0].astype(jnp.float32) + near.astype(jnp.float32) + far.astype(jnp.float32)
    return total if meanwhile is None else (total, done)


def bits_of(size):
    return [1 << n for n in range(size.bit_length() - 1)]


class Flow:
    def __init__(self, stages):
        self.stages = stages
        self.result = None
        self.pending = next(stages)

    def take(self, value):
        try:
            self.pending = self.stages.send(value)
        except StopIteration as stop:
            self.pending = None
            self.result = stop.value

    def finish(self):
        while self.pending is not None:
            self.take(self.pending)
        return self.result


def tick(anchor, *flows):
    flows = [flow for flow in flows if flow is not None and flow.pending is not None]
    if not flows:
        return anchor
    anchor, values = lax.optimization_barrier((anchor, [flow.pending for flow in flows]))
    for flow, value in zip(flows, values):
        flow.take(value)
    return anchor


def block_order(size):
    me = lax.axis_index("dp").astype(jnp.int32)
    if (D // size) % LANES:
        return jnp.arange(D // LANES, dtype=jnp.int32), False
    order = [0]
    for bit in reversed(bits_of(size)):
        order = order + [item | bit for item in order]
    return jnp.array(order, jnp.int32) ^ me, True


def halving(total, size, ordered):
    me = lax.axis_index("dp")
    rows, width = total.shape
    if ordered:
        for bit in bits_of(size):
            half = total.shape[0] // 2
            got = yield exchange(narrow(total[half:]), "dp", bit, size)
            total = total[:half].astype(jnp.float32) + got.astype(jnp.float32)
            if bit * 2 < size:
                total = narrow(total)
        return total
    blocks = total.reshape(size, rows // size, width)
    for n, bit in enumerate(bits_of(size)):
        pairs = blocks.reshape(blocks.shape[0] // 2, 2, rows // size, width)
        mine = (me >> n) & 1
        keep = lax.dynamic_index_in_dim(pairs, mine, 1, keepdims=False)
        send = lax.dynamic_index_in_dim(pairs, 1 - mine, 1, keepdims=False)
        got = yield exchange(send, "dp", bit, size)
        total = keep.astype(jnp.float32) + got.astype(jnp.float32)
        blocks = narrow(total)
    return total.reshape(rows // size, width)


def doubling(own, size):
    me = lax.axis_index("dp")
    rows, width = own.shape
    own = own[None, None]
    for n, bit in reversed(list(enumerate(bits_of(size)))):
        got = yield exchange(own, "dp", bit, size)
        own = jnp.where(((me >> n) & 1) == 0, jnp.concatenate([own, got], axis=1), jnp.concatenate([got, own], axis=1))
        own = own.reshape(own.shape[0] * 2, 1, rows, width)
    return own.reshape(size * rows, width)


def collecting(parts):
    beside, near = yield (exchange(parts[3], "mp", 1, 4), exchange(parts[1], "mp", 1, 4))
    crossing = narrow(parts[2].astype(jnp.float32) + beside.astype(jnp.float32))
    far = yield exchange(crossing, "mp", 2, 4)
    return parts[0].astype(jnp.float32) + near.astype(jnp.float32) + far.astype(jnp.float32)


def collect_then_gather(parts, size):
    total = yield from collecting(parts)
    total = narrow(total)
    got = yield exchange(total, "dp", 1, size)
    slots = narrow(total.astype(jnp.float32) + got.astype(jnp.float32))[None, None]
    me = lax.axis_index("dp")
    for n, bit in reversed(list(enumerate(bits_of(size)))[1:]):
        got = yield exchange(slots, "dp", bit, size)
        slots = jnp.where(((me >> n) & 1) == 0, jnp.concatenate([slots, got], axis=1), jnp.concatenate([got, slots], axis=1))
        slots = slots.reshape((slots.shape[0] * 2, 1) + slots.shape[2:])
    return slots[:, 0]


def pair_up(slots):
    got = yield (exchange(slots[1], "mp", 1, 4), exchange(slots[3], "mp", 1, 4))
    return jnp.concatenate([narrow(slots[2 * k].astype(jnp.float32) + got[k].astype(jnp.float32)) for k in range(2)], axis=1)


def halve_then_cross(total, size, ordered, width):
    total = yield from halving(total, size, ordered)
    got = yield exchange(narrow(total[:, width : 2 * width]), "mp", 2, 4)
    return total[:, :width] + got.astype(jnp.float32), total[:, 2 * width :]


def summing_rows(rows, size):
    for bit in (1, 2):
        got = yield exchange(narrow(rows), "mp", bit, 4)
        rows = rows + got.astype(jnp.float32)
    slots = narrow(rows)[None, None]
    me = lax.axis_index("dp")
    for n, bit in reversed(list(enumerate(bits_of(size)))[1:]):
        got = yield exchange(slots, "dp", bit, size)
        slots = jnp.where(((me >> n) & 1) == 0, jnp.concatenate([slots, got], axis=1), jnp.concatenate([got, slots], axis=1))
        slots = slots.reshape((slots.shape[0] * 2, 1) + slots.shape[2:])
    got = yield exchange(slots, "dp", 1, size)
    return slots.astype(jnp.float32) + got.astype(jnp.float32)


def halving_blocks(blocks, size):
    me = lax.axis_index("dp")
    for n, bit in enumerate(bits_of(size)):
        pairs = blocks.reshape((blocks.shape[0] // 2, 2) + blocks.shape[1:])
        mine = (me >> n) & 1
        got = yield exchange(lax.dynamic_index_in_dim(pairs, 1 - mine, 1, keepdims=False), "dp", bit, size)
        blocks = lax.dynamic_index_in_dim(pairs, mine, 1, keepdims=False) + got
    return blocks[0]


def gathering(own, size):
    me = lax.axis_index("dp")
    slots = own[None]
    for n, bit in enumerate(bits_of(size)):
        got = yield exchange(slots, "dp", bit, size)
        slots = jnp.where(((me >> n) & 1) == 0, jnp.concatenate([slots, got]), jnp.concatenate([got, slots]))
    return slots


def gather_small(own, size):
    return Flow(gathering(own, size)).finish()


def modulate(latent, scale, shift):
    normed, inverse = layer_norm(latent)
    return (normed * (1.0 + scale) + shift).astype(jnp.bfloat16)


def narrow(value):
    return value.astype(jnp.bfloat16)


def mm(a, b, dims=(((1,), (0,)), ((), ()))):
    return lax.dot_general(a, b, dims, preferred_element_type=jnp.float32)


def body(*args):
    (latents, cotangent, text_embed, text_mask, band_ids, rel_index_s, rel_index_t, modulation) = args[:8]
    masters, firsts, seconds = args[8:17], args[17:26], args[26:35]
    groups = lax.axis_size("dp")
    rates = learning_rates()
    own = latents.shape[0]
    half = 2 * own
    wide = masters[1].shape[1]
    index_tables = (rel_index_s, rel_index_t)
    reaches = (masters[7].shape[1] * groups, masters[8].shape[1] * groups)

    order, ordered = block_order(groups)
    plain = jnp.arange(D // LANES, dtype=jnp.int32)

    block = D // groups
    self_shards, pair_shards, text_shards, feed_shards = prepare_call(masters[:7])
    pair_shards = pair_shards.reshape(LAYERS * block, 2 * wide)
    other = exchange(pair_shards, "mp", 2, 4)

    def cross_shard(layer):
        rows = slice(layer * block, (layer + 1) * block)
        return [pair_shards[rows], other[rows], text_shards[layer]]

    def gather(pieces):
        return lax.all_gather(jnp.concatenate(pieces, axis=1), "dp", axis=0, tiled=True)

    split = 4 * wide
    self_flow_0 = Flow(doubling(self_shards[0], groups))
    first_all = gather(cross_shard(0) + [feed_shards[0]])
    next_all = gather([self_shards[1]] + cross_shard(1))
    feed_1 = lax.all_gather(feed_shards[1], "dp", axis=0, tiled=True)
    cross_ws = (first_all[:, : 6 * wide], next_all[:, split:])
    feed_ws = (first_all[:, 6 * wide :], feed_1)

    position = lax.axis_index("mp").astype(jnp.int32)[None]
    clip_index = lax.axis_index("dp") // 2
    text_rows = lax.dynamic_index_in_dim(text_embed, clip_index, 0, keepdims=False)
    texts = text_rows.shape[0]
    texts_pad = -(-texts // 16) * 16
    text_rows = jnp.pad(text_rows, ((0, PAD - texts), (0, 0)))
    mask_row = lax.dynamic_index_in_dim(text_mask, clip_index, 0, keepdims=False)
    column = jnp.arange(PAD, dtype=jnp.int32)
    valid = jnp.maximum(jnp.pad(mask_row, (0, PAD - texts)), (column == 0).astype(jnp.int32)).astype(jnp.float32)
    valid_bias = jnp.where(column < texts, (valid - 1.0) * 1000000000.0, -1e30)[None]
    band_now = lax.dynamic_index_in_dim(band_ids, clip_index, 0, keepdims=False)
    mod_rows = lax.dynamic_index_in_dim(modulation, band_now, 0, keepdims=False)
    text_columns = lax.dynamic_slice_in_dim(text_embed, lax.axis_index("dp") * (D // groups), D // groups, axis=2)

    tables = gather_small(jnp.concatenate([narrow(masters[7]), narrow(masters[8])], axis=1), groups)
    tables = tables.swapaxes(0, 1)
    cut = masters[7].shape[1]
    table_s = tables[:, :, :cut].reshape(tables.shape[0], -1)
    table_t = tables[:, :, cut:].reshape(tables.shape[0], -1)
    biases = (make_bias(table_s, rel_index_s), make_bias(table_t, rel_index_t))

    latent = latents
    saved = []
    weights = []
    for layer in range(LAYERS):
        base = 9 * layer
        record = {"in": latent}
        sending = modulate(latent, mod_rows[base + 1], mod_rows[base])
        if layer == 0:
            self_w = after(self_flow_0.finish(), biases)
        else:
            self_w = next_all[:, :split]
        w_in = self_w[:, : 3 * wide]
        rows, near_qkv = share_rows(sending, lambda one, two: (narrow(mm(one, w_in)), narrow(mm(two, w_in))))
        qkv = jnp.concatenate(near_qkv + tuple(narrow(mm(item, w_in)) for item in rows[2:]), axis=0)
        mixed, probs = self_forward_call(layer, position, qkv, biases[layer])
        w_out = self_w[:, 3 * wide :]
        project = lambda k: narrow(mm(mixed[k * own : (k + 1) * own], w_out, NT))
        p2, p3 = project(2), project(3)
        branch = collect_parts([project(0), project(1), p2, p3])
        record["self"] = (rows, qkv, probs, mixed, branch)
        latent = latent + mod_rows[base + 2] * branch
        record["mid"] = latent
        normed = modulate(latent, mod_rows[base + 4], mod_rows[base + 3])
        cross_w = cross_ws[layer]
        keyval = share_small(narrow(mm(text_rows, cross_w[:, 4 * wide :])))
        keys = jnp.concatenate([item[:, :wide] for item in keyval], axis=1)
        values = jnp.concatenate([item[:, wide:] for item in keyval], axis=1)
        across = exchange(cross_w[:, : 4 * wide], "mp", 1, 4)
        cross_all = (cross_w[:, : 2 * wide], across[:, : 2 * wide], cross_w[:, 2 * wide : 4 * wide], across[:, 2 * wide :])
        w_cq = jnp.concatenate([item[:, :wide] for item in cross_all], axis=1)
        w_cout = jnp.concatenate([item[:, wide:] for item in cross_all], axis=1)
        queries = narrow(mm(normed, w_cq))
        mixed, probs = cross_forward_call(queries, keys, values, valid_bias)
        branch = mm(mixed, w_cout, NT)
        record["cross"] = (normed, queries, keys, values, probs, mixed, branch, w_cq, w_cout)
        latent = latent + mod_rows[base + 5] * branch
        record["late"] = latent
        feed_w = feed_ws[layer]
        weights.append((self_w, feed_w))
        rows, (hidden_near, active_near, p0, p1) = share_rows(
            modulate(latent, mod_rows[base + 7], mod_rows[base + 6]), lambda one, two: feed_forward_call(one, two, feed_w)
        )
        hidden_far, active_far, p2, p3 = feed_forward_call(rows[2], rows[3], feed_w)
        branch = collect_parts([p0, p1, p2, p3])
        record["feed"] = (rows, (hidden_near, hidden_far), (active_near, active_far), branch)
        latent = latent + mod_rows[base + 8] * branch
        saved.append(record)

    grad_latent = cotangent
    mod_grads = [None, None]
    feed_flows, self_flows, cross_flows, tables_sent, kv_grads = [None] * 2, [None] * 2, [None] * 2, [None] * 2, [None] * 2
    kv_flow = None
    for layer in reversed(range(LAYERS)):
        self_w, feed_w = weights[layer]
        last = layer == 0
        base = 9 * layer
        record = saved[layer]
        rows, hiddens, actives, branch = record["feed"]
        gate_m = jnp.sum(grad_latent * branch, axis=0)
        grads, (dh_near, p0, p1) = share_rows(
            narrow(mod_rows[base + 8] * grad_latent), lambda one, two: feed_backward_call(one, two, hiddens[0], feed_w)
        )
        dh_far, p2, p3 = feed_backward_call(grads[2], grads[3], hiddens[1], feed_w)
        units = dh_near.shape[1]
        grad_input, feed_g = collect_parts(
            [p0, p1, p2, p3],
            lambda sent: weight_grad_call(
                plain,
                (rows, grads),
                (((after(dh_near, sent), half, 0), (dh_far, half, 0)), ((actives[0], half, 0), (actives[1], half, 0))),
                (D, 2 * units),
                lambda i, o: (0, i),
            ),
        )
        feed_flows[layer] = lax.psum_scatter(feed_g, "dp", scatter_dimension=0, tiled=True)
        if last:
            grad_input = after(grad_input, feed_flows[1])
        normed, inverse = layer_norm(record["late"])
        grad_latent, shift_m, scale_m = modulate_back(grad_latent, grad_input, normed, inverse, mod_rows[base + 7])

        hidden, queries, keys, values, probs, mixed, branch, w_cq, w_cout = record["cross"]
        gate_c = jnp.sum(grad_latent * branch, axis=0)
        grad_rows = narrow(mod_rows[base + 5] * grad_latent)
        grad_mixed = narrow(mm(grad_rows, w_cout))
        grad_query, grad_key, grad_value = cross_backward_call(queries, keys, values, probs, grad_mixed)
        kv_grads[layer] = [
            narrow(
                jnp.concatenate(
                    [grad_key[:texts_pad, k * wide : (k + 1) * wide], grad_value[:texts_pad, k * wide : (k + 1) * wide]], axis=1
                )
            )
            for k in range(4)
        ]
        if last:
            kv_flow = Flow(
                collect_then_gather([jnp.concatenate([kv_grads[0][k], kv_grads[1][k]], axis=0) for k in range(4)], groups)
            )
        grad_input = mm(grad_query, w_cq, NT)
        normed, inverse = layer_norm(record["mid"])
        grad_latent, shift_c, scale_c = modulate_back(grad_latent, grad_input, normed, inverse, mod_rows[base + 4])
        tiles = queries.shape[1] // GRAD_TILE
        if last:
            grad_latent = tick(grad_latent, kv_flow)
        sending = narrow(mod_rows[base + 2] * grad_latent)
        w_out = self_w[:, 3 * wide :]
        grads, (cross_g, near_mixed) = share_rows(
            sending,
            lambda one, two: (
                weight_grad_call(
                    order if last else plain,
                    ((after(hidden, sending),), (grad_rows,)),
                    (((grad_query, own, 0),), ((mixed, own, 0),)),
                    (tiles, D, 2 * GRAD_TILE),
                    lambda i, o: (i % tiles, 0, i // tiles),
                ),
                (narrow(mm(one, w_out)), narrow(mm(two, w_out))),
            ),
        )
        rows, qkv, probs, mixed, branch = record["self"]
        gate_a = jnp.sum(grad_latent * branch, axis=0)
        grad_mixed = jnp.concatenate(near_mixed + tuple(narrow(mm(item, w_out)) for item in grads[2:]), axis=0)
        pairing = Flow(pair_up(cross_g))
        grad_mixed = tick(grad_mixed, kv_flow)
        grad_qkv, summed = self_backward_call(layer, position, qkv, probs, grad_mixed)
        grad_qkv = tick(grad_qkv, pairing, kv_flow)
        if last:
            cross_flows[0] = Flow(halve_then_cross(pairing.finish(), groups, ordered, 2 * wide))
        back = lambda k: narrow(mm(grad_qkv[k * own : (k + 1) * own], self_w[:, : 3 * wide], NT))
        p2, p3 = back(2), back(3)
        grad_input, self_g = collect_parts(
            [back(0), back(1), p2, p3],
            lambda sent: weight_grad_call(
                order if last else plain,
                (rows, grads),
                (((after(grad_qkv, sent), half, 0), (grad_qkv, half, 1)), ((mixed, half, 0), (mixed, half, 1))),
                (D, 4 * wide),
                lambda i, o: (0, i),
            ),
        )
        if last:
            self_flows[0] = Flow(halving(self_g, groups, ordered))
        else:
            both = jnp.concatenate([pairing.finish(), after(self_g, grad_input)], axis=1)
            upper = lax.psum_scatter(both, "dp", scatter_dimension=0, tiled=True)
            from_pair = exchange(upper[:, 2 * wide : 4 * wide], "mp", 2, 4)
            cross_1 = upper[:, : 2 * wide].astype(jnp.float32) + from_pair.astype(jnp.float32)
            self_1 = upper[:, 4 * wide :]
        tables_sent[layer] = summed
        if last:
            grad_input = tick(grad_input, kv_flow, cross_flows[0])
        normed, inverse = layer_norm(record["in"])
        grad_latent, shift_a, scale_a = modulate_back(grad_latent, grad_input, normed, inverse, mod_rows[base + 1])
        mod_grads[layer] = [shift_a, scale_a, gate_a, shift_c, scale_c, gate_c, shift_m, scale_m, gate_m]
        if last:
            grad_latent = after(grad_latent, upper)

    mod_local = jnp.stack(mod_grads[0] + mod_grads[1], axis=0)
    mod_local = tick(mod_local, cross_flows[0])
    mod_flow = Flow(summing_rows(mod_local, groups))
    summed_1 = tick(tables_sent[1], mod_flow)
    summed_1 = tick(summed_1, mod_flow)
    table_1 = bucket_sum(summed_1, index_tables[1], reaches[1])
    table_1 = tick(table_1, mod_flow, cross_flows[0], self_flows[0], kv_flow)
    table_0 = bucket_sum(after(tables_sent[0], table_1), index_tables[0], reaches[0])
    table_0 = tick(table_0, mod_flow, self_flows[0], cross_flows[0])
    table_grads = [table_0, table_1]
    table_rows = [item.reshape(item.shape[0], groups, -1).swapaxes(0, 1) for item in table_grads]
    table_flow = Flow(halving_blocks(jnp.concatenate(table_rows, axis=2), groups))
    units = masters[5].shape[2]
    state = lambda item: (masters[item], firsts[item], seconds[item])
    updates = [None] * 9
    updates[5], updates[6] = adam_call(
        ((0, 0, units, None, rates[5]), (0, units, units, "turn", rates[6])), [feed_flows], [state(5), state(6)]
    )
    updates[5] = tick(updates[5], mod_flow, self_flows[0], cross_flows[0], table_flow)
    mod_clips = mod_flow.finish()
    bands = (band_ids[None, :] == jnp.arange(modulation.shape[0], dtype=jnp.int32)[:, None]).astype(jnp.float32)
    grad_modulation = jnp.sum(bands[:, :, None, None] * mod_clips[None, :, 0], axis=1)

    table_sum = table_flow.finish()
    kv_all = kv_flow.finish()
    kv_sums = []
    for layer in range(LAYERS):
        grad_kv = kv_all[:, layer * texts_pad : layer * texts_pad + texts]
        kv_sums.append(
            lax.dot_general(text_columns, grad_kv, (((0, 1), (0, 1)), ((), ())), preferred_element_type=jnp.float32)
        )
    cross_sums = [cross_flows[0].finish()[0], cross_1]
    updates[2], updates[3], updates[4] = adam_call(
        ((0, 0, wide, None, rates[2]), (1, 0, 2 * wide, 2, rates[3]), (0, wide, wide, "turn", rates[4])),
        [cross_sums, kv_sums],
        [state(2), state(3), state(4)],
    )
    self_sums = [self_flows[0].finish(), self_1]
    updates[0], updates[1] = adam_call(
        ((0, 0, 3 * wide, 3, rates[0]), (0, 3 * wide, wide, "turn", rates[1])), [self_sums], [state(0), state(1)]
    )
    updates[7] = adam_math(masters[7], firsts[7], seconds[7], table_sum[:, :cut], rates[7])
    updates[8] = adam_math(masters[8], firsts[8], seconds[8], table_sum[:, cut:], rates[8])
    results = [latent, grad_latent, grad_modulation]
    for item in updates:
        results.extend(item)
    return tuple(results)


def solution(mesh):
    in_specs = (
        P(("dp", "mp"), None),
        P(("dp", "mp"), None),
        P(),
        P(),
        P(),
        P(),
        P(),
        P(),
        P(None, "dp", "mp"),
        P(None, "mp", "dp"),
        P(None, "dp", "mp"),
        P(None, "dp", "mp"),
        P(None, "mp", "dp"),
        P(None, "dp", "mp"),
        P(None, "mp", "dp"),
        P("mp", "dp"),
        P("mp", "dp"),
        P(None, "dp", "mp"),
        P(None, "mp", "dp"),
        P(None, "dp", "mp"),
        P(None, "dp", "mp"),
        P(None, "mp", "dp"),
        P(None, "dp", "mp"),
        P(None, "mp", "dp"),
        P("mp", "dp"),
        P("mp", "dp"),
        P(None, "dp", "mp"),
        P(None, "mp", "dp"),
        P(None, "dp", "mp"),
        P(None, "dp", "mp"),
        P(None, "mp", "dp"),
        P(None, "dp", "mp"),
        P(None, "mp", "dp"),
        P("mp", "dp"),
        P("mp", "dp"),
    )
    out_specs = (
        P(("dp", "mp"), None),
        P(("dp", "mp"), None),
        P(),
        P(None, "dp", "mp"),
        P(None, "dp", "mp"),
        P(None, "dp", "mp"),
        P(None, "dp", "mp"),
        P(None, "mp", "dp"),
        P(None, "mp", "dp"),
        P(None, "mp", "dp"),
        P(None, "mp", "dp"),
        P(None, "dp", "mp"),
        P(None, "dp", "mp"),
        P(None, "dp", "mp"),
        P(None, "dp", "mp"),
        P(None, "dp", "mp"),
        P(None, "dp", "mp"),
        P(None, "dp", "mp"),
        P(None, "dp", "mp"),
        P(None, "mp", "dp"),
        P(None, "mp", "dp"),
        P(None, "mp", "dp"),
        P(None, "mp", "dp"),
        P(None, "dp", "mp"),
        P(None, "dp", "mp"),
        P(None, "dp", "mp"),
        P(None, "dp", "mp"),
        P(None, "mp", "dp"),
        P(None, "mp", "dp"),
        P(None, "mp", "dp"),
        P(None, "mp", "dp"),
        P("mp", "dp"),
        P("mp", "dp"),
        P("mp", "dp"),
        P("mp", "dp"),
        P("mp", "dp"),
        P("mp", "dp"),
        P("mp", "dp"),
        P("mp", "dp"),
    )
    return jax.shard_map(body, mesh=mesh, in_specs=in_specs, out_specs=out_specs, check_vma=False)
```
